32 devices in a mesh: head: 2 (over y), blk: 16 (over z, x, core).
Axes of the slice: x: 2, y: 2, z: 4, core: 2. Of those that a mesh axis runs over, the one named last changes fastest.
Arguments:
- inputs: bfloat16 [4096, 768], P(('head', 'blk')), may hold values from -6 to 6
- blocks: int32 [4096], replicated, may hold values from 0 to 15, never falling along the last dimension, each value on 1 to 512 neighbouring positions
- routes: int32 [4096, 2], P(('head', 'blk')), may hold values from 0 to 15, all different within a row; in each aligned block of 128 rows (0 to 127, 128 to 255, ...) at most 32 rows name the same one
- attn_gain: bfloat16 [768], P(('head', 'blk')), may hold values from 0.5 to 1.5
- w_query: bfloat16 [768, 768], P(('head', 'blk')), may hold values from -0.21875 to 0.21875
- w_key: bfloat16 [768, 768], P(('head', 'blk')), may hold values from -0.21875 to 0.21875
- w_value: bfloat16 [768, 768], P(('head', 'blk')), may hold values from -0.21875 to 0.21875
- w_out: bfloat16 [768, 768], P(('head', 'blk')), may hold values from -6 to 6
- ffn_gain: bfloat16 [768], P(('head', 'blk')), may hold values from 0.5 to 1.5
- w_router: bfloat16 [768, 16], P(('head', 'blk')), may hold values from -0.15625 to 0.15625
- shared_gate: bfloat16 [768, 2048], P(('head', 'blk')), may hold values from -0.21875 to 0.21875
- shared_up: bfloat16 [768, 2048], P(('head', 'blk')), may hold values from -0.21875 to 0.21875
- shared_down: bfloat16 [2048, 768], P(('head', 'blk')), may hold values from -0.125 to 0.125
- expert_gate: bfloat16 [32, 768, 1024], P(('head', 'blk')), may hold values from -0.21875 to 0.21875
- expert_up: bfloat16 [32, 768, 1024], P(('head', 'blk')), may hold values from -0.21875 to 0.21875
- expert_down: bfloat16 [32, 1024, 768], P(('head', 'blk')), may hold values from -0.125 to 0.125
- cotangent: bfloat16 [4096, 768], P(('head', 'blk')), may hold values from -6 to 6
Outputs:
- output: bfloat16 [4096, 768], P(('head', 'blk'))
- grad_inputs: float32 [4096, 768], P(('head', 'blk'))
- grad_attn_gain: float32 [768], P(('head', 'blk'))
- grad_query: float32 [768, 768], P(('head', 'blk'))
- grad_key: float32 [768, 768], P(('head', 'blk'))
- grad_value: float32 [768, 768], P(('head', 'blk'))
- grad_out_proj: float32 [768, 768], P(('head', 'blk'))
- grad_ffn_gain: float32 [768], P(('head', 'blk'))
- grad_router: float32 [768, 16], P(('head', 'blk'))
- grad_shared_gate: float32 [768, 2048], P(('head', 'blk'))
- grad_shared_up: float32 [768, 2048], P(('head', 'blk'))
- grad_shared_down: float32 [2048, 768], P(('head', 'blk'))
- grad_expert_gate: float32 [32, 768, 1024], P(('head', 'blk'))
- grad_expert_up: float32 [32, 768, 1024], P(('head', 'blk'))
- grad_expert_down: float32 [32, 1024, 768], P(('head', 'blk'))
The draws below stay inside these ranges and needn't reach their ends.
Inputs may be any that keep to these rules, and one draw needn't show every extreme that they name: `blocks`: block indices never fall along the sequence; every block holds 1 to 512 tokens and one holds exactly 512. `routes`: each token names two different experts; among the tokens of one device (128 in a row, aligned) no expert is named more than 32 times, a bound that some block reaches.
All inputs are finite; a program needn't handle non-finite values.
Results may differ from the reference program's by a relative error of at most 0.025.
Values may be sent and summed in bfloat16 or wider, within the bound.
No kernel may reach another device: no remote copies, remote signals or barrier semaphores. Data moves between devices by JAX's collectives and lax.ppermute only.
A program may use at most 320 MiB of HBM per device.

```python
import math
import jax
import jax.numpy as jnp
import numpy as np
from jax import lax

D = 768
HEADS = 12
HEAD_DIM = 64
FF = 2048
SHARED = 2048
EXPERTS = 16
TOK_DEV = 128
BLOCK = 256
TOKENS = 4096
CAP = 32
PIECES = 32
SLICE = 1024
N_HEAD = 2
N_BLK = 16


def block_scale(rng, extent, split, smallest, top_value):
    level = 1.0
    for position, parts in split:
        heights = jax.random.uniform(jax.random.fold_in(jax.random.fold_in(rng, 6), position), (parts,), jnp.float32, smallest / len(split), top_value / len(split))
        level = level * jnp.repeat(jnp.exp(heights), extent[position] // parts).reshape((-1,) + (1,) * (len(extent) - 1 - position))
    return level


def profile(amount, total, reach, lean):
    loads = [(1 << 20) // math.isqrt(standing ** lean) + 1 for standing in range(2, amount + 1)]
    spare, counts = total - reach - (amount - 1), [1] * (amount - 1)
    while spare > 0:
        movable = [i for i in range(amount - 1) if counts[i] < reach]
        whole, remaining = sum([loads[i] for i in movable]), spare
        for i in movable:
            more = min(reach - counts[i], max(1, remaining * loads[i] // whole), spare)
            counts[i] = counts[i] + more
            spare = spare - more
    return np.array([reach] + counts)


def uneven_parts(own_key, count, total, limit, skew):
    if count == 2:
        one = jax.random.randint(own_key, (), max(1, total - limit), min(limit, total - 1) + 1)
        return jnp.stack([one, total - one])
    tallies = jnp.asarray(profile(count, total, limit, skew), jnp.int32)
    pairs = (count - 1) // 2
    donor, taker = tallies[1:1 + 2 * pairs:2], tallies[2:2 + 2 * pairs:2]
    room = jnp.minimum(donor - 1, limit - taker)
    passed = jax.random.randint(jax.random.fold_in(own_key, 1), (pairs,), 0, 1 << 20) % (room + 1)
    tallies = tallies.at[1:1 + 2 * pairs:2].set(donor - passed).at[2:2 + 2 * pairs:2].set(taker + passed)
    return tallies[jax.random.permutation(jax.random.fold_in(own_key, 2), count)]


def deal_out(key, own, number, rows, amount, top, reach, skew):
    order = jax.random.permutation(key, amount)
    crowded, ordinary = portions_of(amount, rows * top, reach, skew, True), portions_of(amount, rows * top, reach, skew, False)
    places = jnp.arange(amount)

    def named(sizes, rotation):
        used = int((sizes > 0).sum())
        fixed = max(1, used // 4)
        shifted = fixed + (places - fixed + rotation * (used - fixed)) % max(1, amount - fixed)
        return jnp.zeros((amount,), jnp.int32).at[order[jnp.where(places < fixed, places, shifted)]].set(jnp.asarray(sizes, jnp.int32))

    sizes = jnp.where(number % 4 == 0, named(crowded, number // 4), named(ordinary, number - number // 4 - 1))
    mixed = jax.random.permutation(jax.random.fold_in(own, 3), amount)
    giver, taker = mixed[0:amount // 2 * 2:2], mixed[1:amount // 2 * 2:2]
    room = jnp.minimum(sizes[giver] - 1, reach - sizes[taker]) // 2
    room = jnp.where((giver == order[0]) | (taker == order[0]) | (sizes[taker] == 0), 0, jnp.maximum(room, 0))
    shifted = jax.random.randint(jax.random.fold_in(own, 4), (amount // 2,), 0, 1 << 20) % (room + 1)
    sizes = sizes.at[giver].add(-shifted).at[taker].add(shifted)
    items = jnp.searchsorted(jnp.cumsum(sizes), jnp.arange(rows * top), side="right").astype(jnp.int32)
    listing = items.reshape(top, rows).T
    listing = listing[jax.random.permutation(jax.random.fold_in(own, 1), rows)]
    rotation = jax.random.randint(jax.random.fold_in(own, 2), (rows, 1), 0, top)
    return jnp.take_along_axis(listing, (jnp.arange(top)[None, :] + rotation) % top, axis=1)


def portions_of(number_of, total, most, slope, full):
    weights = [(1 << 20) // math.isqrt(rank ** slope) + 1 for rank in range(1, number_of + 1)]
    largest = most if full else min(most, max(-(-total // number_of), total * weights[0] // sum(weights)))
    least = 1 if total - largest >= number_of - 1 else 0
    given, spare = [largest] + [least] * (number_of - 1), total - largest - least * (number_of - 1)
    while spare > 0:
        free = [i for i in range(1, number_of) if given[i] < largest] or [i for i in range(1, number_of) if given[i] < most]
        whole, remaining = sum([weights[i] for i in free]), spare
        for i in free:
            more = min(most - given[i], max(1, remaining * weights[i] // whole), spare)
            given[i] = given[i] + more
            spare = spare - more
    return np.array(given)


def noise(rng, extent, deviation, bound, pieces=(), kind=jnp.bfloat16):
    gain = block_scale(rng, extent, pieces, -0.22, 0.18) if pieces else 1.0
    values = jax.random.normal(rng, extent, jnp.float32) * deviation * gain
    return jnp.minimum(jnp.maximum(values, -bound), bound).astype(kind)


def setup_inputs(seed: int = 0) -> dict:
    streams_of = jax.random.split(jax.random.key(seed), 18)
    inputs = noise(streams_of[0], (TOKENS, D), 1.0, 6.0, ((0, 32),))
    blocks = jnp.searchsorted(jnp.cumsum(uneven_parts(streams_of[1], TOKENS // BLOCK, TOKENS, 2 * BLOCK, 1)), jnp.arange(TOKENS), side="right").astype(jnp.int32)
    routes_keys = jax.random.split(jax.random.fold_in(streams_of[2], 1), TOKENS // TOK_DEV)
    routes_turns = jax.random.permutation(jax.random.fold_in(streams_of[2], 3), TOKENS // TOK_DEV)
    routes = jax.vmap(lambda own, number: deal_out(jax.random.fold_in(streams_of[2], 2), own, number, TOK_DEV, EXPERTS, 2, CAP, 2))(routes_keys, routes_turns).reshape((TOKENS, 2))
    attn_gain = jnp.clip(1.0 + 0.1 * jax.random.normal(streams_of[3], (D,), jnp.float32), 0.5, 1.5).astype(jnp.bfloat16)
    w_query = noise(streams_of[4], (D, D), D ** -0.5, 0.21875, ((0, 32),))
    w_key = noise(streams_of[5], (D, D), D ** -0.5, 0.21875, ((0, 32),))
    w_value = noise(streams_of[6], (D, D), D ** -0.5, 0.21875, ((0, 32),))
    w_out = noise(streams_of[7], (D, D), 1 ** -0.5, 6.0, ((0, 32),))
    ffn_gain = jnp.clip(1.0 + 0.1 * jax.random.normal(streams_of[8], (D,), jnp.float32), 0.5, 1.5).astype(jnp.bfloat16)
    w_router = noise(streams_of[9], (D, EXPERTS), (2 * D) ** -0.5, 0.15625, ((0, 32),))
    shared_gate = noise(streams_of[10], (D, SHARED), D ** -0.5, 0.21875, ((0, 32),))
    shared_up = noise(streams_of[11], (D, SHARED), D ** -0.5, 0.21875, ((0, 32),))
    shared_down = noise(streams_of[12], (SHARED, D), SHARED ** -0.5, 0.125, ((0, 32),))
    expert_gate = noise(streams_of[13], (PIECES, D, SLICE), D ** -0.5, 0.21875, ((0, 32),))
    expert_up = noise(streams_of[14], (PIECES, D, SLICE), D ** -0.5, 0.21875, ((0, 32),))
    expert_down = noise(streams_of[15], (PIECES, SLICE, D), FF ** -0.5, 0.125, ((0, 32),))
    cotangent = noise(streams_of[16], (TOKENS, D), 1.0, 6.0, ((0, 32),))
    return {"inputs": inputs, "blocks": blocks, "routes": routes, "attn_gain": attn_gain, "w_query": w_query, "w_key": w_key, "w_value": w_value, "w_out": w_out, "ffn_gain": ffn_gain, "w_router": w_router, "shared_gate": shared_gate, "shared_up": shared_up, "shared_down": shared_down, "expert_gate": expert_gate, "expert_up": expert_up, "expert_down": expert_down, "cotangent": cotangent}


@jax.custom_vjp
def low(v):
    return lax.optimization_barrier(v.astype(jnp.bfloat16)).astype(jnp.float32)

@jax.custom_vjp
def low_back(v):
    return v

def low_keep(v):
    return (low(v), None)

def low_pass(kept, grad):
    return (grad,)

def back_keep(v):
    return (v, None)

def back_low(kept, grad):
    return (low(grad),)
low.defvjp(low_keep, low_pass)
low_back.defvjp(back_keep, back_low)
highest = lax.Precision.HIGHEST
epsilon = 1e-05
scale_factor = 0.125
masked_value = -1e+30

def product(left_side, right_side):
    return jnp.dot(left_side, right_side, precision=highest)

def rms_scale(values, gain_row):
    return values * lax.rsqrt(lax.optimization_barrier(jnp.mean(values * values, axis=-1, keepdims=True)) + epsilon) * gain_row

def silu_product(gate_pre, up_pre):
    return gate_pre * jax.nn.sigmoid(gate_pre) * up_pre

def attention(query_rows, key_rows, value_rows, blocks):
    total_rows = query_rows.shape[0]
    row_count = min(512, total_rows)
    query_heads = query_rows.reshape(total_rows, HEADS, HEAD_DIM)
    key_heads = key_rows.reshape(total_rows, HEADS, HEAD_DIM)
    value_heads = value_rows.reshape(total_rows, HEADS, HEAD_DIM)

    def one_block(offset):
        query_part = lax.dynamic_slice_in_dim(query_heads, offset, row_count, 0)
        part_ids = lax.dynamic_slice_in_dim(blocks, offset, row_count, 0)
        raw_scores = low_back(jnp.einsum('qhd,khd->hqk', query_part, key_heads, precision=highest))
        scores = raw_scores * scale_factor
        allowed = (blocks[None, :] <= part_ids[:, None])[None]
        scores = jnp.where(allowed, scores, masked_value)
        top_score = lax.optimization_barrier(jnp.max(scores, axis=-1, keepdims=True))
        weights = jnp.exp(scores - top_score)
        probabilities = weights / lax.optimization_barrier(jnp.sum(weights, axis=-1, keepdims=True))
        mixed_part = jnp.einsum('hqk,khd->qhd', low(probabilities), value_heads, precision=highest)
        return mixed_part.reshape(row_count, HEADS * HEAD_DIM)
    offsets = jnp.arange(total_rows // row_count, dtype=jnp.int32) * row_count
    return lax.map(jax.checkpoint(one_block), offsets).reshape(total_rows, HEADS * HEAD_DIM)

def expert_rows(normed_ffn, routes, expert_gate, expert_up, expert_down):
    total_rows = normed_ffn.shape[0]
    devices = N_HEAD * N_BLK
    slices = devices // EXPERTS
    slice_width = FF // slices
    flat_routes = routes.reshape(-1).astype(jnp.int32)
    route_onehot = (flat_routes[:, None] == jnp.arange(EXPERTS, dtype=jnp.int32)[None, :]).astype(jnp.int32)
    blocked = route_onehot.reshape(devices, 2 * TOK_DEV, EXPERTS)
    rank_table = (jnp.cumsum(blocked, axis=1) - blocked).reshape(2 * total_rows, EXPERTS)
    slot_rank = lax.optimization_barrier(jnp.sum(rank_table * route_onehot, axis=1)).astype(jnp.int32)
    owner_device = (jnp.arange(2 * total_rows, dtype=jnp.int32) // (2 * TOK_DEV)).astype(jnp.int32)
    slot_place = ((flat_routes * devices + owner_device) * CAP + slot_rank).astype(jnp.int32)
    repeated = jnp.repeat(normed_ffn, 2, axis=0)
    packed = jnp.zeros((EXPERTS * devices * CAP, D), jnp.float32).at[slot_place].add(repeated)
    grouped = packed.reshape(EXPERTS, devices * CAP, D)
    gate_slices = expert_gate.reshape(slices, EXPERTS, D, slice_width).transpose(1, 0, 2, 3)
    up_slices = expert_up.reshape(slices, EXPERTS, D, slice_width).transpose(1, 0, 2, 3)
    down_slices = expert_down.reshape(slices, EXPERTS, slice_width, D).transpose(1, 0, 2, 3)

    def single_expert(operands):
        rows_in, gate_e, up_e, down_e = operands
        total_out = jnp.zeros(rows_in.shape, jnp.float32)
        for slice_index in range(slices):
            sent_rows = low_back(rows_in)
            gate_pre = low_back(product(sent_rows, gate_e[slice_index]))
            up_pre = low_back(product(sent_rows, up_e[slice_index]))
            hidden = low(silu_product(gate_pre, up_pre))
            total_out = total_out + low_back(low(product(hidden, down_e[slice_index])))
        return total_out
    results = lax.map(jax.checkpoint(single_expert), (grouped, gate_slices, up_slices, down_slices))
    return results.reshape(-1, D)[slot_place].reshape(total_rows, 2, D)

def whole_layer(inputs, attn_gain, w_query, w_key, w_value, w_out, ffn_gain, w_router, shared_gate, shared_up, shared_down, expert_gate, expert_up, expert_down, blocks, routes):
    normed = low(rms_scale(inputs, attn_gain))
    query_rows = low_back(low(product(normed, w_query)))
    key_rows = low_back(low(product(normed, w_key)))
    value_rows = low_back(low(product(normed, w_value)))
    attended = low_back(low(attention(query_rows, key_rows, value_rows, blocks)))
    mixed_rows = inputs + product(attended, w_out)
    normed_ffn = low(rms_scale(mixed_rows, ffn_gain))
    logits = product(normed_ffn, w_router)
    route_onehot = (routes[:, :, None] == jnp.arange(EXPERTS, dtype=jnp.int32)[None, None, :]).astype(jnp.float32)
    chosen = lax.optimization_barrier(jnp.sum(logits[:, None, :] * route_onehot, axis=-1))
    top_logit = lax.optimization_barrier(jnp.max(chosen, axis=-1, keepdims=True))
    gate_weights = jnp.exp(chosen - top_logit)
    gate_share = gate_weights / lax.optimization_barrier(jnp.sum(gate_weights, axis=-1, keepdims=True))
    shared_gate_pre = low_back(product(normed_ffn, shared_gate))
    shared_up_pre = low_back(product(normed_ffn, shared_up))
    shared_hidden = low(silu_product(shared_gate_pre, shared_up_pre))
    shared_out = product(shared_hidden, shared_down)
    picked = expert_rows(normed_ffn, routes, expert_gate, expert_up, expert_down)
    expert_sum = lax.optimization_barrier(jnp.sum(gate_share[:, :, None] * picked, axis=1))
    return mixed_rows + expert_sum + shared_out

def reference(inputs, blocks, routes, attn_gain, w_query, w_key, w_value, w_out, ffn_gain, w_router, shared_gate, shared_up, shared_down, expert_gate, expert_up, expert_down, cotangent):
    params = tuple((arr.astype(jnp.float32) for arr in (inputs, attn_gain, w_query, w_key, w_value, w_out, ffn_gain, w_router, shared_gate, shared_up, shared_down, expert_gate, expert_up, expert_down)))

    def forward(*values):
        return whole_layer(*values, blocks, routes)
    result, pullback = jax.vjp(forward, *params)
    gradients = pullback(cotangent.astype(jnp.float32))
    return (result.astype(jnp.bfloat16), gradients[0], gradients[1], gradients[2], gradients[3], gradients[4], gradients[5], gradients[6], gradients[7], gradients[8], gradients[9], gradients[10], gradients[11], gradients[12], gradients[13])
```

```python
import functools

import jax
import jax.numpy as jnp
import numpy as np
from jax import lax
from jax.experimental import pallas as pl
from jax.experimental.pallas import tpu as pltpu
from jax.sharding import PartitionSpec as P

HEAD_DIM = 64
EXPERTS = 16
CAP = 32
PAIR = 2 * HEAD_DIM
TILE_BLOCKS = 4
BOTH = ("head", "blk")

epsilon = 1e-05
scale_factor = 0.125
masked_value = -1e30
low = jnp.bfloat16
wide = jnp.float32


def matmul(left_side, right_side):
    return jnp.dot(left_side, right_side, preferred_element_type=wide)


def left_contraction(left_side, right_side):
    return lax.dot_general(
        left_side, right_side, (((0,), (0,)), ((), ())), preferred_element_type=wide
    )


def right_contract(left_side, right_side):
    return lax.dot_general(
        left_side, right_side, (((1,), (1,)), ((), ())), preferred_element_type=wide
    )


def rms_scale(values, gain_row):
    return (
        values * lax.rsqrt(jnp.mean(values * values, axis=-1, keepdims=True) + epsilon) * gain_row
    )


def silu_parts(gate_pre, up_pre):
    gate = jax.nn.sigmoid(gate_pre)
    swish = gate_pre * gate
    return swish * up_pre, gate * (1.0 + gate_pre * (1.0 - gate)) * up_pre, swish


def whole_steps(count):
    bits = count.bit_length() - 1
    steps = [functools.partial(flip, bit, bit) for bit in range(bits - 2, 1, -1)]
    return steps + [
        functools.partial(flip, 1, bits - 1),
        functools.partial(flip, bits - 1, 1),
        functools.partial(flip, 0, 0),
    ]


def flip(even_bit, odd_bit, index):
    return index ^ (1 << (odd_bit if index & 1 else even_bit))


def line_steps(count):
    bits = count.bit_length() - 1
    return [functools.partial(flip, bit, bit) for bit in range(bits - 1, -1, -1)]


def slot_sources(count, steps):
    order = [[i] for i in range(count)]
    for step in steps:
        order = [order[i] + order[step(i)] for i in range(count)]
    return np.array(order, np.int32)


def permute(values, axis, count, step):
    return lax.ppermute(values, axis, [(i, step(i)) for i in range(count)])


def gather(values, axis, count, steps):
    held = values[None]
    for step in steps:
        held = jnp.concatenate([held, permute(held, axis, count, step)], axis=0)
    return held


def scatter_sum(slots, axis, count, steps):
    for step in reversed(steps):
        half = slots.shape[0] // 2
        arrived = permute(slots[half:], axis, count, step)
        slots = slots[:half].astype(wide) + arrived.astype(wide)
        if half > 1:
            slots = slots.astype(low)
    return slots[0]


def swap_heads(values):
    return lax.ppermute(values, "head", [(0, 1), (1, 0)])


def head_order(head, own, other):
    return jnp.where(head == 0, jnp.stack([own, other]), jnp.stack([other, own]))


def stack_heads(rows):
    first = lax.broadcasted_iota(jnp.int32, rows.shape, 1) < HEAD_DIM
    zero = jnp.zeros_like(rows)
    return jnp.concatenate([jnp.where(first, rows, zero), jnp.where(first, zero, rows)], axis=0)


def join_heads(stacked):
    half = stacked.shape[0] // 2
    top = stacked[:half]
    first = lax.broadcasted_iota(jnp.int32, top.shape, 1) < HEAD_DIM
    return jnp.where(first, top, stacked[half:])


def load_tile(ref, slots, index):
    return jnp.concatenate(
        [ref[slots[index * TILE_BLOCKS + part]] for part in range(TILE_BLOCKS)], axis=0
    )


def load_ids(ref, index):
    return jnp.concatenate(
        [ref[index * TILE_BLOCKS + part] for part in range(TILE_BLOCKS)], axis=1
    )


def as_column(row):
    return jnp.transpose(jnp.broadcast_to(row, (PAIR, row.shape[1])))[:, :1]


def attend_body(own, slots, bounds, q_ref, k_ref, v_ref, qid_ref, kid_ref, out_ref, lse_ref):
    part = pl.program_id(1)
    stacked = stack_heads(q_ref[0])
    rows = stacked.shape[0]

    def step(masked, index, state):
        top, total, weighted = state
        scores = right_contract(stacked, load_tile(k_ref, slots, index))
        if masked:
            scores = jnp.where(load_ids(kid_ref, index) <= qid_ref[0], scores, masked_value)
        new_top = jnp.maximum(top, jnp.max(scores, axis=-1, keepdims=True))
        weights = jnp.exp(scores - new_top)
        rescale = jnp.exp(top - new_top)
        total = total * rescale + jnp.sum(weights, axis=-1, keepdims=True)
        weighted = weighted * rescale + matmul(weights.astype(low), load_tile(v_ref, slots, index))
        return new_top, total, weighted

    state = (
        jnp.full((rows, 1), masked_value, wide),
        jnp.zeros((rows, 1), wide),
        jnp.zeros((rows, PAIR), wide),
    )
    state = lax.fori_loop(0, bounds[0, part], functools.partial(step, False), state)
    top, total, weighted = lax.fori_loop(
        bounds[0, part], bounds[1, part], functools.partial(step, True), state
    )
    out_ref[0] = join_heads(weighted / total).astype(low)
    lse = jnp.broadcast_to(top + jnp.log(total), (rows, PAIR))
    lse_ref[0, 0] = jnp.transpose(lse)[:1]


def query_body(
    own, slots, bounds, q_ref, k_ref, v_ref, g_ref, lse_ref, delta_ref, qid_ref, kid_ref, dq_ref
):
    part = pl.program_id(1)
    stacked = stack_heads(q_ref[0])
    grads = stack_heads(g_ref[0])
    lse = as_column(lse_ref[0, 0])
    delta = as_column(delta_ref[0, 0])

    def step(masked, index, total):
        keys = load_tile(k_ref, slots, index)
        probs = jnp.exp(right_contract(stacked, keys) - lse)
        if masked:
            probs = jnp.where(load_ids(kid_ref, index) <= qid_ref[0], probs, 0.0)
        moved = right_contract(grads, load_tile(v_ref, slots, index)) - delta
        return total + matmul((probs * moved).astype(low), keys)

    total = jnp.zeros((stacked.shape[0], PAIR), wide)
    total = lax.fori_loop(0, bounds[0, part], functools.partial(step, False), total)
    total = lax.fori_loop(
        bounds[0, part], bounds[1, part], functools.partial(step, True), total
    )
    dq_ref[0] = (join_heads(total) * scale_factor).astype(low)


def key_body(
    own, slots, gslots, bounds, k_ref, v_ref, q_ref, g_ref, stat_ref, kid_ref, qid_ref,
    dk_ref, dv_ref,
):
    pair = pl.program_id(0)
    part = pl.program_id(1)
    pairs = pl.num_programs(0)
    keys = stack_heads(k_ref[0])
    values = stack_heads(v_ref[0])
    rows = keys.shape[0]
    line = pl.num_programs(1)

    def stat_rows(index, which):
        tops, bottoms = [], []
        for piece in range(TILE_BLOCKS):
            slot = gslots[index * TILE_BLOCKS + piece]
            place = (slot // line) * (2 * pairs * line) + (which * pairs + pair) * line + slot % line
            row = stat_ref[place]
            tops.append(row[:, :PAIR])
            bottoms.append(row[:, PAIR:])
        shape = (rows // 2, TILE_BLOCKS * PAIR)
        return jnp.concatenate(
            [
                jnp.broadcast_to(jnp.concatenate(tops, axis=1), shape),
                jnp.broadcast_to(jnp.concatenate(bottoms, axis=1), shape),
            ],
            axis=0,
        )

    def step(masked, index, state):
        dk_total, dv_total = state
        queries = load_tile(q_ref, slots, index)
        grads = load_tile(g_ref, gslots, index)
        probs = jnp.exp(right_contract(keys, queries) - stat_rows(index, 0))
        if masked:
            probs = jnp.where(kid_ref[0] <= load_ids(qid_ref, index), probs, 0.0)
        moved = right_contract(values, grads) - stat_rows(index, 1)
        dk_total = dk_total + matmul((probs * moved).astype(low), queries)
        dv_total = dv_total + matmul(probs.astype(low), grads)
        return dk_total, dv_total

    state = (jnp.zeros((rows, PAIR), wide), jnp.zeros((rows, PAIR), wide))
    state = lax.fori_loop(
        bounds[0, part], bounds[1, part], functools.partial(step, True), state
    )
    dk_total, dv_total = lax.fori_loop(
        bounds[1, part], bounds[2, part], functools.partial(step, False), state
    )
    dk_ref[0] = join_heads(dk_total).astype(low)
    dv_ref[0] = join_heads(dv_total).astype(low)


def attention_call(body, name, tables, arrays, specs, outs, out_specs, grid, cost, count):
    return pl.pallas_call(
        body,
        out_shape=outs,
        grid_spec=pltpu.PrefetchScalarGridSpec(
            num_scalar_prefetch=len(tables), grid=grid, in_specs=specs, out_specs=out_specs
        ),
        compiler_params=pltpu.CompilerParams(
            dimension_semantics=("arbitrary", "arbitrary"),
            vmem_limit_bytes=(12 << 20) + 9 * count * PAIR * PAIR * 2,
        ),
        cost_estimate=pl.CostEstimate(
            flops=cost, bytes_accessed=cost // 512, transcendentals=cost // 512
        ),
        name=name,
    )(*tables, *arrays)


GROUP = 8


def feed_body(
    expert, x_ref, c_ref, route_ref, cat_ref, sd_ref, rt_ref, eg_ref, eu_ref, ed_ref,
    row_ref, out_ref, deg_ref, deu_ref, ded_ref, dcat_ref, dsd_ref,
):
    blocks, tokens, width = x_ref.shape
    count = blocks * tokens

    @pl.when(pl.program_id(0) == 0)
    def clear():
        for ref in (deg_ref, deu_ref, ded_ref, dcat_ref, dsd_ref):
            ref[...] = jnp.zeros_like(ref)

    hidden_rows = x_ref[...].reshape(count, width)
    grad_rows = c_ref[...].reshape(count, width)
    outcome = matmul(hidden_rows, cat_ref[...])
    pre = outcome[:, :PAIR]
    inside = lax.broadcasted_iota(jnp.int32, pre.shape, 1) < HEAD_DIM
    product, gate_slope, up_slope = silu_parts(pre, pltpu.roll(pre, HEAD_DIM, 1))
    shared_hidden = jnp.where(inside, product, 0.0).astype(low)
    shared_hidden_grad = right_contract(grad_rows, sd_ref[...])
    gate_side = jnp.where(inside, shared_hidden_grad * gate_slope, 0.0)
    up_side = jnp.where(inside, shared_hidden_grad * up_slope, 0.0)
    shared_grad = (gate_side + pltpu.roll(up_side, HEAD_DIM, 1)).astype(low)
    dsd_ref[...] += left_contraction(shared_hidden, grad_rows)

    first = route_ref[:, 0, :]
    second = route_ref[:, 1, :]
    is_first = first == expert[0]
    routed = is_first | (second == expert[0])
    before = (
        lax.broadcasted_iota(jnp.int32, (tokens, tokens), 0)
        < lax.broadcasted_iota(jnp.int32, (tokens, tokens), 1)
    )
    routed_low = jnp.where(routed, 1.0, 0.0).astype(low)
    rank = matmul(routed_low, jnp.where(before, 1.0, 0.0).astype(low))
    rank = jnp.where(routed, rank, -1.0)
    slot_ids = lax.broadcasted_iota(jnp.int32, (CAP, tokens), 0).astype(wide)
    expert_ids = lax.broadcasted_iota(jnp.int32, (EXPERTS, tokens), 0)
    selectors, contrasts, shares, leans, picked, picked_grad = [], [], [], [], [], []
    for index in range(blocks):
        span = slice(index * tokens, (index + 1) * tokens)
        logits = jnp.transpose(outcome[span, PAIR:])[:EXPERTS]
        contrast = jnp.where(expert_ids == first[index : index + 1], 1.0, 0.0) - jnp.where(
            expert_ids == second[index : index + 1], 1.0, 0.0
        )
        gap = jnp.sum(logits * contrast, axis=0, keepdims=True)
        share_first = jax.nn.sigmoid(gap)
        share_second = jax.nn.sigmoid(-gap)
        mark = is_first[index : index + 1]
        share = jnp.where(mark, share_first, share_second)
        lean = jnp.where(mark, 1.0, -1.0) * share_first * share_second
        selector = jnp.where(rank[index : index + 1] == slot_ids, 1.0, 0.0)
        selectors.append(selector)
        contrasts.append(contrast)
        shares.append(jnp.sum(selector * share, axis=1, keepdims=True))
        leans.append(jnp.sum(selector * lean, axis=1, keepdims=True))
        selector = selector.astype(low)
        picked.append(matmul(selector, x_ref[index]).astype(low))
        picked_grad.append(matmul(selector, c_ref[index]).astype(low))
    picked = jnp.concatenate(picked, axis=0)
    picked_grad = jnp.concatenate(picked_grad, axis=0).astype(wide)
    share_rows = jnp.concatenate(shares, axis=0)
    lean_rows = jnp.concatenate(leans, axis=0)

    product, gate_slope, up_slope = silu_parts(
        matmul(picked, eg_ref[0]), matmul(picked, eu_ref[0])
    )
    hidden = product.astype(low)
    partial_rows = matmul(hidden, ed_ref[0]).astype(low).astype(wide)
    dots = lean_rows * jnp.sum(picked_grad * partial_rows, axis=1, keepdims=True)
    partial_grad = (share_rows * picked_grad).astype(low)
    shared_rows = (share_rows * partial_rows).astype(low)
    ded_ref[...] += left_contraction(hidden, partial_grad)
    hidden_grad = right_contract(partial_grad, ed_ref[0])
    gate_grad = (hidden_grad * gate_slope).astype(low)
    up_grad = (hidden_grad * up_slope).astype(low)
    deg_ref[...] += left_contraction(picked, gate_grad)
    deu_ref[...] += left_contraction(picked, up_grad)
    row_grad = (
        right_contract(gate_grad, eg_ref[0]) + right_contract(up_grad, eu_ref[0])
    ).astype(low)

    shared_row = right_contract(shared_grad, cat_ref[:, :PAIR])
    shared_out = matmul(shared_hidden, sd_ref[...])
    logits_grads = []
    for index in range(blocks):
        span = slice(index * tokens, (index + 1) * tokens)
        slots = slice(index * CAP, (index + 1) * CAP)
        selector = selectors[index]
        lean = jnp.sum(selector * dots[slots], axis=0, keepdims=True)
        logits_grad = lean * contrasts[index]
        logits_high = logits_grad.astype(low)
        logits_low = (logits_grad - logits_high.astype(wide)).astype(low)
        logits_grad = jnp.concatenate([logits_high, logits_low], axis=0)
        logits_grads.append(logits_grad)
        selector = selector.astype(low)
        row_ref[index] = (
            shared_row[span]
            + left_contraction(
                jnp.concatenate([selector, logits_grad], axis=0),
                jnp.concatenate([row_grad[slots], rt_ref[...]], axis=0),
            )
        ).astype(low)
        out_ref[index] = (
            shared_out[span] + left_contraction(selector, shared_rows[slots])
        ).astype(low)
    dcat_ref[:PAIR] += left_contraction(shared_grad, hidden_rows)
    dcat_ref[PAIR:] += matmul(jnp.concatenate(logits_grads, axis=1), hidden_rows)


def feed_call(expert, hidden_in, second_all, route_rows, cat, sd, rt, gate, up, down):
    count, tokens, width = hidden_in.shape
    units = gate.shape[2]
    block = pl.BlockSpec((GROUP, tokens, width), lambda i, *rest: (i, 0, 0))
    fixed = lambda shape: pl.BlockSpec(
        shape, lambda i, *rest: (0,) * len(shape), pipeline_mode=pl.Buffered(1)
    )
    still = lambda shape: pl.BlockSpec(shape, lambda i, *rest: (0,) * len(shape))
    parts = jax.ShapeDtypeStruct((count, tokens, width), low)
    shapes = ((width, units), (width, units), (units, width), (PAIR + 2 * EXPERTS, width), (PAIR, width))
    return pl.pallas_call(
        feed_body,
        out_shape=(parts, parts) + tuple(jax.ShapeDtypeStruct(shape, wide) for shape in shapes),
        grid_spec=pltpu.PrefetchScalarGridSpec(
            num_scalar_prefetch=1,
            grid=(count // GROUP,),
            in_specs=[
                block,
                block,
                pl.BlockSpec((GROUP, 2, tokens), lambda i, *rest: (i, 0, 0)),
                fixed(cat.shape),
                fixed(sd.shape),
                fixed(rt.shape),
                fixed(gate.shape),
                fixed(up.shape),
                fixed(down.shape),
            ],
            out_specs=(block, block) + tuple(still(shape) for shape in shapes),
        ),
        compiler_params=pltpu.CompilerParams(
            dimension_semantics=("arbitrary",), vmem_limit_bytes=60 << 20
        ),
        cost_estimate=pl.CostEstimate(
            flops=count * (CAP * width * units * 18 + tokens * width * PAIR * 12),
            bytes_accessed=count * tokens * width * 8 + width * units * 18,
            transcendentals=count * CAP * units,
        ),
        name="feed",
    )(expert, hidden_in, second_all, route_rows, cat, sd, rt, gate, up, down)


def shards(
    inputs,
    blocks,
    routes,
    attn_gain,
    w_query,
    w_key,
    w_value,
    w_out,
    ffn_gain,
    w_router,
    shared_gate,
    shared_up,
    shared_down,
    expert_gate,
    expert_up,
    expert_down,
    cotangent,
):
    heads, line = lax.axis_size("head"), lax.axis_size("blk")
    count = heads * line
    head, spot = lax.axis_index("head"), lax.axis_index("blk")
    device = head * line + spot
    tokens, width = inputs.shape
    total = count * tokens
    group = width // heads
    pairs = group // PAIR
    rows = w_query.shape[0]
    steps, short_steps = whole_steps(count), line_steps(line)
    sources = slot_sources(count, steps)
    places = jnp.asarray(np.argsort(sources, axis=1).astype(np.int32))[device]
    short_sources = slot_sources(line, short_steps)
    short_order = jnp.asarray(short_sources)[spot]
    short_places = jnp.asarray(np.argsort(short_sources, axis=1).astype(np.int32))[spot]

    def pad_rows(flat):
        extra = -flat.shape[0] % width
        return jnp.pad(flat, (0, extra)).reshape(-1, width)

    extras = pad_rows(jnp.concatenate([attn_gain, ffn_gain, w_router.reshape(-1)]))
    first = jnp.concatenate([inputs, w_query, w_key, w_value, extras], axis=0)
    first = jnp.pad(first, ((0, -first.shape[0] % 16), (0, 0)))
    first_all = gather(first, BOTH, count, steps)
    second = jnp.concatenate([cotangent, w_out, pad_rows(routes.T.reshape(-1).astype(low))], axis=0)
    second = jnp.pad(second, ((0, -second.shape[0] % 16), (0, 0)))
    second_all = gather(second, BOTH, count, steps)
    shared_slice = shared_gate.shape[1] // count
    shared_pack = jnp.stack(
        [
            shared_gate.reshape(rows, count, shared_slice),
            shared_up.reshape(rows, count, shared_slice),
        ],
        axis=2,
    ).reshape(rows, count * 2 * shared_slice)
    shared_in = lax.all_to_all(shared_pack, BOTH, split_axis=1, concat_axis=0, tiled=True)

    weights = jnp.take(first_all[:, tokens:], places, axis=0, mode="clip")
    qkv_weight = lax.dynamic_slice_in_dim(
        weights[:, : 3 * rows].reshape(count, 3, rows, width), head * group, group, 3
    )
    qkv_weight = qkv_weight.transpose(0, 2, 1, 3).reshape(width, 3 * group)
    flat = weights[:, 3 * rows]
    gain_first = flat[:, :rows].reshape(width).astype(wide)
    gain_second = flat[:, rows : 2 * rows].reshape(width).astype(wide)
    router = flat[:, 2 * rows : 2 * rows + rows * EXPERTS].reshape(width, EXPERTS)

    inputs_slots = first_all[:, :tokens].reshape(total, width).astype(wide)
    normed = rms_scale(inputs_slots, gain_first).astype(low)
    column_scale = jnp.where(jnp.arange(3 * group) < group, scale_factor, 1.0)
    qkv = (matmul(normed, qkv_weight) * column_scale).astype(low).reshape(
        count, tokens, 3 * group
    )
    own_blocks = jnp.arange(heads, dtype=jnp.int32) * line + spot
    own_slots = places[own_blocks]
    normed_own = jnp.take(normed.reshape(count, tokens, width), own_slots, axis=0, mode="clip")
    normed_own = normed_own.reshape(heads * tokens, width)

    tile = TILE_BLOCKS * tokens
    own_ids = jnp.take(blocks.reshape(count, tokens), own_blocks, axis=0, mode="clip")
    low_id, high_id = own_ids[:, :1], own_ids[:, -1:]

    def counted(test):
        return jnp.sum(test, axis=1, dtype=jnp.int32)

    query_bounds = jnp.stack(
        [
            counted(blocks[None] <= low_id) // tile,
            (counted(blocks[None] <= high_id) + tile - 1) // tile,
        ]
    )
    key_bounds = jnp.stack(
        [
            counted(blocks[None] < low_id) // tile,
            (counted(blocks[None] < high_id) + tile - 1) // tile,
            jnp.full((heads,), total // tile, jnp.int32),
        ]
    )
    id_columns = jnp.tile(own_ids, (1, 2))[:, :, None]
    id_rows = blocks.reshape(count, 1, tokens)

    own_spec = lambda column: pl.BlockSpec(
        (1, tokens, PAIR), lambda p, j, own, *rest: (own[j], 0, column + p)
    )
    all_spec = lambda column: pl.BlockSpec(
        (count, tokens, PAIR), lambda p, j, *rest: (0, 0, column + p)
    )
    part_spec = pl.BlockSpec((1, tokens, PAIR), lambda p, j, *rest: (j, 0, p))
    stat_spec = pl.BlockSpec((1, 1, 1, 2 * tokens), lambda p, j, *rest: (p, j, 0, 0))
    column_spec = pl.BlockSpec((1, 2 * tokens, 1), lambda p, j, *rest: (j, 0, 0))
    ids_spec = pl.BlockSpec((count, 1, tokens), lambda p, j, *rest: (0, 0, 0))
    part_shape = jax.ShapeDtypeStruct((heads, tokens, group), low)
    stat_shape = jax.ShapeDtypeStruct((pairs, heads, 1, 2 * tokens), wide)
    grid = (pairs, heads)
    unit = 2 * heads * tokens * total * group

    attended_own, lse = attention_call(
        attend_body,
        "attend",
        (own_slots, places, query_bounds),
        (qkv, qkv, qkv, id_columns, id_rows),
        [own_spec(0), all_spec(pairs), all_spec(2 * pairs), column_spec, ids_spec],
        (part_shape, stat_shape),
        (part_spec, stat_spec),
        grid,
        2 * unit,
        count,
    )
    attended_back = swap_heads(lax.dynamic_index_in_dim(attended_own, 1 - head, 0, False))
    attended_kept = lax.dynamic_index_in_dim(attended_own, head, 0, False)
    attended = jnp.where(
        head == 0,
        jnp.concatenate([attended_kept, attended_back], axis=1),
        jnp.concatenate([attended_back, attended_kept], axis=1),
    )
    full_out = jnp.take(second_all[:, tokens : tokens + rows], places, axis=0, mode="clip")
    full_out = full_out.reshape(width, width)
    inputs_wide = inputs.astype(wide)
    mixed_rows = inputs_wide + matmul(attended, full_out)
    normed_ffn = rms_scale(mixed_rows, gain_second).astype(low)

    hidden_in = gather(normed_ffn, BOTH, count, steps)
    route_rows = second_all[:, tokens + rows :].reshape(count, -1)[:, : 2 * tokens]
    route_rows = route_rows.reshape(count, 2, tokens).astype(jnp.int32)
    expert = (device % EXPERTS).astype(jnp.int32).reshape(1)
    half_pad = HEAD_DIM - shared_slice
    shared_pair = jnp.pad(
        shared_in.reshape(width, 2, shared_slice), ((0, 0), (0, 0), (0, half_pad))
    ).reshape(width, PAIR)
    feed_weight = jnp.concatenate(
        [shared_pair, router, jnp.zeros((width, PAIR - EXPERTS), low)], axis=1
    )
    down_pad = jnp.pad(shared_down, ((0, PAIR - shared_slice), (0, 0)))
    router_rows = jnp.transpose(jnp.concatenate([router, router], axis=1))
    (
        row_part,
        out_part,
        grad_egate,
        grad_eup,
        grad_edown,
        grad_feed,
        grad_sdown,
    ) = feed_call(
        expert, hidden_in, second_all, route_rows, feed_weight, down_pad, router_rows,
        expert_gate, expert_up, expert_down,
    )
    grad_sdown = grad_sdown[:shared_slice]
    grad_router = jnp.transpose(
        grad_feed[PAIR : PAIR + EXPERTS] + grad_feed[PAIR + EXPERTS : PAIR + 2 * EXPERTS]
    )
    grad_shared = jnp.transpose(
        grad_feed[:PAIR].reshape(2, HEAD_DIM, width)[:, :shared_slice].reshape(-1, width)
    )
    normed_ffn_grad = scatter_sum(row_part, BOTH, count, steps)
    feed_out = scatter_sum(out_part, BOTH, count, steps)
    output = (mixed_rows + feed_out).astype(low)

    grad_shared_back = lax.all_to_all(grad_shared, BOTH, split_axis=0, concat_axis=1, tiled=True)
    grad_shared_back = grad_shared_back.reshape(rows, count, 2, shared_slice)
    grad_sgate = grad_shared_back[:, :, 0].reshape(rows, -1)
    grad_sup = grad_shared_back[:, :, 1].reshape(rows, -1)

    unused_second, second_pull = jax.vjp(rms_scale, mixed_rows, gain_second)
    mixed_part, grad_gain_ffn = second_pull(normed_ffn_grad)
    mixed_grad = cotangent.astype(wide) + mixed_part
    mixed_low = mixed_grad.astype(low)
    mixed_pair = head_order(head, mixed_low, swap_heads(mixed_low)).reshape(heads * tokens, width)
    own_out = lax.dynamic_slice_in_dim(full_out, head * group, group, 0)
    attended_grad = right_contract(mixed_pair, own_out).astype(low)
    attended_flat = attended_own.reshape(heads * tokens, group)
    grad_wout = left_contraction(attended_flat, mixed_pair)
    head_marks = (
        jnp.arange(group)[None] // HEAD_DIM == jnp.arange(2 * pairs)[:, None]
    ).astype(wide)
    delta = lax.dot_general(
        head_marks,
        attended_grad.astype(wide) * attended_flat.astype(wide),
        (((1,), (1,)), ((), ())),
        precision=lax.Precision.HIGHEST,
    )
    delta = (
        delta.reshape(pairs, 2, heads, tokens)
        .transpose(0, 2, 1, 3)
        .reshape(pairs, heads, 1, 2 * tokens)
    )
    stats = jnp.stack([lse, delta]).reshape(2 * pairs * heads, 2 * tokens)
    stats_all = gather(stats, "blk", line, short_steps).reshape(-1, 1, 2 * tokens)
    grad_parts = attended_grad.reshape(heads, tokens, group)
    grads_all = gather(grad_parts, "blk", line, short_steps).reshape(count, tokens, group)
    block_ids = jnp.arange(count, dtype=jnp.int32)
    grad_slots = short_places[block_ids % line] * heads + block_ids // line

    query_grad = attention_call(
        query_body,
        "query_gradient",
        (own_slots, places, query_bounds),
        (qkv, qkv, qkv, grad_parts, lse, delta, id_columns, id_rows),
        [
            own_spec(0),
            all_spec(pairs),
            all_spec(2 * pairs),
            part_spec,
            stat_spec,
            stat_spec,
            column_spec,
            ids_spec,
        ],
        part_shape,
        part_spec,
        grid,
        3 * unit,
        count,
    )
    key_grad, value_grad = attention_call(
        key_body,
        "key_gradient",
        (own_slots, places, grad_slots, key_bounds),
        (qkv, qkv, qkv, grads_all, stats_all, id_columns, id_rows),
        [
            own_spec(pairs),
            own_spec(2 * pairs),
            all_spec(0),
            all_spec(0),
            pl.BlockSpec(stats_all.shape, lambda p, j, *rest: (0, 0, 0)),
            column_spec,
            ids_spec,
        ],
        (part_shape, part_shape),
        (part_spec, part_spec),
        grid,
        4 * unit,
        count,
    )

    qkv_grad = jnp.concatenate([query_grad, key_grad, value_grad], axis=2).reshape(
        heads * tokens, 3 * group
    )
    normed_part = right_contract(qkv_grad, qkv_weight)
    grad_qkv = left_contraction(normed_own, qkv_grad)

    pieces = grad_qkv.reshape(heads, line, rows, 3 * group).transpose(1, 0, 2, 3).astype(low)
    pieces = jnp.take(pieces, short_order, axis=0, mode="clip")
    summed = scatter_sum(pieces, "blk", line, short_steps)
    summed_back = swap_heads(lax.dynamic_index_in_dim(summed, 1 - head, 0, False))
    summed_kept = lax.dynamic_index_in_dim(summed, head, 0, False)
    joined = head_order(head, summed_kept, summed_back).reshape(heads, rows, 3, group)
    joined = joined.transpose(2, 1, 0, 3).reshape(3, rows, width)
    out_pieces = jnp.take(
        grad_wout.reshape(line, rows, width).astype(low), short_order, axis=0, mode="clip"
    )
    grad_wout_own = scatter_sum(out_pieces, "blk", line, short_steps)

    normed_parts = normed_part.reshape(heads, tokens, width)
    arrived = swap_heads(lax.dynamic_index_in_dim(normed_parts, 1 - head, 0, False).astype(low))
    normed_grad = lax.dynamic_index_in_dim(normed_parts, head, 0, False) + arrived.astype(wide)
    unused_first, first_pull = jax.vjp(lambda rows_in: rms_scale(rows_in, gain_first), inputs_wide)
    grad_inputs = mixed_grad + first_pull(normed_grad)[0]
    pair_inputs = jnp.take(
        first_all[:, :tokens], own_slots, axis=0, mode="clip"
    ).reshape(heads * tokens, width).astype(wide)
    grad_gain_attn = jnp.sum(
        normed_part * rms_scale(pair_inputs, jnp.ones((width,), wide)), axis=0
    )

    def small_sum(values):
        moved = lax.all_to_all(
            values.reshape(count, -1), BOTH, split_axis=0, concat_axis=0, tiled=True
        )
        return jnp.sum(moved, axis=0).reshape(rows, -1)

    early = small_sum(jnp.concatenate([grad_gain_ffn[:, None], grad_router], axis=1))
    late = small_sum(grad_gain_attn[:, None])
    return (
        output,
        grad_inputs,
        late[:, 0],
        joined[0].astype(wide),
        joined[1].astype(wide),
        joined[2].astype(wide),
        grad_wout_own.astype(wide),
        early[:, 0],
        early[:, 1:],
        grad_sgate,
        grad_sup,
        grad_sdown,
        grad_egate[None],
        grad_eup[None],
        grad_edown[None],
    )


def solution(mesh):
    both = P(BOTH)
    rows = P(BOTH, None)
    slabs = P(BOTH, None, None)
    return jax.shard_map(
        shards,
        mesh=mesh,
        in_specs=(
            rows, P(), rows, both, rows, rows, rows, rows, both, rows, rows, rows, rows,
            slabs, slabs, slabs, rows,
        ),
        out_specs=(
            rows, rows, both, rows, rows, rows, rows, both, rows, rows, rows, rows,
            slabs, slabs, slabs,
        ),
        check_vma=False,
    )
```

```python
import functools

import jax
import jax.numpy as jnp
import numpy as np
from jax import lax
from jax.experimental import pallas as pl
from jax.experimental.pallas import tpu as pltpu
from jax.sharding import PartitionSpec as P

HEAD_DIM = 64
EXPERTS = 16
CAP = 32
PAIR = 2 * HEAD_DIM
TILE_BLOCKS = 4
BOTH = ("head", "blk")

epsilon = 1e-05
scale_factor = 0.125
masked_value = -1e30
low = jnp.bfloat16
wide = jnp.float32


def matmul(left_side, right_side):
    return jnp.dot(left_side, right_side, preferred_element_type=wide)


def left_contraction(left_side, right_side):
    return lax.dot_general(
        left_side, right_side, (((0,), (0,)), ((), ())), preferred_element_type=wide
    )


def right_contract(left_side, right_side):
    return lax.dot_general(
        left_side, right_side, (((1,), (1,)), ((), ())), preferred_element_type=wide
    )


def rms_scale(values, gain_row):
    return (
        values * lax.rsqrt(jnp.mean(values * values, axis=-1, keepdims=True) + epsilon) * gain_row
    )


def silu_parts(gate_pre, up_pre):
    gate = jax.nn.sigmoid(gate_pre)
    swish = gate_pre * gate
    return swish * up_pre, gate * (1.0 + gate_pre * (1.0 - gate)) * up_pre, swish


def whole_steps(count):
    bits = count.bit_length() - 1
    steps = [functools.partial(flip, bit, bit) for bit in range(bits - 2, 1, -1)]
    return steps + [
        functools.partial(flip, 1, bits - 1),
        functools.partial(flip, bits - 1, 1),
        functools.partial(flip, 0, 0),
    ]


def flip(even_bit, odd_bit, index):
    return index ^ (1 << (odd_bit if index & 1 else even_bit))


def line_steps(count):
    bits = count.bit_length() - 1
    return [functools.partial(flip, bit, bit) for bit in range(bits - 1, -1, -1)]


def slot_sources(count, steps):
    order = [[i] for i in range(count)]
    for step in steps:
        order = [order[i] + order[step(i)] for i in range(count)]
    return np.array(order, np.int32)


def permute(values, axis, count, step):
    return lax.ppermute(values, axis, [(i, step(i)) for i in range(count)])


def after(value, *needed):
    return lax.optimization_barrier((value,) + needed)[0]


def two_parts(values):
    high = lax.reduce_precision(values, 8, 7)
    return [high.astype(low), (values - high).astype(low)]


def grow(held, arrived):
    return jnp.concatenate([held, arrived], axis=0)


def gather(values, axis, count, steps):
    held = values[None]
    for step in steps:
        held = grow(held, permute(held, axis, count, step))
    return held


def upper(terms):
    half = terms[0].shape[0] // 2
    return sum(term[half:].astype(wide) for term in terms).astype(low)


def lower(terms):
    half = terms[0].shape[0] // 2
    return [term[:half] for term in terms]


def scatter_step(terms, axis, count, step):
    return lower(terms) + [permute(upper(terms), axis, count, step)]


def finish(terms):
    return sum(term[0].astype(wide) for term in terms)


def scatter_sum(slots, axis, count, steps):
    terms = [slots]
    for step in reversed(steps):
        terms = scatter_step(terms, axis, count, step)
    return finish(terms)


def swap_heads(values):
    return lax.ppermute(values, "head", [(0, 1), (1, 0)])


def head_order(head, own, other):
    return jnp.where(head == 0, jnp.stack([own, other]), jnp.stack([other, own]))


def stack_heads(rows):
    first = lax.broadcasted_iota(jnp.int32, rows.shape, 1) < HEAD_DIM
    zero = jnp.zeros_like(rows)
    return jnp.concatenate([jnp.where(first, rows, zero), jnp.where(first, zero, rows)], axis=0)


def join_heads(stacked):
    half = stacked.shape[0] // 2
    top = stacked[:half]
    first = lax.broadcasted_iota(jnp.int32, top.shape, 1) < HEAD_DIM
    return jnp.where(first, top, stacked[half:])


def load_tile(ref, slots, index):
    return jnp.concatenate(
        [ref[slots[index * TILE_BLOCKS + part]] for part in range(TILE_BLOCKS)], axis=0
    )


def load_ids(ref, index):
    return jnp.concatenate(
        [ref[index * TILE_BLOCKS + part] for part in range(TILE_BLOCKS)], axis=1
    )


def as_column(row):
    return jnp.transpose(jnp.broadcast_to(row, (PAIR, row.shape[1])))[:, :1]


def attend_body(own, slots, bounds, q_ref, k_ref, v_ref, qid_ref, kid_ref, out_ref, lse_ref):
    part = pl.program_id(1)
    stacked = stack_heads(q_ref[0])
    rows = stacked.shape[0]

    def step(masked, index, state):
        top, total, weighted = state
        scores = right_contract(stacked, load_tile(k_ref, slots, index))
        if masked:
            scores = jnp.where(load_ids(kid_ref, index) <= qid_ref[0], scores, masked_value)
        new_top = jnp.maximum(top, jnp.max(scores, axis=-1, keepdims=True))
        weights = jnp.exp(scores - new_top)
        rescale = jnp.exp(top - new_top)
        total = total * rescale + jnp.sum(weights, axis=-1, keepdims=True)
        weighted = weighted * rescale + matmul(weights.astype(low), load_tile(v_ref, slots, index))
        return new_top, total, weighted

    state = (
        jnp.full((rows, 1), masked_value, wide),
        jnp.zeros((rows, 1), wide),
        jnp.zeros((rows, PAIR), wide),
    )
    state = lax.fori_loop(0, bounds[0, part], functools.partial(step, False), state)
    top, total, weighted = lax.fori_loop(
        bounds[0, part], bounds[1, part], functools.partial(step, True), state
    )
    out_ref[0] = join_heads(weighted / total).astype(low)
    lse = jnp.broadcast_to(top + jnp.log(total), (rows, PAIR))
    lse_ref[0, 0] = jnp.transpose(lse)[:1]


def query_body(
    own, slots, bounds, q_ref, k_ref, v_ref, g_ref, lse_ref, delta_ref, qid_ref, kid_ref, dq_ref
):
    part = pl.program_id(1)
    stacked = stack_heads(q_ref[0])
    grads = stack_heads(g_ref[0])
    lse = as_column(lse_ref[0, 0])
    delta = as_column(delta_ref[0, 0])

    def step(masked, index, total):
        keys = load_tile(k_ref, slots, index)
        probs = jnp.exp(right_contract(stacked, keys) - lse)
        if masked:
            probs = jnp.where(load_ids(kid_ref, index) <= qid_ref[0], probs, 0.0)
        moved = right_contract(grads, load_tile(v_ref, slots, index)) - delta
        return total + matmul((probs * moved).astype(low), keys)

    total = jnp.zeros((stacked.shape[0], PAIR), wide)
    total = lax.fori_loop(0, bounds[0, part], functools.partial(step, False), total)
    total = lax.fori_loop(
        bounds[0, part], bounds[1, part], functools.partial(step, True), total
    )
    dq_ref[0] = (join_heads(total) * scale_factor).astype(low)


def key_body(
    own, slots, gslots, bounds, k_ref, v_ref, q_ref, g_ref, stat_ref, kid_ref, qid_ref,
    dk_ref, dv_ref,
):
    pair = pl.program_id(0)
    part = pl.program_id(1)
    pairs = pl.num_programs(0)
    keys = stack_heads(k_ref[0])
    values = stack_heads(v_ref[0])
    rows = keys.shape[0]

    def stat_rows(index, which):
        tops, bottoms = [], []
        for piece in range(TILE_BLOCKS):
            slot = gslots[index * TILE_BLOCKS + piece]
            place = slot * (2 * pairs) + which * pairs + pair
            row = stat_ref[place]
            tops.append(row[:, :PAIR])
            bottoms.append(row[:, PAIR:])
        shape = (rows // 2, TILE_BLOCKS * PAIR)
        return jnp.concatenate(
            [
                jnp.broadcast_to(jnp.concatenate(tops, axis=1), shape),
                jnp.broadcast_to(jnp.concatenate(bottoms, axis=1), shape),
            ],
            axis=0,
        )

    def step(masked, index, state):
        dk_total, dv_total = state
        queries = load_tile(q_ref, slots, index)
        grads = load_tile(g_ref, gslots, index)
        probs = jnp.exp(right_contract(keys, queries) - stat_rows(index, 0))
        if masked:
            probs = jnp.where(kid_ref[0] <= load_ids(qid_ref, index), probs, 0.0)
        moved = right_contract(values, grads) - stat_rows(index, 1)
        dk_total = dk_total + matmul((probs * moved).astype(low), queries)
        dv_total = dv_total + matmul(probs.astype(low), grads)
        return dk_total, dv_total

    state = (jnp.zeros((rows, PAIR), wide), jnp.zeros((rows, PAIR), wide))
    state = lax.fori_loop(
        bounds[0, part], bounds[1, part], functools.partial(step, True), state
    )
    dk_total, dv_total = lax.fori_loop(
        bounds[1, part], bounds[2, part], functools.partial(step, False), state
    )
    dk_ref[0] = join_heads(dk_total).astype(low)
    dv_ref[0] = join_heads(dv_total).astype(low)


def attention_call(body, name, tables, arrays, specs, outs, out_specs, grid, cost, count):
    return pl.pallas_call(
        body,
        out_shape=outs,
        grid_spec=pltpu.PrefetchScalarGridSpec(
            num_scalar_prefetch=len(tables), grid=grid, in_specs=specs, out_specs=out_specs
        ),
        compiler_params=pltpu.CompilerParams(
            dimension_semantics=("arbitrary", "arbitrary"),
            vmem_limit_bytes=60 << 20,
        ),
        cost_estimate=pl.CostEstimate(
            flops=8 * cost, bytes_accessed=cost // 512, transcendentals=cost // 512
        ),
        name=name,
    )(*tables, *arrays)


def unpack_body(slots, near_ref, far_ref, qkv_ref, out_ref):
    half, heads, unused, group = near_ref.shape
    line = 2 * half
    rows = qkv_ref.shape[0] // (heads * line)
    for spot in range(line):
        slot = slots[spot]
        is_near = slot < half
        low_slot, high_slot = jnp.minimum(slot, half - 1), jnp.maximum(slot - half, 0)
        for source in range(heads):
            block = jnp.where(is_near, near_ref[low_slot, source], far_ref[high_slot, source])
            first = (source * line + spot) * rows
            for part in range(3):
                qkv_ref[first : first + rows, part * group : (part + 1) * group] = block[
                    part * rows : (part + 1) * rows
                ]
            for part in range(heads):
                piece = block[(3 + part) * rows : (4 + part) * rows]
                out_ref[first : first + rows, part * group : (part + 1) * group] = piece


def unpack_call(slots, near, far, width):
    half, heads, unused, group = near.shape
    whole = lambda shape: pl.BlockSpec(shape, lambda i, *rest: (0,) * len(shape))
    shapes = ((width, 3 * group), (width, width))
    return pl.pallas_call(
        unpack_body,
        out_shape=tuple(jax.ShapeDtypeStruct(shape, low) for shape in shapes),
        grid_spec=pltpu.PrefetchScalarGridSpec(
            num_scalar_prefetch=1,
            grid=(1,),
            in_specs=[whole(near.shape), whole(far.shape)],
            out_specs=tuple(whole(shape) for shape in shapes),
        ),
        compiler_params=pltpu.CompilerParams(
            dimension_semantics=("arbitrary",), vmem_limit_bytes=32 << 20
        ),
        cost_estimate=pl.CostEstimate(
            flops=0, bytes_accessed=8 * near.size, transcendentals=0
        ),
        name="unpack",
    )(slots, near, far)


PROJECT = 4


def project_body(x_ref, gain_ref, weight_ref, scale_ref, *refs):
    out_ref, token_ref = refs[-2:]
    token_ref[...] = jnp.zeros_like(token_ref)
    blocks, tokens, width = x_ref.shape
    rows = x_ref[...].reshape(blocks * tokens, width).astype(wide)
    normed = rms_scale(rows, gain_ref[...]).astype(low)
    out = matmul(normed, weight_ref[...]) * scale_ref[...]
    out_ref[...] = out.astype(low).reshape(blocks, tokens, -1)


def project_call(rows, gain, weight, scale, count, before):
    blocks, tokens, width = rows.shape
    columns = weight.shape[1]
    skip = 0 if before is None else (count - blocks) // PROJECT
    fixed = lambda array: pl.BlockSpec(array.shape, lambda i: (0, 0))
    more = [] if before is None else [before]
    return pl.pallas_call(
        project_body,
        out_shape=(
            jax.ShapeDtypeStruct((count, tokens, columns), low),
            jax.ShapeDtypeStruct((8, PAIR), wide),
        ),
        grid=(blocks // PROJECT,),
        in_specs=[
            pl.BlockSpec((PROJECT, tokens, width), lambda i: (i, 0, 0)),
            fixed(gain),
            fixed(weight),
            fixed(scale),
        ]
        + [pl.BlockSpec(memory_space=pl.ANY)] * len(more),
        out_specs=(
            pl.BlockSpec((PROJECT, tokens, columns), lambda i: (i + skip, 0, 0)),
            pl.BlockSpec((8, PAIR), lambda i: (0, 0)),
        ),
        input_output_aliases={4: 0} if more else {},
        compiler_params=pltpu.CompilerParams(
            dimension_semantics=("arbitrary",), vmem_limit_bytes=60 << 20
        ),
        cost_estimate=pl.CostEstimate(
            flops=4 * blocks * tokens * width * columns,
            bytes_accessed=2 * blocks * tokens * (width + columns),
            transcendentals=0,
        ),
        name="project",
    )(rows, gain, weight, scale, *more)


GROUP = 8


def feed_body(
    expert, order, x_near, x_far, c_all, route_ref, cat_ref, sd_ref, rt_ref, eg_ref, eu_ref, ed_ref,
    row_near, row_far, out_near, out_far, deg_ref, deu_ref, ded_ref, dcat_ref, dsd_ref,
    x_bufs, c_bufs, row_bufs, out_bufs, in_sems, out_sems,
):
    unused, blocks, tokens, width = x_bufs.shape
    count = blocks * tokens
    turn = pl.program_id(0)
    turns = pl.num_programs(0)
    slot = turn % 2

    def loads(index, place, near):
        first = (index if near else index - turns // 2) * blocks
        source = x_near if near else x_far
        return [
            pltpu.make_async_copy(
                source.at[pl.ds(first, blocks)], x_bufs.at[place], in_sems.at[0, place]
            )
        ] + [
            pltpu.make_async_copy(
                c_all.at[order[index * blocks + part]], c_bufs.at[place, part], in_sems.at[1, place]
            )
            for part in range(blocks)
        ]

    def stores(index, place, near):
        first = (index if near else index - turns // 2) * blocks
        pairs = (
            ((row_near, row_bufs), (out_near, out_bufs))
            if near
            else ((row_far, row_bufs), (out_far, out_bufs))
        )
        return [
            pltpu.make_async_copy(
                source.at[place], target.at[pl.ds(first, blocks)], out_sems.at[number, place]
            )
            for number, (target, source) in enumerate(pairs)
        ]

    def begin(copies, index, place):
        @pl.when(index < turns // 2)
        def from_near():
            for copy in copies(index, place, True):
                copy.start()

        @pl.when(index >= turns // 2)
        def from_far():
            for copy in copies(index, place, False):
                copy.start()

    @pl.when(turn == 0)
    def clear():
        begin(loads, turn, slot)
        for ref in (deg_ref, deu_ref, ded_ref, dcat_ref, dsd_ref):
            ref[...] = jnp.zeros_like(ref)

    @pl.when(turn + 1 < turns)
    def ahead():
        begin(loads, turn + 1, 1 - slot)

    pltpu.make_async_copy(
        x_near.at[pl.ds(0, blocks)], x_bufs.at[slot], in_sems.at[0, slot]
    ).wait()
    pltpu.make_async_copy(
        c_all.at[pl.ds(0, blocks)], c_bufs.at[slot], in_sems.at[1, slot]
    ).wait()

    @pl.when(turn >= 2)
    def free():
        for copy in stores(0, slot, True):
            copy.wait()

    x_ref, c_ref = x_bufs.at[slot], c_bufs.at[slot]
    row_ref, out_ref = row_bufs.at[slot], out_bufs.at[slot]
    hidden_rows = x_ref[...].reshape(count, width)
    grad_rows = c_ref[...].reshape(count, width)
    outcome = matmul(hidden_rows, cat_ref[...])
    pre = outcome[:, :PAIR]
    inside = lax.broadcasted_iota(jnp.int32, pre.shape, 1) < HEAD_DIM
    product, gate_slope, up_slope = silu_parts(pre, pltpu.roll(pre, HEAD_DIM, 1))
    shared_hidden = jnp.where(inside, product, 0.0).astype(low)
    shared_hidden_grad = right_contract(grad_rows, sd_ref[...])
    gate_side = jnp.where(inside, shared_hidden_grad * gate_slope, 0.0)
    up_side = jnp.where(inside, shared_hidden_grad * up_slope, 0.0)
    shared_grad = (gate_side + pltpu.roll(up_side, HEAD_DIM, 1)).astype(low)
    dsd_ref[...] += left_contraction(shared_hidden, grad_rows)

    first = route_ref[:, 0, :]
    second = route_ref[:, 1, :]
    is_first = first == expert[0]
    routed = is_first | (second == expert[0])
    before = (
        lax.broadcasted_iota(jnp.int32, (tokens, tokens), 0)
        < lax.broadcasted_iota(jnp.int32, (tokens, tokens), 1)
    )
    routed_low = jnp.where(routed, 1.0, 0.0).astype(low)
    rank = matmul(routed_low, jnp.where(before, 1.0, 0.0).astype(low))
    rank = jnp.where(routed, rank, -1.0)
    slot_ids = lax.broadcasted_iota(jnp.int32, (CAP, tokens), 0).astype(wide)
    expert_ids = lax.broadcasted_iota(jnp.int32, (EXPERTS, tokens), 0)
    selectors, contrasts, shares, leans, picked, picked_grad = [], [], [], [], [], []
    for index in range(blocks):
        span = slice(index * tokens, (index + 1) * tokens)
        logits = jnp.transpose(outcome[span, PAIR:])[:EXPERTS]
        contrast = jnp.where(expert_ids == first[index : index + 1], 1.0, 0.0) - jnp.where(
            expert_ids == second[index : index + 1], 1.0, 0.0
        )
        gap = jnp.sum(logits * contrast, axis=0, keepdims=True)
        share_first = jax.nn.sigmoid(gap)
        share_second = jax.nn.sigmoid(-gap)
        mark = is_first[index : index + 1]
        share = jnp.where(mark, share_first, share_second)
        lean = jnp.where(mark, 1.0, -1.0) * share_first * share_second
        selector = jnp.where(rank[index : index + 1] == slot_ids, 1.0, 0.0)
        selectors.append(selector)
        contrasts.append(contrast)
        shares.append(jnp.sum(selector * share, axis=1, keepdims=True))
        leans.append(jnp.sum(selector * lean, axis=1, keepdims=True))
        selector = selector.astype(low)
        picked.append(matmul(selector, x_ref[index]).astype(low))
        picked_grad.append(matmul(selector, c_ref[index]).astype(low))
    picked = jnp.concatenate(picked, axis=0)
    picked_grad = jnp.concatenate(picked_grad, axis=0).astype(wide)
    share_rows = jnp.concatenate(shares, axis=0)
    lean_rows = jnp.concatenate(leans, axis=0)

    product, gate_slope, up_slope = silu_parts(
        matmul(picked, eg_ref[0]), matmul(picked, eu_ref[0])
    )
    hidden = product.astype(low)
    partial_rows = matmul(hidden, ed_ref[0]).astype(low).astype(wide)
    dots = lean_rows * jnp.sum(picked_grad * partial_rows, axis=1, keepdims=True)
    partial_grad = (share_rows * picked_grad).astype(low)
    shared_rows = (share_rows * partial_rows).astype(low)
    ded_ref[...] += left_contraction(hidden, partial_grad)
    hidden_grad = right_contract(partial_grad, ed_ref[0])
    gate_grad = (hidden_grad * gate_slope).astype(low)
    up_grad = (hidden_grad * up_slope).astype(low)
    deg_ref[...] += left_contraction(picked, gate_grad)
    deu_ref[...] += left_contraction(picked, up_grad)
    row_grad = (
        right_contract(gate_grad, eg_ref[0]) + right_contract(up_grad, eu_ref[0])
    ).astype(low)

    shared_row = right_contract(shared_grad, cat_ref[:, :PAIR])
    shared_out = matmul(shared_hidden, sd_ref[...])
    logits_grads = []
    for index in range(blocks):
        span = slice(index * tokens, (index + 1) * tokens)
        slots = slice(index * CAP, (index + 1) * CAP)
        selector = selectors[index]
        lean = jnp.sum(selector * dots[slots], axis=0, keepdims=True)
        logits_grad = lean * contrasts[index]
        logits_high = logits_grad.astype(low)
        logits_low = (logits_grad - logits_high.astype(wide)).astype(low)
        logits_grad = jnp.concatenate([logits_high, logits_low], axis=0)
        logits_grads.append(logits_grad)
        selector = selector.astype(low)
        row_ref[index] = (
            shared_row[span]
            + left_contraction(
                jnp.concatenate([selector, logits_grad], axis=0),
                jnp.concatenate([row_grad[slots], rt_ref[...]], axis=0),
            )
        ).astype(low)
        out_ref[index] = (
            shared_out[span] + left_contraction(selector, shared_rows[slots])
        ).astype(low)
    dcat_ref[:PAIR] += left_contraction(shared_grad, hidden_rows)
    dcat_ref[PAIR:] += matmul(jnp.concatenate(logits_grads, axis=1), hidden_rows)

    begin(stores, turn, slot)

    @pl.when(turn == turns - 1)
    def drain():
        for place in range(2):
            for copy in stores(0, place, True):
                copy.wait()


def feed_call(expert, order, x_near, x_far, c_all, route_rows, cat, sd, rt, gate, up, down):
    half, tokens, width = x_near.shape
    units = gate.shape[2]
    turns = half // GROUP
    whole = pl.BlockSpec(memory_space=pl.ANY)
    fixed = lambda shape: pl.BlockSpec(
        shape, lambda i, *rest: (0,) * len(shape), pipeline_mode=pl.Buffered(1)
    )
    parts = jax.ShapeDtypeStruct((half, tokens, width), low)
    shapes = ((width, units), (width, units), (units, width), (PAIR + 2 * EXPERTS, width), (PAIR, width))
    return pl.pallas_call(
        feed_body,
        out_shape=(parts,) * 4 + tuple(jax.ShapeDtypeStruct(shape, wide) for shape in shapes),
        grid_spec=pltpu.PrefetchScalarGridSpec(
            num_scalar_prefetch=2,
            grid=(2 * turns,),
            in_specs=[
                whole,
                whole,
                whole,
                pl.BlockSpec((GROUP, 2, tokens), lambda i, *rest: (i, 0, 0)),
                fixed(cat.shape),
                fixed(sd.shape),
                fixed(rt.shape),
                fixed(gate.shape),
                fixed(up.shape),
                fixed(down.shape),
            ],
            out_specs=(whole,) * 4 + tuple(fixed(shape) for shape in shapes),
            scratch_shapes=[pltpu.VMEM((2, GROUP, tokens, width), low)] * 4
            + [pltpu.SemaphoreType.DMA((2, 2))] * 2,
        ),
        compiler_params=pltpu.CompilerParams(
            dimension_semantics=("arbitrary",), vmem_limit_bytes=62 << 20
        ),
        cost_estimate=pl.CostEstimate(
            flops=4 * half * (CAP * width * units * 18 + tokens * width * PAIR * 12),
            bytes_accessed=half * tokens * width * 16 + width * units * 18,
            transcendentals=2 * half * CAP * units,
        ),
        name="feed",
    )(expert, order, x_near, x_far, c_all, route_rows, cat, sd, rt, gate, up, down)


def shards(
    inputs,
    blocks,
    routes,
    attn_gain,
    w_query,
    w_key,
    w_value,
    w_out,
    ffn_gain,
    w_router,
    shared_gate,
    shared_up,
    shared_down,
    expert_gate,
    expert_up,
    expert_down,
    cotangent,
):
    heads, line = lax.axis_size("head"), lax.axis_size("blk")
    count = heads * line
    head, spot = lax.axis_index("head"), lax.axis_index("blk")
    device = head * line + spot
    tokens, width = inputs.shape
    total = count * tokens
    group = width // heads
    pairs = group // PAIR
    rows = w_query.shape[0]
    steps, short_steps = whole_steps(count), line_steps(line)
    sources = slot_sources(count, steps)
    places = jnp.asarray(np.argsort(sources, axis=1).astype(np.int32))[device]
    slot_sources_own = jnp.asarray(sources)[device]
    short_sources = slot_sources(line, short_steps)
    short_order = jnp.asarray(short_sources)[spot]
    short_places = jnp.asarray(np.argsort(short_sources, axis=1).astype(np.int32))[spot]

    def pad_rows(flat):
        extra = -flat.shape[0] % width
        return jnp.pad(flat, (0, extra)).reshape(-1, width)

    def pad_tall(values):
        return jnp.pad(values, ((0, -values.shape[0] % 16), (0, 0)))

    hop = lambda values, step: permute(values, BOTH, count, step)
    far_steps, cross, chip = steps[:-3], steps[-3:-1], steps[-1]

    halves = lambda matrix: matrix.reshape(rows, heads, group).transpose(1, 0, 2)
    extras = jnp.concatenate(
        [attn_gain, ffn_gain, w_router.reshape(-1), routes.T.reshape(-1).astype(low)]
    )
    extras = jnp.pad(extras, (0, -extras.shape[0] % group)).reshape(-1, group)
    extras = jnp.concatenate([halves(w_out).reshape(heads * rows, group), extras], axis=0)
    split = [halves(matrix) for matrix in (w_query, w_key, w_value)]
    split = jnp.concatenate(split + [jnp.broadcast_to(extras, (heads,) + extras.shape)], axis=1)
    split = jnp.pad(split, ((0, 0), (0, -split.shape[1] % 16), (0, 0)))
    kept = lax.dynamic_index_in_dim(split, head, 0, False)
    sent = lax.dynamic_index_in_dim(split, 1 - head, 0, False)
    weights = [head_order(head, kept, swap_heads(sent))[None]]
    for step in short_steps[:-1]:
        weights.append(grow(weights[-1], permute(weights[-1], "blk", line, step)))
    weights_far = permute(weights[-1], "blk", line, short_steps[-1])
    held = [inputs[None]]
    for place, step in enumerate(steps[:-1]):
        start = held[-1] if place == 0 else after(held[-1], weights[place - 1])
        held.append(grow(start, hop(start, step)))
    inputs_near = held[-1]
    inputs_far = hop(inputs_near, chip)

    shared_slice = shared_gate.shape[1] // count
    shared_pack = jnp.stack(
        [
            shared_gate.reshape(rows, count, shared_slice),
            shared_up.reshape(rows, count, shared_slice),
        ],
        axis=2,
    ).reshape(rows, count * 2 * shared_slice)
    cot_all = lax.all_gather(after(cotangent, inputs_near), BOTH, axis=0, tiled=False)

    qkv_weight, full_out = unpack_call(short_places, weights[-1], weights_far, width)
    first_row = (3 + heads) * rows
    flat = grow(weights[-1][:, :, first_row:], weights_far[:, :, first_row:])
    flat = flat.reshape(line, heads, -1)
    flat = jnp.take(flat, short_places, axis=0, mode="clip").transpose(1, 0, 2)
    flat = flat.reshape(count, -1)
    gain_first = flat[:, :rows].reshape(width).astype(wide)
    gain_second = flat[:, rows : 2 * rows].reshape(width).astype(wide)
    router = flat[:, 2 * rows : (2 + EXPERTS) * rows].reshape(width, EXPERTS)
    route_rows = flat[:, (2 + EXPERTS) * rows : (2 + EXPERTS) * rows + 2 * tokens]
    route_rows = jnp.take(route_rows, slot_sources_own, axis=0, mode="clip")
    route_rows = route_rows.reshape(count, 2, tokens).astype(jnp.int32)

    column_scale = jnp.where(jnp.arange(3 * group) < group, scale_factor, 1.0)[None]
    qkv, token = project_call(inputs_near, gain_first[None], qkv_weight, column_scale, count, None)
    qkv, token = project_call(inputs_far, gain_first[None], qkv_weight, column_scale, count, qkv)
    own_blocks = jnp.arange(heads, dtype=jnp.int32) * line + spot
    own_slots = places[own_blocks]
    neighbour = lax.dynamic_index_in_dim(
        inputs_near, places[(1 - head) * line + spot], 0, False
    )
    pair_inputs = head_order(head, inputs, neighbour).reshape(heads * tokens, width)
    expert = (device % EXPERTS).astype(jnp.int32).reshape(1)

    tile = TILE_BLOCKS * tokens
    own_ids = jnp.take(blocks.reshape(count, tokens), own_blocks, axis=0, mode="clip")
    low_id, high_id = own_ids[:, :1], own_ids[:, -1:]

    def counted(test):
        return jnp.sum(test, axis=1, dtype=jnp.int32)

    query_bounds = jnp.stack(
        [
            counted(blocks[None] <= low_id) // tile,
            (counted(blocks[None] <= high_id) + tile - 1) // tile,
        ]
    )
    key_bounds = jnp.stack(
        [
            counted(blocks[None] < low_id) // tile,
            (counted(blocks[None] < high_id) + tile - 1) // tile,
            jnp.full((heads,), total // tile, jnp.int32),
        ]
    )
    id_columns = jnp.tile(own_ids, (1, 2))[:, :, None]
    id_rows = blocks.reshape(count, 1, tokens)

    own_spec = lambda column: pl.BlockSpec(
        (1, tokens, PAIR), lambda p, j, own, *rest: (own[j], 0, column + p)
    )
    all_spec = lambda column: pl.BlockSpec(
        (count, tokens, PAIR), lambda p, j, *rest: (0, 0, column + p)
    )
    part_spec = pl.BlockSpec((1, tokens, PAIR), lambda p, j, *rest: (j, 0, p))
    stat_spec = pl.BlockSpec((1, 1, 1, 2 * tokens), lambda p, j, *rest: (p, j, 0, 0))
    column_spec = pl.BlockSpec((1, 2 * tokens, 1), lambda p, j, *rest: (j, 0, 0))
    ids_spec = pl.BlockSpec((count, 1, tokens), lambda p, j, *rest: (0, 0, 0))
    part_shape = jax.ShapeDtypeStruct((heads, tokens, group), low)
    stat_shape = jax.ShapeDtypeStruct((pairs, heads, 1, 2 * tokens), wide)
    grid = (pairs, heads)
    unit = 2 * heads * tokens * total * group

    attended_own, lse = attention_call(
        attend_body,
        "attend",
        (
            after(own_slots, route_rows),
            places,
            query_bounds,
        ),
        (qkv, qkv, qkv, id_columns, id_rows),
        [own_spec(0), all_spec(pairs), all_spec(2 * pairs), column_spec, ids_spec],
        (part_shape, stat_shape),
        (part_spec, stat_spec),
        grid,
        2 * unit,
        count,
    )
    attended_back = swap_heads(lax.dynamic_index_in_dim(attended_own, 1 - head, 0, False))
    attended_kept = lax.dynamic_index_in_dim(attended_own, head, 0, False)
    attended = jnp.where(
        head == 0,
        jnp.concatenate([attended_kept, attended_back], axis=1),
        jnp.concatenate([attended_back, attended_kept], axis=1),
    )
    inputs_wide = inputs.astype(wide)
    mixed_rows = inputs_wide + matmul(attended, full_out)
    normed_ffn = rms_scale(mixed_rows, gain_second).astype(low)

    near = normed_ffn[None]
    for step in steps[:-1]:
        if step is steps[-2]:
            shared_pack = after(shared_pack, near)
        near = grow(near, hop(near, step))
    arrived = hop(near, chip)
    shared_in = lax.all_to_all(shared_pack, BOTH, split_axis=1, concat_axis=0, tiled=True)
    half_pad = HEAD_DIM - shared_slice
    shared_pair = jnp.pad(
        shared_in.reshape(width, 2, shared_slice), ((0, 0), (0, 0), (0, half_pad))
    ).reshape(width, PAIR)
    feed_weight = jnp.concatenate(
        [shared_pair, router, jnp.zeros((width, PAIR - EXPERTS), low)], axis=1
    )
    down_pad = jnp.pad(shared_down, ((0, PAIR - shared_slice), (0, 0)))
    router_rows = jnp.transpose(jnp.concatenate([router, router], axis=1))

    (
        row_near, row_far, out_near, out_far,
        grad_egate, grad_eup, grad_edown, grad_feed, grad_sdown,
    ) = feed_call(
        expert, slot_sources_own, near, arrived, cot_all, route_rows, feed_weight, down_pad, router_rows,
        expert_gate, expert_up, expert_down,
    )
    terms = [row_near, hop(row_far, chip)]
    out_terms = [out_near, hop(after(out_far, terms[1]), chip)]
    terms = scatter_step(terms, BOTH, count, cross[1])
    grad_sdown = grad_sdown[:shared_slice]
    terms = scatter_step(terms, BOTH, count, cross[0])
    grad_shared = after(grad_feed[:PAIR], terms[-1]).reshape(2, HEAD_DIM, width)
    grad_shared = jnp.transpose(grad_shared[:, :shared_slice].reshape(-1, width)).astype(low)
    grad_shared_back = lax.all_to_all(grad_shared, BOTH, split_axis=0, concat_axis=1, tiled=True)
    for step in reversed(far_steps):
        if step is far_steps[0]:
            terms[-1] = after(terms[-1], grad_shared_back)
        terms = scatter_step(terms, BOTH, count, step)
    out_sum = sum(term.astype(wide) for term in out_terms).astype(low)
    out_sum = out_sum.reshape((2, 2, -1) + out_sum.shape[1:])
    out_sum = jnp.where(spot % 2 == 0, out_sum, out_sum.swapaxes(0, 1))
    out_terms = [out_sum.reshape((-1,) + out_sum.shape[3:])]
    normed_ffn_grad = finish(terms)
    grad_router = jnp.transpose(
        grad_feed[PAIR : PAIR + EXPERTS] + grad_feed[PAIR + EXPERTS : PAIR + 2 * EXPERTS]
    )

    unused_second, second_pull = jax.vjp(rms_scale, mixed_rows, gain_second)
    mixed_part, grad_gain_ffn = second_pull(normed_ffn_grad)
    mixed_grad = cotangent.astype(wide) + mixed_part
    mixed_low = mixed_grad.astype(low)
    mixed_pair = head_order(head, mixed_low, swap_heads(mixed_low)).reshape(heads * tokens, width)
    own_out = lax.dynamic_slice_in_dim(full_out, head * group, group, 0)
    attended_grad = right_contract(mixed_pair, own_out).astype(low)
    attended_flat = attended_own.reshape(heads * tokens, group)
    grad_wout = left_contraction(attended_flat, after(mixed_pair, attended_grad)).astype(low)
    grad_wout_own = lax.psum_scatter(grad_wout, "blk", scatter_dimension=0, tiled=True)
    head_marks = (
        jnp.arange(group)[None] // HEAD_DIM == jnp.arange(2 * pairs)[:, None]
    ).astype(wide)
    delta = lax.dot_general(
        head_marks,
        attended_grad.astype(wide) * attended_flat.astype(wide),
        (((1,), (1,)), ((), ())),
        precision=lax.Precision.HIGHEST,
    )
    delta = (
        delta.reshape(pairs, 2, heads, tokens)
        .transpose(0, 2, 1, 3)
        .reshape(pairs, heads, 1, 2 * tokens)
    )
    stats = jnp.stack([lse, delta]).transpose(2, 0, 1, 3, 4).reshape(heads, -1)
    stats_rows = jnp.concatenate(two_parts(stats), axis=1).reshape(heads, -1, group)
    grad_parts = attended_grad.reshape(heads, tokens, group)
    grads = [jnp.concatenate([grad_parts, stats_rows], axis=1)[None]]

    out_arrived = swap_heads(after(upper(out_terms), grads[0]))
    out_terms = lower(out_terms)
    for step in short_steps[:-1]:
        grads.append(grow(grads[-1], permute(grads[-1], "blk", line, step)))
    query_q = after(own_slots, grads[-2])
    query_grad = attention_call(
        query_body,
        "query_gradient",
        (query_q, places, query_bounds),
        (qkv, qkv, qkv, grad_parts, lse, delta, id_columns, id_rows),
        [
            own_spec(0),
            all_spec(pairs),
            all_spec(2 * pairs),
            part_spec,
            stat_spec,
            stat_spec,
            column_spec,
            ids_spec,
        ],
        part_shape,
        part_spec,
        grid,
        3 * unit,
        count,
    )
    start = after(grads[-1], query_grad, out_arrived)
    out_terms.append(out_arrived)
    grads.append(grow(start, permute(start, "blk", line, short_steps[-1])))
    grads_all = grads[-1].reshape(count, -1, group)
    stats_all = grads_all[:, tokens:].reshape(line, heads, 2, -1).astype(wide)
    stats_all = (stats_all[:, :, 0] + stats_all[:, :, 1]).reshape(-1, 1, 2 * tokens)
    block_ids = jnp.arange(count, dtype=jnp.int32)
    grad_slots = short_places[block_ids % line] * heads + block_ids // line

    key_grad, value_grad = attention_call(
        key_body,
        "key_gradient",
        (own_slots, places, grad_slots, key_bounds),
        (qkv, qkv, qkv, grads_all, stats_all, id_columns, id_rows),
        [
            own_spec(pairs),
            own_spec(2 * pairs),
            all_spec(0),
            all_spec(0),
            pl.BlockSpec(stats_all.shape, lambda p, j, *rest: (0, 0, 0)),
            column_spec,
            ids_spec,
        ],
        (part_shape, part_shape),
        (part_spec, part_spec),
        grid,
        4 * unit,
        count,
    )

    qkv_grad = jnp.concatenate([query_grad, key_grad, value_grad], axis=2).reshape(
        heads * tokens, 3 * group
    )
    pair_unit = rms_scale(pair_inputs.astype(wide), 1.0)
    normed_own = (pair_unit * gain_first).astype(low)
    normed_part = right_contract(qkv_grad, qkv_weight)
    grad_gain_attn = jnp.sum(normed_part * pair_unit, axis=0)
    columns = [grad_gain_attn[:, None], grad_gain_ffn[:, None], grad_router]
    columns = jnp.concatenate(two_parts(jnp.concatenate(columns, axis=1)), axis=1)
    extra = columns.shape[1]
    columns = jnp.pad(columns, ((0, 0), (0, PAIR - extra)))
    grad_qkv = left_contraction(normed_own, qkv_grad)
    pieces = jnp.concatenate([grad_qkv.astype(low), columns], axis=1)
    pieces = pieces.reshape(heads, line, rows, 3 * group + PAIR).transpose(1, 0, 2, 3)
    pieces = jnp.take(pieces, short_order, axis=0, mode="clip")
    sums = [[pieces]]
    for step in reversed(short_steps):
        sums.append(scatter_step(sums[-1], "blk", line, step))
    summed = finish(sums[-1])
    summed_back = swap_heads(
        lax.dynamic_index_in_dim(summed, 1 - head, 0, False).astype(low)
    ).astype(wide)
    summed_kept = lax.dynamic_index_in_dim(summed, head, 0, False)
    joined = head_order(head, summed_kept, summed_back)
    small = jnp.sum(joined[:, :, 3 * group :], axis=0)
    small = small[:, : extra // 2] + small[:, extra // 2 : extra]
    joined = joined[:, :, : 3 * group].reshape(heads, rows, 3, group)
    joined = joined.transpose(2, 1, 0, 3).reshape(3, rows, width)

    for place, step in enumerate([short_steps[-2]] + list(reversed(far_steps))):
        sent = after(upper(out_terms), grads[-2]) if place == 0 else upper(out_terms)
        arrived = permute(sent, "blk", line, short_steps[-2]) if place == 0 else hop(sent, step)
        out_terms = lower(out_terms) + [after(arrived, key_grad, *sums[min(place, 3)][1:])]
    output = (mixed_rows + finish(out_terms)).astype(low)

    normed_parts = normed_part.reshape(heads, tokens, width)
    arrived = swap_heads(lax.dynamic_index_in_dim(normed_parts, 1 - head, 0, False).astype(low))
    normed_grad = lax.dynamic_index_in_dim(normed_parts, head, 0, False) + arrived.astype(wide)
    unused_first, first_pull = jax.vjp(lambda rows_in: rms_scale(rows_in, gain_first), inputs_wide)
    grad_inputs = mixed_grad + first_pull(after(normed_grad, sums[1][-1]))[0]
    grad_shared_back = after(grad_shared_back, sums[1][-1]).reshape(rows, count, 2, shared_slice)
    grad_sgate = grad_shared_back[:, :, 0].reshape(rows, -1).astype(wide)
    grad_sup = grad_shared_back[:, :, 1].reshape(rows, -1).astype(wide)

    return (
        output,
        grad_inputs,
        small[:, 0],
        joined[0].astype(wide),
        joined[1].astype(wide),
        joined[2].astype(wide),
        grad_wout_own.astype(wide),
        small[:, 1],
        small[:, 2:],
        grad_sgate,
        grad_sup,
        grad_sdown,
        grad_egate[None],
        grad_eup[None],
        grad_edown[None],
    )


def solution(mesh):
    both = P(BOTH)
    rows = P(BOTH, None)
    slabs = P(BOTH, None, None)
    return jax.shard_map(
        shards,
        mesh=mesh,
        in_specs=(
            rows, P(), rows, both, rows, rows, rows, rows, both, rows, rows, rows, rows,
            slabs, slabs, slabs, rows,
        ),
        out_specs=(
            rows, rows, both, rows, rows, rows, rows, both, rows, rows, rows, rows,
            slabs, slabs, slabs,
        ),
        check_vma=False,
    )
```

```python
import functools

import jax
import jax.numpy as jnp
import numpy as np
from jax import lax
from jax.experimental import pallas as pl
from jax.experimental.pallas import tpu as pltpu
from jax.sharding import PartitionSpec as P

HEAD_DIM = 64
EXPERTS = 16
CAP = 32
PAIR = 2 * HEAD_DIM
TILE_BLOCKS = 8
BOTH = ("head", "blk")

epsilon = 1e-05
scale_factor = 0.125
masked_value = -1e30
low = jnp.bfloat16
wide = jnp.float32


def matmul(left_side, right_side):
    return jnp.dot(left_side, right_side, preferred_element_type=wide)


def left_contraction(left_side, right_side):
    return lax.dot_general(
        left_side, right_side, (((0,), (0,)), ((), ())), preferred_element_type=wide
    )


def right_contract(left_side, right_side):
    return lax.dot_general(
        left_side, right_side, (((1,), (1,)), ((), ())), preferred_element_type=wide
    )


def rms_scale(values, gain_row):
    return (
        values * lax.rsqrt(jnp.mean(values * values, axis=-1, keepdims=True) + epsilon) * gain_row
    )


def silu_parts(gate_pre, up_pre):
    gate = jax.nn.sigmoid(gate_pre)
    swish = gate_pre * gate
    return swish * up_pre, gate * (1.0 + gate_pre * (1.0 - gate)) * up_pre, swish


def whole_steps(count):
    bits = count.bit_length() - 1
    steps = [functools.partial(flip, bit, bit) for bit in range(bits - 2, 1, -1)]
    return steps + [
        functools.partial(flip, 1, bits - 1),
        functools.partial(flip, bits - 1, 1),
        functools.partial(flip, 0, 0),
    ]


def flip(even_bit, odd_bit, index):
    return index ^ (1 << (odd_bit if index & 1 else even_bit))


def line_steps(count):
    bits = count.bit_length() - 1
    return [functools.partial(flip, bit, bit) for bit in range(bits - 1, -1, -1)]


def weight_steps(count):
    steps = line_steps(count)
    return [steps[-2]] + steps[:-2] + [steps[-1]]


def slot_sources(count, steps):
    order = [[i] for i in range(count)]
    for step in steps:
        order = [order[i] + order[step(i)] for i in range(count)]
    return np.array(order, np.int32)


def permute(values, axis, count, step):
    return lax.ppermute(values, axis, [(i, step(i)) for i in range(count)])


def after(value, *needed):
    return lax.optimization_barrier((value,) + needed)[0]


def two_parts(values):
    high = lax.reduce_precision(values, 8, 7)
    return [high.astype(low), (values - high).astype(low)]


def grow(held, arrived):
    return jnp.concatenate([held, arrived], axis=0)


def gather(values, axis, count, steps):
    held = values[None]
    for step in steps:
        held = grow(held, permute(held, axis, count, step))
    return held


def upper(terms):
    half = terms[0].shape[0] // 2
    return sum(term[half:].astype(wide) for term in terms).astype(low)


def lower(terms):
    half = terms[0].shape[0] // 2
    return [term[:half] for term in terms]


def scatter_step(terms, axis, count, step):
    return lower(terms) + [permute(upper(terms), axis, count, step)]


def finish(terms):
    return sum(term[0].astype(wide) for term in terms)


def scatter_sum(slots, axis, count, steps):
    terms = [slots]
    for step in reversed(steps):
        terms = scatter_step(terms, axis, count, step)
    return finish(terms)


def swap_heads(values):
    return lax.ppermute(values, "head", [(0, 1), (1, 0)])


def head_order(head, own, other):
    return jnp.where(head == 0, jnp.stack([own, other]), jnp.stack([other, own]))


def stack_heads(rows):
    first = lax.broadcasted_iota(jnp.int32, rows.shape, 1) < HEAD_DIM
    zero = jnp.zeros_like(rows)
    return jnp.concatenate([jnp.where(first, rows, zero), jnp.where(first, zero, rows)], axis=0)


def join_heads(stacked):
    half = stacked.shape[0] // 2
    top = stacked[:half]
    first = lax.broadcasted_iota(jnp.int32, top.shape, 1) < HEAD_DIM
    return jnp.where(first, top, stacked[half:])


def load_tile(ref, slots, index):
    return jnp.concatenate(
        [ref[slots[index * TILE_BLOCKS + part]] for part in range(TILE_BLOCKS)], axis=0
    )


def load_ids(ref, index):
    return jnp.concatenate(
        [ref[index * TILE_BLOCKS + part] for part in range(TILE_BLOCKS)], axis=1
    )


def as_column(row):
    return jnp.transpose(jnp.broadcast_to(row, (PAIR, row.shape[1])))[:, :1]


def attend_body(own, slots, bounds, q_ref, k_ref, v_ref, qid_ref, kid_ref, out_ref, lse_ref):
    part = pl.program_id(1)
    stacked = stack_heads(q_ref[0])
    rows = stacked.shape[0]

    def step(masked, index, state):
        top, total, weighted = state
        scores = right_contract(stacked, load_tile(k_ref, slots, index))
        if masked:
            scores = jnp.where(load_ids(kid_ref, index) <= qid_ref[0], scores, masked_value)
        new_top = jnp.maximum(top, jnp.max(scores, axis=-1, keepdims=True))
        weights = jnp.exp(scores - new_top)
        rescale = jnp.exp(top - new_top)
        total = total * rescale + jnp.sum(weights, axis=-1, keepdims=True)
        weighted = weighted * rescale + matmul(weights.astype(low), load_tile(v_ref, slots, index))
        return new_top, total, weighted

    state = (
        jnp.full((rows, 1), masked_value, wide),
        jnp.zeros((rows, 1), wide),
        jnp.zeros((rows, PAIR), wide),
    )
    state = lax.fori_loop(0, bounds[0, part], functools.partial(step, False), state)
    top, total, weighted = lax.fori_loop(
        bounds[0, part], bounds[1, part], functools.partial(step, True), state
    )
    out_ref[0] = join_heads(weighted / total).astype(low)
    lse = jnp.broadcast_to(top + jnp.log(total), (rows, PAIR))
    lse_ref[0, 0] = jnp.transpose(lse)[:1]


def query_body(
    own, slots, bounds, q_ref, k_ref, v_ref, g_ref, lse_ref, delta_ref, qid_ref, kid_ref, dq_ref
):
    part = pl.program_id(1)
    stacked = stack_heads(q_ref[0])
    grads = stack_heads(g_ref[0])
    lse = as_column(lse_ref[0, 0])
    delta = as_column(delta_ref[0, 0])

    def step(masked, index, total):
        keys = load_tile(k_ref, slots, index)
        probs = jnp.exp(right_contract(stacked, keys) - lse)
        if masked:
            probs = jnp.where(load_ids(kid_ref, index) <= qid_ref[0], probs, 0.0)
        moved = right_contract(grads, load_tile(v_ref, slots, index)) - delta
        return total + matmul((probs * moved).astype(low), keys)

    total = jnp.zeros((stacked.shape[0], PAIR), wide)
    total = lax.fori_loop(0, bounds[0, part], functools.partial(step, False), total)
    total = lax.fori_loop(
        bounds[0, part], bounds[1, part], functools.partial(step, True), total
    )
    dq_ref[0] = (join_heads(total) * scale_factor).astype(low)


def key_body(
    own, slots, gslots, bounds, k_ref, v_ref, q_ref, g_ref, stat_ref, kid_ref, qid_ref,
    dk_ref, dv_ref,
):
    pair = pl.program_id(0)
    part = pl.program_id(1)
    pairs = pl.num_programs(0)
    keys = stack_heads(k_ref[0])
    values = stack_heads(v_ref[0])
    rows = keys.shape[0]

    def stat_rows(index, which):
        tops, bottoms = [], []
        for piece in range(TILE_BLOCKS):
            slot = gslots[index * TILE_BLOCKS + piece]
            place = slot * (2 * pairs) + which * pairs + pair
            row = stat_ref[place]
            tops.append(row[:, :PAIR])
            bottoms.append(row[:, PAIR:])
        shape = (rows // 2, TILE_BLOCKS * PAIR)
        return jnp.concatenate(
            [
                jnp.broadcast_to(jnp.concatenate(tops, axis=1), shape),
                jnp.broadcast_to(jnp.concatenate(bottoms, axis=1), shape),
            ],
            axis=0,
        )

    def step(masked, index, state):
        dk_total, dv_total = state
        queries = load_tile(q_ref, slots, index)
        grads = load_tile(g_ref, gslots, index)
        probs = jnp.exp(right_contract(keys, queries) - stat_rows(index, 0))
        if masked:
            probs = jnp.where(kid_ref[0] <= load_ids(qid_ref, index), probs, 0.0)
        moved = right_contract(values, grads) - stat_rows(index, 1)
        dk_total = dk_total + matmul((probs * moved).astype(low), queries)
        dv_total = dv_total + matmul(probs.astype(low), grads)
        return dk_total, dv_total

    state = (jnp.zeros((rows, PAIR), wide), jnp.zeros((rows, PAIR), wide))
    state = lax.fori_loop(
        bounds[0, part], bounds[1, part], functools.partial(step, True), state
    )
    dk_total, dv_total = lax.fori_loop(
        bounds[1, part], bounds[2, part], functools.partial(step, False), state
    )
    dk_ref[0] = join_heads(dk_total).astype(low)
    dv_ref[0] = join_heads(dv_total).astype(low)


def attention_call(body, name, tables, arrays, specs, outs, out_specs, grid, cost, count):
    return pl.pallas_call(
        body,
        out_shape=outs,
        grid_spec=pltpu.PrefetchScalarGridSpec(
            num_scalar_prefetch=len(tables), grid=grid, in_specs=specs, out_specs=out_specs
        ),
        compiler_params=pltpu.CompilerParams(
            dimension_semantics=("arbitrary", "arbitrary"),
            vmem_limit_bytes=60 << 20,
        ),
        cost_estimate=pl.CostEstimate(
            flops=8 * cost, bytes_accessed=cost // 512, transcendentals=cost // 512
        ),
        name=name,
    )(*tables, *arrays)


def unpack_body(slots, near_ref, far_ref, qkv_ref):
    half, heads, unused, group = near_ref.shape
    line = 2 * half
    rows = qkv_ref.shape[0] // (heads * line)
    for spot in range(line):
        slot = slots[spot]
        is_near = slot < half
        low_slot, high_slot = jnp.minimum(slot, half - 1), jnp.maximum(slot - half, 0)
        for source in range(heads):
            block = jnp.where(is_near, near_ref[low_slot, source], far_ref[high_slot, source])
            first = (source * line + spot) * rows
            for part in range(3):
                qkv_ref[first : first + rows, part * group : (part + 1) * group] = block[
                    part * rows : (part + 1) * rows
                ]


def unpack_call(slots, near, far, width):
    half, heads, unused, group = near.shape
    whole = lambda shape: pl.BlockSpec(shape, lambda i, *rest: (0,) * len(shape))
    shape = (width, 3 * group)
    return pl.pallas_call(
        unpack_body,
        out_shape=jax.ShapeDtypeStruct(shape, low),
        grid_spec=pltpu.PrefetchScalarGridSpec(
            num_scalar_prefetch=1,
            grid=(1,),
            in_specs=[whole(near.shape), whole(far.shape)],
            out_specs=whole(shape),
        ),
        compiler_params=pltpu.CompilerParams(
            dimension_semantics=("arbitrary",), vmem_limit_bytes=32 << 20
        ),
        cost_estimate=pl.CostEstimate(
            flops=0, bytes_accessed=8 * near.size, transcendentals=0
        ),
        name="unpack",
    )(slots, near, far)


PROJECT = 4


def project_body(x_ref, gain_ref, weight_ref, scale_ref, *refs):
    out_ref, token_ref = refs[-2:]
    token_ref[...] = jnp.zeros_like(token_ref)
    blocks, tokens, width = x_ref.shape
    rows = x_ref[...].reshape(blocks * tokens, width).astype(wide)
    normed = rms_scale(rows, gain_ref[...]).astype(low)
    out = matmul(normed, weight_ref[...]) * scale_ref[...]
    out_ref[...] = out.astype(low).reshape(blocks, tokens, -1)


def project_call(rows, gain, weight, scale, count, before):
    blocks, tokens, width = rows.shape
    columns = weight.shape[1]
    skip = 0 if before is None else (count - blocks) // PROJECT
    fixed = lambda array: pl.BlockSpec(array.shape, lambda i: (0, 0))
    more = [] if before is None else [before]
    return pl.pallas_call(
        project_body,
        out_shape=(
            jax.ShapeDtypeStruct((count, tokens, columns), low),
            jax.ShapeDtypeStruct((8, PAIR), wide),
        ),
        grid=(blocks // PROJECT,),
        in_specs=[
            pl.BlockSpec((PROJECT, tokens, width), lambda i: (i, 0, 0)),
            fixed(gain),
            fixed(weight),
            fixed(scale),
        ]
        + [pl.BlockSpec(memory_space=pl.ANY)] * len(more),
        out_specs=(
            pl.BlockSpec((PROJECT, tokens, columns), lambda i: (i + skip, 0, 0)),
            pl.BlockSpec((8, PAIR), lambda i: (0, 0)),
        ),
        input_output_aliases={4: 0} if more else {},
        compiler_params=pltpu.CompilerParams(
            dimension_semantics=("arbitrary",), vmem_limit_bytes=60 << 20
        ),
        cost_estimate=pl.CostEstimate(
            flops=4 * blocks * tokens * width * columns,
            bytes_accessed=2 * blocks * tokens * (width + columns),
            transcendentals=0,
        ),
        name="project",
    )(rows, gain, weight, scale, *more)


def weights_body(
    slots, x_ref, gain_ref, dq_ref, dk_ref, dv_ref, weight_ref, columns_ref, attended_ref, mixed_ref,
    near_ref, far_ref, part_ref,
):
    half, heads, rows, unused = near_ref.shape
    group = dq_ref.shape[1]
    unit = rms_scale(x_ref[...].astype(wide), 1.0)
    normed = (unit * gain_ref[...]).astype(low)
    grads = (dq_ref[...], dk_ref[...], dv_ref[...])
    part = sum(
        right_contract(grad, weight_ref[:, index * group : (index + 1) * group])
        for index, grad in enumerate(grads)
    )
    part_ref[...] = part
    gain = jnp.sum(part * unit, axis=0, keepdims=True)
    gain = jnp.transpose(jnp.broadcast_to(gain, (PAIR, gain.shape[1])))
    gain_high = gain.astype(low)
    gain_low = (gain - gain_high.astype(wide)).astype(low)
    lane = lax.broadcasted_iota(jnp.int32, gain.shape, 1)
    columns = jnp.where(lane == 0, gain_high, columns_ref[...])
    columns = jnp.where(lane == PAIR - 1, gain_low, columns)
    pieces = [left_contraction(normed, grad).astype(low) for grad in grads] + [columns]
    wout = left_contraction(attended_ref[...], mixed_ref[...]).astype(low)
    starts = [0, group, 2 * group, 3 * group]
    for spot in range(2 * half):
        slot = slots[spot]

        def give(ref, at, spot=spot):
            for source in range(heads):
                first = (source * 2 * half + spot) * rows
                for start, piece in zip(starts, pieces):
                    ref[at, source, :, start : start + piece.shape[1]] = piece[first : first + rows]
                ref[at, source, :, 3 * group + PAIR :] = wout[
                    spot * rows : (spot + 1) * rows, source * group : (source + 1) * group
                ]

        @pl.when(slot < half)
        def to_near():
            give(near_ref, slot)

        @pl.when(slot >= half)
        def to_far():
            give(far_ref, slot - half)


def weights_call(slots, inputs, gain, dq, dk, dv, weight, columns, attended, mixed, line):
    heads, tokens, group = dq.shape
    width = inputs.shape[1]
    rows = width // (heads * line)
    flat = lambda array: array.reshape(heads * tokens, group)
    arrays = (inputs, gain, flat(dq), flat(dk), flat(dv), weight, columns, attended, mixed)
    whole = lambda shape: pl.BlockSpec(shape, lambda i, *rest: (0,) * len(shape))
    parts = (line // 2, heads, rows, 4 * group + PAIR)
    return pl.pallas_call(
        weights_body,
        out_shape=(
            jax.ShapeDtypeStruct(parts, low),
            jax.ShapeDtypeStruct(parts, low),
            jax.ShapeDtypeStruct(inputs.shape, wide),
        ),
        grid_spec=pltpu.PrefetchScalarGridSpec(
            num_scalar_prefetch=1,
            grid=(1,),
            in_specs=[whole(array.shape) for array in arrays],
            out_specs=(whole(parts), whole(parts), whole(inputs.shape)),
        ),
        compiler_params=pltpu.CompilerParams(
            dimension_semantics=("arbitrary",), vmem_limit_bytes=60 << 20
        ),
        cost_estimate=pl.CostEstimate(
            flops=20 * heads * tokens * width * group, bytes_accessed=8 << 20, transcendentals=0
        ),
        name="weight_gradients",
    )(slots, *arrays)


GROUP = 8


def feed_body(
    expert, order, x_near, x_far, c_all, route_ref, cat_ref, sd_ref, rt_ref, eg_ref, eu_ref, ed_ref,
    row_near, row_far, out_near, out_far, deg_ref, deu_ref, ded_ref, dcat_ref, dsd_ref,
    x_bufs, c_bufs, row_bufs, out_bufs, in_sems, out_sems,
):
    unused, blocks, tokens, width = x_bufs.shape
    count = blocks * tokens
    turn = pl.program_id(0)
    turns = pl.num_programs(0)
    slot = turn % 2

    def loads(index, place, near):
        first = (index if near else index - turns // 2) * blocks
        source = x_near if near else x_far
        return [
            pltpu.make_async_copy(
                source.at[pl.ds(first, blocks)], x_bufs.at[place], in_sems.at[0, place]
            )
        ] + [
            pltpu.make_async_copy(
                c_all.at[order[index * blocks + part], pl.ds(0, tokens)], c_bufs.at[place, part], in_sems.at[1, place]
            )
            for part in range(blocks)
        ]

    def stores(index, place, near):
        first = (index if near else index - turns // 2) * blocks
        pairs = (
            ((row_near, row_bufs), (out_near, out_bufs))
            if near
            else ((row_far, row_bufs), (out_far, out_bufs))
        )
        return [
            pltpu.make_async_copy(
                source.at[place], target.at[pl.ds(first, blocks)], out_sems.at[number, place]
            )
            for number, (target, source) in enumerate(pairs)
        ]

    def begin(copies, index, place):
        @pl.when(index < turns // 2)
        def from_near():
            for copy in copies(index, place, True):
                copy.start()

        @pl.when(index >= turns // 2)
        def from_far():
            for copy in copies(index, place, False):
                copy.start()

    @pl.when(turn == 0)
    def clear():
        begin(loads, turn, slot)
        for ref in (deg_ref, deu_ref, ded_ref, dcat_ref, dsd_ref):
            ref[...] = jnp.zeros_like(ref)

    @pl.when(turn + 1 < turns)
    def ahead():
        begin(loads, turn + 1, 1 - slot)

    pltpu.make_async_copy(
        x_near.at[pl.ds(0, blocks)], x_bufs.at[slot], in_sems.at[0, slot]
    ).wait()
    pltpu.make_async_copy(
        c_all.at[pl.ds(0, blocks), pl.ds(0, tokens)], c_bufs.at[slot], in_sems.at[1, slot]
    ).wait()

    @pl.when(turn >= 2)
    def free():
        for copy in stores(0, slot, True):
            copy.wait()

    x_ref, c_ref = x_bufs.at[slot], c_bufs.at[slot]
    row_ref, out_ref = row_bufs.at[slot], out_bufs.at[slot]
    hidden_rows = x_ref[...].reshape(count, width)
    grad_rows = c_ref[...].reshape(count, width)
    outcome = matmul(hidden_rows, cat_ref[...])
    pre = outcome[:, :PAIR]
    inside = lax.broadcasted_iota(jnp.int32, pre.shape, 1) < HEAD_DIM
    product, gate_slope, up_slope = silu_parts(pre, pltpu.roll(pre, HEAD_DIM, 1))
    shared_hidden = jnp.where(inside, product, 0.0).astype(low)
    shared_hidden_grad = right_contract(grad_rows, sd_ref[...])
    gate_side = jnp.where(inside, shared_hidden_grad * gate_slope, 0.0)
    up_side = jnp.where(inside, shared_hidden_grad * up_slope, 0.0)
    shared_grad = (gate_side + pltpu.roll(up_side, HEAD_DIM, 1)).astype(low)
    dsd_ref[...] += left_contraction(shared_hidden, grad_rows)

    first = route_ref[:, 0, :]
    second = route_ref[:, 1, :]
    is_first = first == expert[0]
    routed = is_first | (second == expert[0])
    before = (
        lax.broadcasted_iota(jnp.int32, (tokens, tokens), 0)
        < lax.broadcasted_iota(jnp.int32, (tokens, tokens), 1)
    )
    routed_low = jnp.where(routed, 1.0, 0.0).astype(low)
    rank = matmul(routed_low, jnp.where(before, 1.0, 0.0).astype(low))
    rank = jnp.where(routed, rank, -1.0)
    slot_ids = lax.broadcasted_iota(jnp.int32, (CAP, tokens), 0).astype(wide)
    expert_ids = lax.broadcasted_iota(jnp.int32, (EXPERTS, tokens), 0)
    selectors, contrasts, shares, leans, picked, picked_grad = [], [], [], [], [], []
    for index in range(blocks):
        span = slice(index * tokens, (index + 1) * tokens)
        logits = jnp.transpose(outcome[span, PAIR:])[:EXPERTS]
        contrast = jnp.where(expert_ids == first[index : index + 1], 1.0, 0.0) - jnp.where(
            expert_ids == second[index : index + 1], 1.0, 0.0
        )
        gap = jnp.sum(logits * contrast, axis=0, keepdims=True)
        share_first = jax.nn.sigmoid(gap)
        share_second = jax.nn.sigmoid(-gap)
        mark = is_first[index : index + 1]
        share = jnp.where(mark, share_first, share_second)
        lean = jnp.where(mark, 1.0, -1.0) * share_first * share_second
        selector = jnp.where(rank[index : index + 1] == slot_ids, 1.0, 0.0)
        selectors.append(selector)
        contrasts.append(contrast)
        shares.append(jnp.sum(selector * share, axis=1, keepdims=True))
        leans.append(jnp.sum(selector * lean, axis=1, keepdims=True))
        selector = selector.astype(low)
        picked.append(matmul(selector, x_ref[index]).astype(low))
        picked_grad.append(matmul(selector, c_ref[index]).astype(low))
    picked = jnp.concatenate(picked, axis=0)
    picked_grad = jnp.concatenate(picked_grad, axis=0).astype(wide)
    share_rows = jnp.concatenate(shares, axis=0)
    lean_rows = jnp.concatenate(leans, axis=0)

    product, gate_slope, up_slope = silu_parts(
        matmul(picked, eg_ref[0]), matmul(picked, eu_ref[0])
    )
    hidden = product.astype(low)
    partial_rows = matmul(hidden, ed_ref[0]).astype(low).astype(wide)
    dots = lean_rows * jnp.sum(picked_grad * partial_rows, axis=1, keepdims=True)
    partial_grad = (share_rows * picked_grad).astype(low)
    shared_rows = (share_rows * partial_rows).astype(low)
    ded_ref[...] += left_contraction(hidden, partial_grad)
    hidden_grad = right_contract(partial_grad, ed_ref[0])
    gate_grad = (hidden_grad * gate_slope).astype(low)
    up_grad = (hidden_grad * up_slope).astype(low)
    deg_ref[...] += left_contraction(picked, gate_grad)
    deu_ref[...] += left_contraction(picked, up_grad)
    row_grad = (
        right_contract(gate_grad, eg_ref[0]) + right_contract(up_grad, eu_ref[0])
    ).astype(low)

    shared_row = right_contract(shared_grad, cat_ref[:, :PAIR])
    shared_out = matmul(shared_hidden, sd_ref[...])
    logits_grads = []
    for index in range(blocks):
        span = slice(index * tokens, (index + 1) * tokens)
        slots = slice(index * CAP, (index + 1) * CAP)
        selector = selectors[index]
        lean = jnp.sum(selector * dots[slots], axis=0, keepdims=True)
        logits_grad = lean * contrasts[index]
        logits_high = logits_grad.astype(low)
        logits_low = (logits_grad - logits_high.astype(wide)).astype(low)
        logits_grad = jnp.concatenate([logits_high, logits_low], axis=0)
        logits_grads.append(logits_grad)
        selector = selector.astype(low)
        row_ref[index] = (
            shared_row[span]
            + left_contraction(
                jnp.concatenate([selector, logits_grad], axis=0),
                jnp.concatenate([row_grad[slots], rt_ref[...]], axis=0),
            )
        ).astype(low)
        out_ref[index] = (
            shared_out[span] + left_contraction(selector, shared_rows[slots])
        ).astype(low)
    dcat_ref[:PAIR] += left_contraction(shared_grad, hidden_rows)
    dcat_ref[PAIR:] += matmul(jnp.concatenate(logits_grads, axis=1), hidden_rows)

    begin(stores, turn, slot)

    @pl.when(turn == turns - 1)
    def drain():
        for place in range(2):
            for copy in stores(0, place, True):
                copy.wait()


def feed_call(expert, order, x_near, x_far, c_all, route_rows, cat, sd, rt, gate, up, down):
    half, tokens, width = x_near.shape
    units = gate.shape[2]
    turns = half // GROUP
    whole = pl.BlockSpec(memory_space=pl.ANY)
    fixed = lambda shape: pl.BlockSpec(
        shape, lambda i, *rest: (0,) * len(shape), pipeline_mode=pl.Buffered(1)
    )
    parts = jax.ShapeDtypeStruct((half, tokens, width), low)
    shapes = ((width, units), (width, units), (units, width), (PAIR + 2 * EXPERTS, width), (PAIR, width))
    return pl.pallas_call(
        feed_body,
        out_shape=(parts,) * 4 + tuple(jax.ShapeDtypeStruct(shape, wide) for shape in shapes),
        grid_spec=pltpu.PrefetchScalarGridSpec(
            num_scalar_prefetch=2,
            grid=(2 * turns,),
            in_specs=[
                whole,
                whole,
                whole,
                pl.BlockSpec((GROUP, 2, tokens), lambda i, *rest: (i, 0, 0)),
                fixed(cat.shape),
                fixed(sd.shape),
                fixed(rt.shape),
                fixed(gate.shape),
                fixed(up.shape),
                fixed(down.shape),
            ],
            out_specs=(whole,) * 4 + tuple(fixed(shape) for shape in shapes),
            scratch_shapes=[pltpu.VMEM((2, GROUP, tokens, width), low)] * 4
            + [pltpu.SemaphoreType.DMA((2, 2))] * 2,
        ),
        compiler_params=pltpu.CompilerParams(
            dimension_semantics=("arbitrary",), vmem_limit_bytes=62 << 20
        ),
        cost_estimate=pl.CostEstimate(
            flops=4 * half * (CAP * width * units * 18 + tokens * width * PAIR * 12),
            bytes_accessed=half * tokens * width * 16 + width * units * 18,
            transcendentals=2 * half * CAP * units,
        ),
        name="feed",
    )(expert, order, x_near, x_far, c_all, route_rows, cat, sd, rt, gate, up, down)


def shards(
    inputs,
    blocks,
    routes,
    attn_gain,
    w_query,
    w_key,
    w_value,
    w_out,
    ffn_gain,
    w_router,
    shared_gate,
    shared_up,
    shared_down,
    expert_gate,
    expert_up,
    expert_down,
    cotangent,
):
    heads, line = lax.axis_size("head"), lax.axis_size("blk")
    count = heads * line
    head, spot = lax.axis_index("head"), lax.axis_index("blk")
    device = head * line + spot
    tokens, width = inputs.shape
    total = count * tokens
    group = width // heads
    pairs = group // PAIR
    rows = w_query.shape[0]
    steps, short_steps = whole_steps(count), line_steps(line)
    sources = slot_sources(count, steps)
    places = jnp.asarray(np.argsort(sources, axis=1).astype(np.int32))[device]
    slot_sources_own = jnp.asarray(sources)[device]
    short_sources = slot_sources(line, short_steps)
    short_order = jnp.asarray(short_sources)[spot]
    short_places = jnp.asarray(np.argsort(short_sources, axis=1).astype(np.int32))[spot]

    def pad_rows(flat):
        extra = -flat.shape[0] % width
        return jnp.pad(flat, (0, extra)).reshape(-1, width)

    def pad_tall(values):
        return jnp.pad(values, ((0, -values.shape[0] % 16), (0, 0)))

    hop = lambda values, step: permute(values, BOTH, count, step)
    far_steps, cross, chip = steps[:-3], steps[-3:-1], steps[-1]

    own_blocks = jnp.arange(heads, dtype=jnp.int32) * line + spot
    own_slots = places[own_blocks]
    tile = TILE_BLOCKS * tokens
    own_ids = jnp.take(blocks.reshape(count, tokens), own_blocks, axis=0, mode="clip")
    low_id, high_id = own_ids[:, :1], own_ids[:, -1:]

    def counted(test):
        return jnp.sum(test, axis=1, dtype=jnp.int32)

    query_bounds = jnp.stack(
        [
            counted(blocks[None] <= low_id) // tile,
            (counted(blocks[None] <= high_id) + tile - 1) // tile,
        ]
    )
    key_bounds = jnp.stack(
        [
            counted(blocks[None] < low_id) // tile,
            (counted(blocks[None] < high_id) + tile - 1) // tile,
            jnp.full((heads,), total // tile, jnp.int32),
        ]
    )
    id_columns = jnp.tile(own_ids, (1, 2))[:, :, None]
    id_rows = blocks.reshape(count, 1, tokens)

    tables = (own_slots, query_bounds, key_bounds, id_columns)

    halves = lambda matrix: matrix.reshape(rows, heads, group).transpose(1, 0, 2)
    extras = jnp.concatenate(
        [attn_gain, ffn_gain, w_router.reshape(-1), routes.T.reshape(-1).astype(low)]
    )
    extras = jnp.pad(extras, (0, -extras.shape[0] % group)).reshape(-1, group)
    split = [halves(matrix) for matrix in (w_query, w_key, w_value)]
    split = jnp.concatenate(split + [jnp.broadcast_to(extras, (heads,) + extras.shape)], axis=1)
    split = jnp.pad(split, ((0, 0), (0, -split.shape[1] % 16), (0, 0)))
    kept = lax.dynamic_index_in_dim(split, head, 0, False)
    sent = lax.dynamic_index_in_dim(split, 1 - head, 0, False)
    weights = [head_order(head, kept, swap_heads(sent))[None]]
    first_steps = weight_steps(line)
    first_places = jnp.asarray(
        np.argsort(slot_sources(line, first_steps), axis=1).astype(np.int32)
    )[spot]
    for step in first_steps[:-1]:
        weights.append(grow(weights[-1], permute(weights[-1], "blk", line, step)))
    weights_far = permute(weights[-1], "blk", line, first_steps[-1])
    held = [inputs[None]]
    shared_slice = shared_gate.shape[1] // count
    shared_pack = jnp.stack(
        [
            shared_gate.reshape(rows, count, shared_slice),
            shared_up.reshape(rows, count, shared_slice),
        ],
        axis=2,
    ).reshape(rows, count * 2 * shared_slice)
    for place, step in enumerate(steps[:-1]):
        start = after(held[-1], weights[min(place, len(weights)) - 1]) if place else held[-1]
        if step is cross[1]:
            start, shared_pack = lax.optimization_barrier((start, shared_pack))
            start = after(start, *tables)
        held.append(grow(start, hop(start, step)))
    shared_in = lax.all_to_all(shared_pack, BOTH, split_axis=1, concat_axis=0, tiled=True)
    inputs_near = held[-1]
    inputs_far = hop(after(inputs_near, weights[-1], shared_in), chip)

    cot_all = after(jnp.concatenate([cotangent, w_out], axis=0), held[len(far_steps) + 1])
    cot_all = lax.all_gather(cot_all, BOTH, axis=0, tiled=False)
    full_out = cot_all[:, tokens:].reshape(width, width)

    qkv_weight = unpack_call(first_places, weights[-1], weights_far, width)
    first_row = 3 * rows
    flat = grow(weights[-1][:, :, first_row:], weights_far[:, :, first_row:])
    flat = flat.reshape(line, heads, -1)
    flat = jnp.take(flat, first_places, axis=0, mode="clip").transpose(1, 0, 2)
    flat = flat.reshape(count, -1)
    gain_first = flat[:, :rows].reshape(width).astype(wide)
    gain_second = flat[:, rows : 2 * rows].reshape(width).astype(wide)
    router = flat[:, 2 * rows : (2 + EXPERTS) * rows].reshape(width, EXPERTS)
    route_rows = flat[:, (2 + EXPERTS) * rows : (2 + EXPERTS) * rows + 2 * tokens]
    route_rows = jnp.take(route_rows, slot_sources_own, axis=0, mode="clip")
    route_rows = route_rows.reshape(count, 2, tokens).astype(jnp.int32)

    column_scale = jnp.where(jnp.arange(3 * group) < group, scale_factor, 1.0)[None]
    qkv, token = project_call(inputs_near, gain_first[None], qkv_weight, column_scale, count, None)
    qkv, token = project_call(inputs_far, gain_first[None], qkv_weight, column_scale, count, qkv)
    neighbour = lax.dynamic_index_in_dim(
        inputs_near, places[(1 - head) * line + spot], 0, False
    )
    pair_inputs = head_order(head, inputs, neighbour).reshape(heads * tokens, width)
    expert = (device % EXPERTS).astype(jnp.int32).reshape(1)

    own_spec = lambda column: pl.BlockSpec(
        (1, tokens, PAIR), lambda p, j, own, *rest: (own[j], 0, column + p)
    )
    all_spec = lambda column: pl.BlockSpec(
        (count, tokens, PAIR), lambda p, j, *rest: (0, 0, column + p)
    )
    part_spec = pl.BlockSpec((1, tokens, PAIR), lambda p, j, *rest: (j, 0, p))
    stat_spec = pl.BlockSpec((1, 1, 1, 2 * tokens), lambda p, j, *rest: (p, j, 0, 0))
    column_spec = pl.BlockSpec((1, 2 * tokens, 1), lambda p, j, *rest: (j, 0, 0))
    ids_spec = pl.BlockSpec((count, 1, tokens), lambda p, j, *rest: (0, 0, 0))
    part_shape = jax.ShapeDtypeStruct((heads, tokens, group), low)
    stat_shape = jax.ShapeDtypeStruct((pairs, heads, 1, 2 * tokens), wide)
    grid = (pairs, heads)
    unit = 2 * heads * tokens * total * group

    attended_own, lse = attention_call(
        attend_body,
        "attend",
        (
            after(own_slots, route_rows),
            places,
            query_bounds,
        ),
        (qkv, qkv, qkv, id_columns, id_rows),
        [own_spec(0), all_spec(pairs), all_spec(2 * pairs), column_spec, ids_spec],
        (part_shape, stat_shape),
        (part_spec, stat_spec),
        grid,
        2 * unit,
        count,
    )
    attended_back = swap_heads(lax.dynamic_index_in_dim(attended_own, 1 - head, 0, False))
    attended_kept = lax.dynamic_index_in_dim(attended_own, head, 0, False)
    attended = jnp.where(
        head == 0,
        jnp.concatenate([attended_kept, attended_back], axis=1),
        jnp.concatenate([attended_back, attended_kept], axis=1),
    )
    inputs_wide = inputs.astype(wide)
    mixed_rows = inputs_wide + matmul(attended, full_out)
    normed_ffn = rms_scale(mixed_rows, gain_second).astype(low)

    near = normed_ffn[None]
    for step in steps[:-1]:
        near = grow(near, hop(near, step))
    arrived = hop(near, chip)
    half_pad = HEAD_DIM - shared_slice
    shared_pair = jnp.pad(
        shared_in.reshape(width, 2, shared_slice), ((0, 0), (0, 0), (0, half_pad))
    ).reshape(width, PAIR)
    feed_weight = jnp.concatenate(
        [shared_pair, router, jnp.zeros((width, PAIR - EXPERTS), low)], axis=1
    )
    down_pad = jnp.pad(shared_down, ((0, PAIR - shared_slice), (0, 0)))
    router_rows = jnp.transpose(jnp.concatenate([router, router], axis=1))

    (
        row_near, row_far, out_near, out_far,
        grad_egate, grad_eup, grad_edown, grad_feed, grad_sdown,
    ) = feed_call(
        expert, slot_sources_own, near, arrived, cot_all, route_rows, feed_weight, down_pad, router_rows,
        expert_gate, expert_up, expert_down,
    )
    terms = [row_near, hop(row_far, chip)]
    out_terms = [out_near, hop(after(out_far, terms[1]), chip)]
    terms = scatter_step(terms, BOTH, count, cross[1])
    grad_sdown = grad_sdown[:shared_slice]
    out_upper = upper(out_terms)
    grad_shared = after(grad_feed[:PAIR], terms[1]).reshape(2, HEAD_DIM, width)
    grad_shared = jnp.transpose(grad_shared[:, :shared_slice].reshape(-1, width)).astype(low)
    grad_shared_back = lax.all_to_all(grad_shared, BOTH, split_axis=0, concat_axis=1, tiled=True)
    terms[-1] = after(terms[-1], out_upper, grad_shared)
    terms = scatter_step(terms, BOTH, count, cross[0])
    terms[-1], out_upper = lax.optimization_barrier((terms[-1], out_upper))
    out_arrived = hop(out_upper, cross[1])
    terms[-1] = after(terms[-1], grad_shared_back)
    for step in reversed(far_steps):
        terms = scatter_step(terms, BOTH, count, step)
    normed_ffn_grad = finish(terms)
    grad_router = jnp.transpose(
        grad_feed[PAIR : PAIR + EXPERTS] + grad_feed[PAIR + EXPERTS : PAIR + 2 * EXPERTS]
    )

    unused_second, second_pull = jax.vjp(rms_scale, mixed_rows, gain_second)
    mixed_part, grad_gain_ffn = second_pull(normed_ffn_grad)
    mixed_grad = cotangent.astype(wide) + mixed_part
    mixed_low = after(mixed_grad.astype(low), out_arrived)
    mixed_pair = head_order(head, mixed_low, swap_heads(mixed_low)).reshape(heads * tokens, width)
    own_out = lax.dynamic_slice_in_dim(full_out, head * group, group, 0)
    attended_grad = right_contract(mixed_pair, own_out).astype(low)
    attended_flat = attended_own.reshape(heads * tokens, group)
    head_marks = (
        jnp.arange(group)[None] // HEAD_DIM == jnp.arange(2 * pairs)[:, None]
    ).astype(wide)
    delta = lax.dot_general(
        head_marks,
        attended_grad.astype(wide) * attended_flat.astype(wide),
        (((1,), (1,)), ((), ())),
        precision=lax.Precision.HIGHEST,
    )
    delta = (
        delta.reshape(pairs, 2, heads, tokens)
        .transpose(0, 2, 1, 3)
        .reshape(pairs, heads, 1, 2 * tokens)
    )
    stats = jnp.stack([lse, delta]).transpose(2, 0, 1, 3, 4).reshape(heads, -1)
    stats_rows = jnp.concatenate(two_parts(stats), axis=1).reshape(heads, -1, group)
    grad_parts = attended_grad.reshape(heads, tokens, group)
    grads = [jnp.concatenate([grad_parts, stats_rows], axis=1)[None]]
    def next_out(terms, arrived, gate):
        terms = terms + [arrived]
        sent = upper(terms)
        gate, sent = lax.optimization_barrier((gate, sent))
        return lower(terms), sent, gate

    out_terms, sent, grads[0] = next_out(lower(out_terms), out_arrived, grads[0])
    out_arrived = hop(sent, cross[0])
    tail = list(reversed(far_steps))
    for place, step in enumerate(short_steps[:-1]):
        if place == 1:
            grads[-1] = after(grads[-1], out_arrived)
        if place == len(short_steps) - 2:
            out_terms, sent, grads[-1] = next_out(out_terms, out_arrived, grads[-1])
            out_arrived = hop(sent, tail[0])
        grads.append(grow(grads[-1], permute(grads[-1], "blk", line, step)))
    query_q = after(own_slots, grads[-2])
    query_grad = attention_call(
        query_body,
        "query_gradient",
        (query_q, places, query_bounds),
        (qkv, qkv, qkv, grad_parts, lse, delta, id_columns, id_rows),
        [
            own_spec(0),
            all_spec(pairs),
            all_spec(2 * pairs),
            part_spec,
            stat_spec,
            stat_spec,
            column_spec,
            ids_spec,
        ],
        part_shape,
        part_spec,
        grid,
        3 * unit,
        count,
    )
    start = after(grads[-1], query_grad)
    out_terms, sent, start = next_out(out_terms, out_arrived, start)
    for step in tail[1:-1]:
        out_terms, sent, start = next_out(out_terms, hop(sent, step), start)
    out_arrived = hop(sent, tail[-1])
    grads.append(grow(start, permute(start, "blk", line, short_steps[-1])))
    grads_all = grads[-1].reshape(count, -1, group)
    stats_all = grads_all[:, tokens:].reshape(line, heads, 2, -1).astype(wide)
    stats_all = (stats_all[:, :, 0] + stats_all[:, :, 1]).reshape(-1, 1, 2 * tokens)
    block_ids = jnp.arange(count, dtype=jnp.int32)
    grad_slots = short_places[block_ids % line] * heads + block_ids // line

    key_grad, value_grad = attention_call(
        key_body,
        "key_gradient",
        (own_slots, places, grad_slots, key_bounds),
        (qkv, qkv, qkv, grads_all, stats_all, id_columns, id_rows),
        [
            own_spec(pairs),
            own_spec(2 * pairs),
            all_spec(0),
            all_spec(0),
            pl.BlockSpec(stats_all.shape, lambda p, j, *rest: (0, 0, 0)),
            column_spec,
            ids_spec,
        ],
        (part_shape, part_shape),
        (part_spec, part_spec),
        grid,
        4 * unit,
        count,
    )

    columns = two_parts(jnp.concatenate([grad_gain_ffn[:, None], grad_router], axis=1))
    extra = columns[0].shape[1]
    columns = jnp.concatenate(columns, axis=1)
    columns = jnp.pad(columns, ((0, 0), (1, PAIR - 1 - 2 * extra)))
    near, far, normed_part = weights_call(
        short_places, pair_inputs, gain_first[None], query_grad, key_grad, value_grad,
        qkv_weight, columns, attended_flat, mixed_pair, line,
    )
    backward = list(reversed(short_steps))
    sums = [near, permute(far, "blk", line, backward[0])]
    out_terms.append(out_arrived)
    for place, step in enumerate(backward[1:]):
        sums = scatter_step(sums, "blk", line, step)
        if place == 0:
            first_sum = sums[-1]
            sums[-1] = after(sums[-1], out_arrived)
    output = (mixed_rows + finish(out_terms)).astype(low)
    sums = [sums]
    summed = finish(sums[0])
    grad_wout_own = summed[:, :, 3 * group + PAIR :].transpose(1, 0, 2).reshape(rows, width)
    summed = summed[:, :, : 3 * group + PAIR]
    summed_back = swap_heads(
        lax.dynamic_index_in_dim(summed, 1 - head, 0, False).astype(low)
    ).astype(wide)
    summed_kept = lax.dynamic_index_in_dim(summed, head, 0, False)
    joined = head_order(head, summed_kept, summed_back)
    small = jnp.sum(joined[:, :, 3 * group :], axis=0)
    gain_column = small[:, 0] + small[:, PAIR - 1]
    small = small[:, 1 : extra + 1] + small[:, extra + 1 : 2 * extra + 1]
    joined = joined[:, :, : 3 * group].reshape(heads, rows, 3, group)
    joined = joined.transpose(2, 1, 0, 3).reshape(3, rows, width)

    normed_parts = normed_part.reshape(heads, tokens, width)
    arrived = swap_heads(lax.dynamic_index_in_dim(normed_parts, 1 - head, 0, False).astype(low))
    normed_grad = lax.dynamic_index_in_dim(normed_parts, head, 0, False) + arrived.astype(wide)
    unused_first, first_pull = jax.vjp(lambda rows_in: rms_scale(rows_in, gain_first), inputs_wide)
    grad_inputs = mixed_grad + first_pull(after(normed_grad, first_sum))[0]
    grad_shared_back = after(grad_shared_back, first_sum).reshape(rows, count, 2, shared_slice)
    grad_sgate = grad_shared_back[:, :, 0].reshape(rows, -1).astype(wide)
    grad_sup = grad_shared_back[:, :, 1].reshape(rows, -1).astype(wide)

    return (
        output,
        grad_inputs,
        gain_column,
        joined[0].astype(wide),
        joined[1].astype(wide),
        joined[2].astype(wide),
        grad_wout_own,
        small[:, 0],
        small[:, 1:],
        grad_sgate,
        grad_sup,
        grad_sdown,
        grad_egate[None],
        grad_eup[None],
        grad_edown[None],
    )


def solution(mesh):
    both = P(BOTH)
    rows = P(BOTH, None)
    slabs = P(BOTH, None, None)
    return jax.shard_map(
        shards,
        mesh=mesh,
        in_specs=(
            rows, P(), rows, both, rows, rows, rows, rows, both, rows, rows, rows, rows,
            slabs, slabs, slabs, rows,
        ),
        out_specs=(
            rows, rows, both, rows, rows, rows, rows, both, rows, rows, rows, rows,
            slabs, slabs, slabs,
        ),
        check_vma=False,
    )
```

```python
import functools

import jax
import jax.numpy as jnp
import numpy as np
from jax import lax
from jax.experimental import pallas as pl
from jax.experimental.pallas import tpu as pltpu
from jax.sharding import PartitionSpec as P

HEAD_DIM = 64
EXPERTS = 16
CAP = 32
PAIR = 2 * HEAD_DIM
TILE_BLOCKS = 8
BOTH = ("head", "blk")

epsilon = 1e-05
scale_factor = 0.125
masked_value = -1e30
low = jnp.bfloat16
wide = jnp.float32


def matmul(left_side, right_side):
    return jnp.dot(left_side, right_side, preferred_element_type=wide)


def left_contraction(left_side, right_side):
    return lax.dot_general(
        left_side, right_side, (((0,), (0,)), ((), ())), preferred_element_type=wide
    )


def right_contract(left_side, right_side):
    return lax.dot_general(
        left_side, right_side, (((1,), (1,)), ((), ())), preferred_element_type=wide
    )


def rms_scale(values, gain_row):
    return (
        values * lax.rsqrt(jnp.mean(values * values, axis=-1, keepdims=True) + epsilon) * gain_row
    )


def silu_parts(gate_pre, up_pre):
    gate = jax.nn.sigmoid(gate_pre)
    swish = gate_pre * gate
    return swish * up_pre, gate * (1.0 + gate_pre * (1.0 - gate)) * up_pre, swish


def whole_steps(count):
    bits = count.bit_length() - 1
    steps = [functools.partial(flip, bit, bit) for bit in range(bits - 2, 1, -1)]
    return steps + [
        functools.partial(flip, 1, bits - 1),
        functools.partial(flip, bits - 1, 1),
        functools.partial(flip, 0, 0),
    ]


def flip(even_bit, odd_bit, index):
    return index ^ (1 << (odd_bit if index & 1 else even_bit))


def line_steps(count):
    bits = count.bit_length() - 1
    return [functools.partial(flip, bit, bit) for bit in range(bits - 1, -1, -1)]


def weight_steps(count):
    steps = line_steps(count)
    return [steps[-2]] + steps[:-2] + [steps[-1]]


def slot_sources(count, steps):
    order = [[i] for i in range(count)]
    for step in steps:
        order = [order[i] + order[step(i)] for i in range(count)]
    return np.array(order, np.int32)


def permute(values, axis, count, step):
    return lax.ppermute(values, axis, [(i, step(i)) for i in range(count)])


def after(value, *needed):
    return lax.optimization_barrier((value,) + needed)[0]


def two_parts(values):
    high = lax.reduce_precision(values, 8, 7)
    return [high.astype(low), (values - high).astype(low)]


def grow(held, arrived):
    return jnp.concatenate([held, arrived], axis=0)


def gather(values, axis, count, steps):
    held = values[None]
    for step in steps:
        held = grow(held, permute(held, axis, count, step))
    return held


def upper(terms):
    half = terms[0].shape[0] // 2
    return sum(term[half:].astype(wide) for term in terms).astype(low)


def lower(terms):
    half = terms[0].shape[0] // 2
    return [term[:half] for term in terms]


def scatter_step(terms, axis, count, step):
    return lower(terms) + [permute(upper(terms), axis, count, step)]


def finish(terms):
    return sum(term[0].astype(wide) for term in terms)


def scatter_sum(slots, axis, count, steps):
    terms = [slots]
    for step in reversed(steps):
        terms = scatter_step(terms, axis, count, step)
    return finish(terms)


def swap_heads(values):
    return lax.ppermute(values, "head", [(0, 1), (1, 0)])


def head_order(head, own, other):
    return jnp.where(head == 0, jnp.stack([own, other]), jnp.stack([other, own]))


def stack_heads(rows):
    first = lax.broadcasted_iota(jnp.int32, rows.shape, 1) < HEAD_DIM
    zero = jnp.zeros_like(rows)
    return jnp.concatenate([jnp.where(first, rows, zero), jnp.where(first, zero, rows)], axis=0)


def join_heads(stacked):
    half = stacked.shape[0] // 2
    top = stacked[:half]
    first = lax.broadcasted_iota(jnp.int32, top.shape, 1) < HEAD_DIM
    return jnp.where(first, top, stacked[half:])


def load_tile(ref, slots, index):
    return jnp.concatenate(
        [ref[slots[index * TILE_BLOCKS + part]] for part in range(TILE_BLOCKS)], axis=0
    )


def load_ids(ref, index):
    return jnp.concatenate(
        [ref[index * TILE_BLOCKS + part] for part in range(TILE_BLOCKS)], axis=1
    )


def as_column(row):
    return jnp.transpose(jnp.broadcast_to(row, (PAIR, row.shape[1])))[:, :1]


def attend_body(own, slots, bounds, q_ref, k_ref, v_ref, qid_ref, kid_ref, out_ref, lse_ref):
    part = pl.program_id(1)
    stacked = stack_heads(q_ref[0])
    rows = stacked.shape[0]

    def step(masked, index, state):
        top, total, weighted = state
        scores = right_contract(stacked, load_tile(k_ref, slots, index))
        if masked:
            scores = jnp.where(load_ids(kid_ref, index) <= qid_ref[0], scores, masked_value)
        new_top = jnp.maximum(top, jnp.max(scores, axis=-1, keepdims=True))
        weights = jnp.exp(scores - new_top)
        rescale = jnp.exp(top - new_top)
        total = total * rescale + jnp.sum(weights, axis=-1, keepdims=True)
        weighted = weighted * rescale + matmul(weights.astype(low), load_tile(v_ref, slots, index))
        return new_top, total, weighted

    state = (
        jnp.full((rows, 1), masked_value, wide),
        jnp.zeros((rows, 1), wide),
        jnp.zeros((rows, PAIR), wide),
    )
    state = lax.fori_loop(0, bounds[0, part], functools.partial(step, False), state)
    top, total, weighted = lax.fori_loop(
        bounds[0, part], bounds[1, part], functools.partial(step, True), state
    )
    out_ref[0] = join_heads(weighted / total).astype(low)
    lse = jnp.broadcast_to(top + jnp.log(total), (rows, PAIR))
    lse_ref[0, 0] = jnp.transpose(lse)[:1]


def query_body(
    own, slots, bounds, q_ref, k_ref, v_ref, g_ref, lse_ref, delta_ref, qid_ref, kid_ref, dq_ref
):
    part = pl.program_id(1)
    stacked = stack_heads(q_ref[0])
    grads = stack_heads(g_ref[0])
    lse = as_column(lse_ref[0, 0])
    delta = as_column(delta_ref[0, 0])

    def step(masked, index, total):
        keys = load_tile(k_ref, slots, index)
        probs = jnp.exp(right_contract(stacked, keys) - lse)
        if masked:
            probs = jnp.where(load_ids(kid_ref, index) <= qid_ref[0], probs, 0.0)
        moved = right_contract(grads, load_tile(v_ref, slots, index)) - delta
        return total + matmul((probs * moved).astype(low), keys)

    total = jnp.zeros((stacked.shape[0], PAIR), wide)
    total = lax.fori_loop(0, bounds[0, part], functools.partial(step, False), total)
    total = lax.fori_loop(
        bounds[0, part], bounds[1, part], functools.partial(step, True), total
    )
    dq_ref[0] = (join_heads(total) * scale_factor).astype(low)


def key_body(
    own, slots, gslots, bounds, k_ref, v_ref, q_ref, g_ref, stat_ref, kid_ref, qid_ref,
    dk_ref, dv_ref,
):
    pair = pl.program_id(0)
    part = pl.program_id(1)
    pairs = pl.num_programs(0)
    keys = stack_heads(k_ref[0])
    values = stack_heads(v_ref[0])
    rows = keys.shape[0]

    def stat_rows(index, which):
        tops, bottoms = [], []
        for piece in range(TILE_BLOCKS):
            slot = gslots[index * TILE_BLOCKS + piece]
            place = slot * (2 * pairs) + which * pairs + pair
            row = stat_ref[place]
            tops.append(row[:, :PAIR])
            bottoms.append(row[:, PAIR:])
        shape = (rows // 2, TILE_BLOCKS * PAIR)
        return jnp.concatenate(
            [
                jnp.broadcast_to(jnp.concatenate(tops, axis=1), shape),
                jnp.broadcast_to(jnp.concatenate(bottoms, axis=1), shape),
            ],
            axis=0,
        )

    def step(masked, index, state):
        dk_total, dv_total = state
        queries = load_tile(q_ref, slots, index)
        grads = load_tile(g_ref, gslots, index)
        probs = jnp.exp(right_contract(keys, queries) - stat_rows(index, 0))
        if masked:
            probs = jnp.where(kid_ref[0] <= load_ids(qid_ref, index), probs, 0.0)
        moved = right_contract(values, grads) - stat_rows(index, 1)
        dk_total = dk_total + matmul((probs * moved).astype(low), queries)
        dv_total = dv_total + matmul(probs.astype(low), grads)
        return dk_total, dv_total

    state = (jnp.zeros((rows, PAIR), wide), jnp.zeros((rows, PAIR), wide))
    state = lax.fori_loop(
        bounds[0, part], bounds[1, part], functools.partial(step, True), state
    )
    dk_total, dv_total = lax.fori_loop(
        bounds[1, part], bounds[2, part], functools.partial(step, False), state
    )
    dk_ref[0] = join_heads(dk_total).astype(low)
    dv_ref[0] = join_heads(dv_total).astype(low)


def attention_call(body, name, tables, arrays, specs, outs, out_specs, grid, cost, count):
    return pl.pallas_call(
        body,
        out_shape=outs,
        grid_spec=pltpu.PrefetchScalarGridSpec(
            num_scalar_prefetch=len(tables), grid=grid, in_specs=specs, out_specs=out_specs
        ),
        compiler_params=pltpu.CompilerParams(
            dimension_semantics=("arbitrary", "arbitrary"),
            vmem_limit_bytes=60 << 20,
        ),
        cost_estimate=pl.CostEstimate(
            flops=8 * cost, bytes_accessed=cost // 512, transcendentals=cost // 512
        ),
        name=name,
    )(*tables, *arrays)


def unpack_body(slots, near_ref, far_ref, query_ref, key_ref):
    half, heads, unused, group = near_ref.shape
    line = 2 * half
    rows = query_ref.shape[0] // (heads * line)
    for spot in range(line):
        slot = slots[spot]
        is_near = slot < half
        low_slot, high_slot = jnp.minimum(slot, half - 1), jnp.maximum(slot - half, 0)
        for source in range(heads):
            block = jnp.where(is_near, near_ref[low_slot, source], far_ref[high_slot, source])
            first = (source * line + spot) * rows
            query_ref[first : first + rows] = block[:rows]
            for part in range(2):
                key_ref[first : first + rows, part * group : (part + 1) * group] = block[
                    (part + 1) * rows : (part + 2) * rows
                ]


def unpack_call(slots, near, far, width):
    half, heads, unused, group = near.shape
    whole = lambda shape: pl.BlockSpec(shape, lambda i, *rest: (0,) * len(shape))
    shapes = ((width, group), (width, 2 * group))
    return pl.pallas_call(
        unpack_body,
        out_shape=tuple(jax.ShapeDtypeStruct(shape, low) for shape in shapes),
        grid_spec=pltpu.PrefetchScalarGridSpec(
            num_scalar_prefetch=1,
            grid=(1,),
            in_specs=[whole(near.shape), whole(far.shape)],
            out_specs=tuple(whole(shape) for shape in shapes),
        ),
        compiler_params=pltpu.CompilerParams(
            dimension_semantics=("arbitrary",), vmem_limit_bytes=32 << 20
        ),
        cost_estimate=pl.CostEstimate(
            flops=0, bytes_accessed=8 * near.size, transcendentals=0
        ),
        name="unpack",
    )(slots, near, far)


PROJECT = 4


def project_body(scale, x_ref, gain_ref, weight_ref, *refs):
    out_ref, token_ref = refs[-2:]
    token_ref[...] = jnp.zeros_like(token_ref)
    blocks, tokens, width = x_ref.shape
    rows = x_ref[...].reshape(blocks * tokens, width).astype(wide)
    normed = rms_scale(rows, gain_ref[...]).astype(low)
    out = matmul(normed, weight_ref[...]) * scale
    out_ref[...] = out.astype(low).reshape(blocks, tokens, -1)


def project_call(rows, gain, weight, scale, count, before):
    blocks, tokens, width = rows.shape
    columns = weight.shape[1]
    skip = 0 if before is None else (count - blocks) // PROJECT
    flat = lambda array: pl.BlockSpec(array.shape, lambda i: (0, 0))
    more = [] if before is None else [before]
    return pl.pallas_call(
        functools.partial(project_body, scale),
        out_shape=(
            jax.ShapeDtypeStruct((count, tokens, columns), low),
            jax.ShapeDtypeStruct((8, PAIR), wide),
        ),
        grid=(blocks // PROJECT,),
        in_specs=[
            pl.BlockSpec((PROJECT, tokens, width), lambda i: (i, 0, 0)),
            flat(gain),
            flat(weight),
        ]
        + [pl.BlockSpec(memory_space=pl.ANY)] * len(more),
        out_specs=(
            pl.BlockSpec((PROJECT, tokens, columns), lambda i: (i + skip, 0, 0)),
            pl.BlockSpec((8, PAIR), lambda i: (0, 0)),
        ),
        input_output_aliases={3: 0} if more else {},
        compiler_params=pltpu.CompilerParams(
            dimension_semantics=("arbitrary",), vmem_limit_bytes=60 << 20
        ),
        cost_estimate=pl.CostEstimate(
            flops=4 * blocks * tokens * width * columns,
            bytes_accessed=2 * blocks * tokens * (width + columns),
            transcendentals=0,
        ),
        name="project",
    )(rows, gain, weight, *more)


def weights_body(
    slots, x_ref, gain_ref, dq_ref, dk_ref, dv_ref, query_ref, key_ref, columns_ref, attended_ref, mixed_ref,
    near_ref, far_ref, part_ref,
):
    half, heads, rows, unused = near_ref.shape
    group = dq_ref.shape[1]
    unit = rms_scale(x_ref[...].astype(wide), 1.0)
    normed = (unit * gain_ref[...]).astype(low)
    grads = (dq_ref[...], dk_ref[...], dv_ref[...])
    part = (
        right_contract(grads[0], query_ref[...])
        + right_contract(grads[1], key_ref[:, :group])
        + right_contract(grads[2], key_ref[:, group:])
    )
    part_ref[...] = part
    gain = jnp.sum(part * unit, axis=0, keepdims=True)
    gain = jnp.transpose(jnp.broadcast_to(gain, (PAIR, gain.shape[1])))
    gain_high = gain.astype(low)
    gain_low = (gain - gain_high.astype(wide)).astype(low)
    lane = lax.broadcasted_iota(jnp.int32, gain.shape, 1)
    columns = jnp.where(lane == 0, gain_high, columns_ref[...])
    columns = jnp.where(lane == PAIR - 1, gain_low, columns)
    pieces = [left_contraction(normed, grad).astype(low) for grad in grads] + [columns]
    wout = left_contraction(attended_ref[...], mixed_ref[...]).astype(low)
    starts = [0, group, 2 * group, 3 * group]
    for spot in range(2 * half):
        slot = slots[spot]

        def give(ref, at, spot=spot):
            for source in range(heads):
                first = (source * 2 * half + spot) * rows
                for start, piece in zip(starts, pieces):
                    ref[at, source, :, start : start + piece.shape[1]] = piece[first : first + rows]
                ref[at, source, :, 3 * group + PAIR :] = wout[
                    spot * rows : (spot + 1) * rows, source * group : (source + 1) * group
                ]

        @pl.when(slot < half)
        def to_near():
            give(near_ref, slot)

        @pl.when(slot >= half)
        def to_far():
            give(far_ref, slot - half)


def weights_call(slots, inputs, gain, dq, dk, dv, query_weight, key_weight, columns, attended, mixed, line):
    heads, tokens, group = dq.shape
    width = inputs.shape[1]
    rows = width // (heads * line)
    flat = lambda array: array.reshape(heads * tokens, group)
    arrays = (inputs, gain, flat(dq), flat(dk), flat(dv), query_weight, key_weight, columns, attended, mixed)
    whole = lambda shape: pl.BlockSpec(shape, lambda i, *rest: (0,) * len(shape))
    parts = (line // 2, heads, rows, 4 * group + PAIR)
    return pl.pallas_call(
        weights_body,
        out_shape=(
            jax.ShapeDtypeStruct(parts, low),
            jax.ShapeDtypeStruct(parts, low),
            jax.ShapeDtypeStruct(inputs.shape, wide),
        ),
        grid_spec=pltpu.PrefetchScalarGridSpec(
            num_scalar_prefetch=1,
            grid=(1,),
            in_specs=[whole(array.shape) for array in arrays],
            out_specs=(whole(parts), whole(parts), whole(inputs.shape)),
        ),
        compiler_params=pltpu.CompilerParams(
            dimension_semantics=("arbitrary",), vmem_limit_bytes=60 << 20
        ),
        cost_estimate=pl.CostEstimate(
            flops=20 * heads * tokens * width * group, bytes_accessed=8 << 20, transcendentals=0
        ),
        name="weight_gradients",
    )(slots, *arrays)


GROUP = 8


class Stream:
    def __init__(self, near, far, buffers, semaphores, turns):
        self.near, self.far, self.buffers, self.semaphores = near, far, buffers, semaphores
        self.half, self.blocks = turns // 2, buffers.shape[1]

    def part(self, side, index, first):
        return side.at[pl.ds((index - first) * self.blocks, self.blocks)]

    def load(self, index, place):
        self.begin(index, place, lambda part, buffer: (part, buffer))

    def store(self, index, place):
        self.begin(index, place, lambda part, buffer: (buffer, part))

    def begin(self, index, place, ends):
        for side, first, here in (
            (self.near, 0, index < self.half),
            (self.far, self.half, index >= self.half),
        ):

            @pl.when(here)
            def start(side=side, first=first):
                source, target = ends(self.part(side, index, first), self.buffers.at[place])
                pltpu.make_async_copy(source, target, self.semaphores.at[place]).start()

    def loaded(self, place):
        pltpu.make_async_copy(
            self.part(self.near, 0, 0), self.buffers.at[place], self.semaphores.at[place]
        ).wait()

    def stored(self, place):
        pltpu.make_async_copy(
            self.buffers.at[place], self.part(self.near, 0, 0), self.semaphores.at[place]
        ).wait()


class Picked:
    def __init__(self, source, order, buffers, semaphores):
        self.source, self.order, self.buffers, self.semaphores = source, order, buffers, semaphores
        self.blocks, self.rows = buffers.shape[1:3]

    def load(self, index, place):
        for part in range(self.blocks):
            block = self.source.at[self.order[index * self.blocks + part], pl.ds(0, self.rows)]
            pltpu.make_async_copy(
                block, self.buffers.at[place, part], self.semaphores.at[place]
            ).start()

    def loaded(self, place):
        pltpu.make_async_copy(
            self.source.at[pl.ds(0, self.blocks), pl.ds(0, self.rows)],
            self.buffers.at[place],
            self.semaphores.at[place],
        ).wait()


def load_ahead(streams, turn, turns):
    slot = turn % 2

    @pl.when(turn == 0)
    def first():
        for stream in streams:
            stream.load(turn, slot)

    @pl.when(turn + 1 < turns)
    def ahead():
        for stream in streams:
            stream.load(turn + 1, 1 - slot)

    for stream in streams:
        stream.loaded(slot)
    return slot


def free_slot(streams, turn, slot):
    @pl.when(turn >= 2)
    def free():
        for stream in streams:
            stream.stored(slot)


def store_out(streams, turn, turns, slot):
    for stream in streams:
        stream.store(turn, slot)

    @pl.when(turn == turns - 1)
    def drain():
        for place in range(2):
            for stream in streams:
                stream.stored(place)


def choose_body(
    expert, order, c_all, route_ref, sd_ref, pick_ref, hidden_ref, chosen_ref, c_bufs, c_sems
):
    turn, turns = pl.program_id(0), pl.num_programs(0)
    slot = load_ahead([Picked(c_all, order, c_bufs, c_sems)], turn, turns)
    c_ref = c_bufs.at[slot]
    blocks, tokens, width = c_ref.shape
    hidden_ref[...] = right_contract(c_ref[...].reshape(blocks * tokens, width), sd_ref[...])
    routed = (route_ref[:, 0, :] == expert[0]) | (route_ref[:, 1, :] == expert[0])
    before = (
        lax.broadcasted_iota(jnp.int32, (tokens, tokens), 0)
        < lax.broadcasted_iota(jnp.int32, (tokens, tokens), 1)
    )
    rank = matmul(
        jnp.where(routed, 1.0, 0.0).astype(low), jnp.where(before, 1.0, 0.0).astype(low)
    )
    rank = jnp.where(routed, rank, -1.0)
    slot_ids = lax.broadcasted_iota(jnp.int32, (CAP, tokens), 0).astype(wide)
    for index in range(blocks):
        selector = jnp.where(rank[index : index + 1] == slot_ids, 1.0, 0.0).astype(low)
        chosen_ref[index] = selector
        pick_ref[index * CAP : (index + 1) * CAP] = matmul(selector, c_ref[index]).astype(low)


def feed_body(
    expert, x_near, x_far, route_ref, pick_ref, shared_ref, chosen_ref, cat_ref, rt_ref,
    eg_ref, eu_ref, ed_ref,
    row_near, row_far, xs_ref, pg_ref, hid_ref, gg_ref, ug_ref, give_ref, sh_ref, sg_ref, lg_ref,
    x_bufs, row_bufs, x_sems, row_sems,
):
    turn, turns = pl.program_id(0), pl.num_programs(0)
    slot = load_ahead([Stream(x_near, x_far, x_bufs, x_sems, turns)], turn, turns)
    rows_out = [Stream(row_near, row_far, row_bufs, row_sems, turns)]
    free_slot(rows_out, turn, slot)
    x_ref, row_ref = x_bufs.at[slot], row_bufs.at[slot]
    blocks, tokens, width = x_ref.shape
    count = blocks * tokens

    outcome = matmul(x_ref[...].reshape(count, width), cat_ref[...])
    pre = outcome[:, :PAIR]
    inside = lax.broadcasted_iota(jnp.int32, pre.shape, 1) < HEAD_DIM
    product, gate_slope, up_slope = silu_parts(pre, pltpu.roll(pre, HEAD_DIM, 1))
    sh_ref[...] = jnp.where(inside, product, 0.0).astype(low)
    shared_hidden_grad = shared_ref[...]
    gate_side = jnp.where(inside, shared_hidden_grad * gate_slope, 0.0)
    up_side = jnp.where(inside, shared_hidden_grad * up_slope, 0.0)
    shared_grad = (gate_side + pltpu.roll(up_side, HEAD_DIM, 1)).astype(low)
    sg_ref[...] = shared_grad

    first = route_ref[:, 0, :]
    second = route_ref[:, 1, :]
    is_first = first == expert[0]
    expert_ids = lax.broadcasted_iota(jnp.int32, (EXPERTS, tokens), 0)
    contrasts, shares, leans, picked = [], [], [], []
    for index in range(blocks):
        span = slice(index * tokens, (index + 1) * tokens)
        logits = jnp.transpose(outcome[span, PAIR:])[:EXPERTS]
        contrast = jnp.where(expert_ids == first[index : index + 1], 1.0, 0.0) - jnp.where(
            expert_ids == second[index : index + 1], 1.0, 0.0
        )
        gap = jnp.sum(logits * contrast, axis=0, keepdims=True)
        share_first = jax.nn.sigmoid(gap)
        share_second = jax.nn.sigmoid(-gap)
        mark = is_first[index : index + 1]
        share = jnp.where(mark, share_first, share_second)
        lean = jnp.where(mark, 1.0, -1.0) * share_first * share_second
        selector = chosen_ref[index].astype(wide)
        contrasts.append(contrast)
        shares.append(jnp.sum(selector * share, axis=1, keepdims=True))
        leans.append(jnp.sum(selector * lean, axis=1, keepdims=True))
        picked.append(matmul(chosen_ref[index], x_ref[index]).astype(low))
    picked = jnp.concatenate(picked, axis=0)
    picked_grad = pick_ref[...].astype(wide)
    share_rows = jnp.concatenate(shares, axis=0)
    lean_rows = jnp.concatenate(leans, axis=0)
    xs_ref[...] = picked

    product, gate_slope, up_slope = silu_parts(
        matmul(picked, eg_ref[0]), matmul(picked, eu_ref[0])
    )
    hidden = product.astype(low)
    hid_ref[...] = hidden
    partial_rows = matmul(hidden, ed_ref[0]).astype(low).astype(wide)
    dots = lean_rows * jnp.sum(picked_grad * partial_rows, axis=1, keepdims=True)
    partial_grad = (share_rows * picked_grad).astype(low)
    pg_ref[...] = partial_grad
    give_ref[...] = (share_rows * partial_rows).astype(low)
    hidden_grad = right_contract(partial_grad, ed_ref[0])
    gate_grad = (hidden_grad * gate_slope).astype(low)
    up_grad = (hidden_grad * up_slope).astype(low)
    gg_ref[...] = gate_grad
    ug_ref[...] = up_grad
    row_grad = (
        right_contract(gate_grad, eg_ref[0]) + right_contract(up_grad, eu_ref[0])
    ).astype(low)

    shared_row = right_contract(shared_grad, cat_ref[:, :PAIR])
    for index in range(blocks):
        span = slice(index * tokens, (index + 1) * tokens)
        slots = slice(index * CAP, (index + 1) * CAP)
        selector = chosen_ref[index]
        lean = jnp.sum(selector.astype(wide) * dots[slots], axis=0, keepdims=True)
        logits_grad = lean * contrasts[index]
        logits_high = logits_grad.astype(low)
        logits_low = (logits_grad - logits_high.astype(wide)).astype(low)
        logits_grad = jnp.concatenate([logits_high, logits_low], axis=0)
        lg_ref[index] = logits_grad
        row_ref[index] = (
            shared_row[span]
            + left_contraction(
                jnp.concatenate([selector, logits_grad], axis=0),
                jnp.concatenate([row_grad[slots], rt_ref[...]], axis=0),
            )
        ).astype(low)
    store_out(rows_out, turn, turns, slot)


def rest_body(
    gate, order, x_near, x_far, c_all, chosen_ref, xs_ref, pg_ref, hid_ref, gg_ref, ug_ref, give_ref,
    sh_ref, sg_ref, lg_ref, sd_ref,
    out_near, out_far, deg_ref, deu_ref, ded_ref, dcat_ref, dsd_ref,
    x_bufs, c_bufs, out_bufs, x_sems, c_sems, out_sems,
):
    turn, turns = pl.program_id(0), pl.num_programs(0)
    streams = [Stream(x_near, x_far, x_bufs, x_sems, turns), Picked(c_all, order, c_bufs, c_sems)]
    slot = load_ahead(streams, turn, turns)
    outs = [Stream(out_near, out_far, out_bufs, out_sems, turns)]
    free_slot(outs, turn, slot)
    x_ref, c_ref, out_ref = x_bufs.at[slot], c_bufs.at[slot], out_bufs.at[slot]
    blocks, tokens, width = x_ref.shape

    @pl.when(turn == 0)
    def clear():
        for ref in (deg_ref, deu_ref, ded_ref, dcat_ref, dsd_ref):
            ref[...] = jnp.zeros_like(ref)

    hidden_rows = x_ref[...].reshape(blocks * tokens, width)
    picked = xs_ref[...]
    ded_ref[...] += left_contraction(hid_ref[...], pg_ref[...])
    deg_ref[...] += left_contraction(picked, gg_ref[...])
    deu_ref[...] += left_contraction(picked, ug_ref[...])
    dsd_ref[...] += left_contraction(sh_ref[...], c_ref[...].reshape(blocks * tokens, width))
    dcat_ref[:PAIR] += left_contraction(sg_ref[...], hidden_rows)
    logits = jnp.concatenate([lg_ref[index] for index in range(blocks)], axis=1)
    dcat_ref[PAIR:] += matmul(logits, hidden_rows)
    shared_out = matmul(sh_ref[...], sd_ref[...])
    for index in range(blocks):
        span = slice(index * tokens, (index + 1) * tokens)
        slots = slice(index * CAP, (index + 1) * CAP)
        out_ref[index] = (
            shared_out[span] + left_contraction(chosen_ref[index], give_ref[slots])
        ).astype(low)
    store_out(outs, turn, turns, slot)


def grouped(shape):
    return pl.BlockSpec(shape, lambda i, *rest: (i,) + (0,) * (len(shape) - 1))


def fixed(shape):
    return pl.BlockSpec(
        shape, lambda i, *rest: (0,) * len(shape), pipeline_mode=pl.Buffered(1)
    )


def feed_kernel(body, name, scalars, arrays, in_specs, shapes, out_specs, scratch, flops, moved, turns):
    return pl.pallas_call(
        body,
        out_shape=shapes,
        grid_spec=pltpu.PrefetchScalarGridSpec(
            num_scalar_prefetch=len(scalars),
            grid=(turns,),
            in_specs=in_specs,
            out_specs=out_specs,
            scratch_shapes=scratch,
        ),
        compiler_params=pltpu.CompilerParams(
            dimension_semantics=("arbitrary",), vmem_limit_bytes=60 << 20
        ),
        cost_estimate=pl.CostEstimate(flops=flops, bytes_accessed=moved, transcendentals=0),
        name=name,
    )(*scalars, *arrays)


anywhere = pl.BlockSpec(memory_space=pl.ANY)


def choose_call(expert, order, c_all, route_rows, sd, count, tokens):
    width = c_all.shape[2]
    return feed_kernel(
        choose_body,
        "choose",
        (expert, order),
        (c_all, route_rows, sd),
        [anywhere, grouped((GROUP, 2, tokens)), fixed(sd.shape)],
        (
            jax.ShapeDtypeStruct((count * CAP, width), low),
            jax.ShapeDtypeStruct((count * tokens, PAIR), wide),
            jax.ShapeDtypeStruct((count, CAP, tokens), low),
        ),
        (grouped((GROUP * CAP, width)), grouped((GROUP * tokens, PAIR)), grouped((GROUP, CAP, tokens))),
        [pltpu.VMEM((2, GROUP, tokens, width), low), pltpu.SemaphoreType.DMA((2,))],
        8 * count * tokens * width * PAIR,
        count * tokens * width * 3,
        count // GROUP,
    )


def feed_call(expert, x_near, x_far, route_rows, pick, shared, chosen, cat, rt, gate, up, down):
    half, tokens, width = x_near.shape
    count, units = 2 * half, gate.shape[2]
    slots, rows = GROUP * CAP, GROUP * tokens
    parts = jax.ShapeDtypeStruct((half, tokens, width), low)
    saved = (
        (count * CAP, width), (count * CAP, width), (count * CAP, units), (count * CAP, units),
        (count * CAP, units), (count * CAP, width), (count * tokens, PAIR), (count * tokens, PAIR),
        (count, 2 * EXPERTS, tokens),
    )
    return feed_kernel(
        feed_body,
        "feed",
        (expert,),
        (x_near, x_far, route_rows, pick, shared, chosen, cat, rt, gate, up, down),
        [
            anywhere,
            anywhere,
            grouped((GROUP, 2, tokens)),
            grouped((slots, width)),
            grouped((rows, PAIR)),
            grouped((GROUP, CAP, tokens)),
            fixed(cat.shape),
            fixed(rt.shape),
            fixed(gate.shape),
            fixed(up.shape),
            fixed(down.shape),
        ],
        (parts, parts) + tuple(jax.ShapeDtypeStruct(shape, low) for shape in saved),
        (anywhere, anywhere)
        + tuple(grouped((shape[0] * GROUP // count,) + shape[1:]) for shape in saved),
        [pltpu.VMEM((2, GROUP, tokens, width), low)] * 2 + [pltpu.SemaphoreType.DMA((2,))] * 2,
        48 * count * CAP * width * units // 2,
        count * tokens * width * 6,
        count // GROUP,
    )


def rest_call(gate, order, x_near, x_far, c_all, chosen, saved, sd, units):
    half, tokens, width = x_near.shape
    count = 2 * half
    parts = jax.ShapeDtypeStruct((half, tokens, width), low)
    shapes = ((width, units), (width, units), (units, width), (PAIR + 2 * EXPERTS, width), (PAIR, width))
    return feed_kernel(
        rest_body,
        "rest",
        (gate, order),
        (x_near, x_far, c_all, chosen) + tuple(saved) + (sd,),
        [anywhere, anywhere, anywhere, grouped((GROUP, CAP, tokens))]
        + [grouped((array.shape[0] * GROUP // count,) + array.shape[1:]) for array in saved]
        + [fixed(sd.shape)],
        (parts, parts) + tuple(jax.ShapeDtypeStruct(shape, wide) for shape in shapes),
        (anywhere, anywhere) + tuple(fixed(shape) for shape in shapes),
        [pltpu.VMEM((2, GROUP, tokens, width), low)] * 3 + [pltpu.SemaphoreType.DMA((2,))] * 3,
        24 * count * CAP * width * units // 2,
        count * tokens * width * 8,
        count // GROUP,
    )


def shards(
    inputs,
    blocks,
    routes,
    attn_gain,
    w_query,
    w_key,
    w_value,
    w_out,
    ffn_gain,
    w_router,
    shared_gate,
    shared_up,
    shared_down,
    expert_gate,
    expert_up,
    expert_down,
    cotangent,
):
    heads, line = lax.axis_size("head"), lax.axis_size("blk")
    count = heads * line
    head, spot = lax.axis_index("head"), lax.axis_index("blk")
    device = head * line + spot
    tokens, width = inputs.shape
    total = count * tokens
    group = width // heads
    pairs = group // PAIR
    rows = w_query.shape[0]
    steps, short_steps = whole_steps(count), line_steps(line)
    sources = slot_sources(count, steps)
    places = jnp.asarray(np.argsort(sources, axis=1).astype(np.int32))[device]
    slot_sources_own = jnp.asarray(sources)[device]
    short_sources = slot_sources(line, short_steps)
    short_order = jnp.asarray(short_sources)[spot]
    short_places = jnp.asarray(np.argsort(short_sources, axis=1).astype(np.int32))[spot]

    def pad_rows(flat):
        extra = -flat.shape[0] % width
        return jnp.pad(flat, (0, extra)).reshape(-1, width)

    def pad_tall(values):
        return jnp.pad(values, ((0, -values.shape[0] % 16), (0, 0)))

    hop = lambda values, step: permute(values, BOTH, count, step)
    far_steps, cross, chip = steps[:-3], steps[-3:-1], steps[-1]

    own_blocks = jnp.arange(heads, dtype=jnp.int32) * line + spot
    own_slots = places[own_blocks]
    tile = TILE_BLOCKS * tokens
    own_ids = jnp.take(blocks.reshape(count, tokens), own_blocks, axis=0, mode="clip")
    low_id, high_id = own_ids[:, :1], own_ids[:, -1:]

    def counted(test):
        return jnp.sum(test, axis=1, dtype=jnp.int32)

    query_bounds = jnp.stack(
        [
            counted(blocks[None] <= low_id) // tile,
            (counted(blocks[None] <= high_id) + tile - 1) // tile,
        ]
    )
    key_bounds = jnp.stack(
        [
            counted(blocks[None] < low_id) // tile,
            (counted(blocks[None] < high_id) + tile - 1) // tile,
            jnp.full((heads,), total // tile, jnp.int32),
        ]
    )
    id_columns = jnp.tile(own_ids, (1, 2))[:, :, None]
    id_rows = blocks.reshape(count, 1, tokens)

    block_ids = jnp.arange(count, dtype=jnp.int32)
    grad_slots = short_places[block_ids % line] * heads + block_ids // line
    tables = (own_slots, query_bounds, key_bounds, id_columns, grad_slots)

    halves = lambda matrix: matrix.reshape(rows, heads, group).transpose(1, 0, 2)
    extras = jnp.concatenate(
        [attn_gain, ffn_gain, w_router.reshape(-1), routes.T.reshape(-1).astype(low)]
    )
    extras = jnp.pad(extras, (0, -extras.shape[0] % group)).reshape(-1, group)
    split = [halves(matrix) for matrix in (w_query, w_key, w_value)]
    split = jnp.concatenate(split + [jnp.broadcast_to(extras, (heads,) + extras.shape)], axis=1)
    split = jnp.pad(split, ((0, 0), (0, -split.shape[1] % 16), (0, 0)))
    kept = lax.dynamic_index_in_dim(split, head, 0, False)
    sent = lax.dynamic_index_in_dim(split, 1 - head, 0, False)
    weights = [head_order(head, kept, swap_heads(sent))[None]]
    first_steps = weight_steps(line)
    first_places = jnp.asarray(
        np.argsort(slot_sources(line, first_steps), axis=1).astype(np.int32)
    )[spot]
    for step in first_steps[:-1]:
        weights.append(grow(weights[-1], permute(weights[-1], "blk", line, step)))
    weights_far = permute(weights[-1], "blk", line, first_steps[-1])
    held = [inputs[None]]
    shared_slice = shared_gate.shape[1] // count
    shared_pack = jnp.stack(
        [
            shared_gate.reshape(rows, count, shared_slice),
            shared_up.reshape(rows, count, shared_slice),
        ],
        axis=2,
    ).reshape(rows, count * 2 * shared_slice)
    for place, step in enumerate(steps[:-1]):
        start = held[-1]
        if step is cross[1]:
            start, shared_pack = lax.optimization_barrier((start, shared_pack))
            start = after(start, *tables)
        held.append(grow(start, after(hop(start, step), weights[min(place, len(weights) - 1)])))
    shared_in = lax.all_to_all(shared_pack, BOTH, split_axis=1, concat_axis=0, tiled=True)
    inputs_near = held[-1]
    inputs_far = hop(after(inputs_near, shared_in), chip)

    cot_all = after(jnp.concatenate([cotangent, w_out], axis=0), held[len(far_steps) + 1])
    cot_all = lax.all_gather(cot_all, BOTH, axis=0, tiled=False)
    full_out = cot_all[:, tokens:].reshape(width, width)

    query_weight, key_weight = unpack_call(first_places, weights[-1], weights_far, width)
    first_row = 3 * rows
    flat = grow(weights[-1][:, :, first_row:], weights_far[:, :, first_row:])
    flat = flat.reshape(line, heads, -1)
    flat = jnp.take(flat, first_places, axis=0, mode="clip").transpose(1, 0, 2)
    flat = flat.reshape(count, -1)
    gain_first = flat[:, :rows].reshape(width).astype(wide)
    gain_second = flat[:, rows : 2 * rows].reshape(width).astype(wide)
    router = flat[:, 2 * rows : (2 + EXPERTS) * rows].reshape(width, EXPERTS)
    route_rows = flat[:, (2 + EXPERTS) * rows : (2 + EXPERTS) * rows + 2 * tokens]
    route_rows = jnp.take(route_rows, slot_sources_own, axis=0, mode="clip")
    route_rows = route_rows.reshape(count, 2, tokens).astype(jnp.int32)

    keys, token = project_call(inputs_near, gain_first[None], key_weight, 1.0, count, None)
    keys, token = project_call(inputs_far, gain_first[None], key_weight, 1.0, count, keys)
    neighbour = lax.dynamic_index_in_dim(
        inputs_near, places[(1 - head) * line + spot], 0, False
    )
    pair_inputs = head_order(head, inputs, neighbour).reshape(heads * tokens, width)
    pair_normed = rms_scale(pair_inputs.astype(wide), gain_first).astype(low)
    own_queries = (matmul(pair_normed, query_weight) * scale_factor).astype(low)
    own_queries = own_queries.reshape(heads, tokens, group)
    expert = (device % EXPERTS).astype(jnp.int32).reshape(1)

    own_spec = lambda column: pl.BlockSpec(
        (1, tokens, PAIR), lambda p, j, own, *rest: (own[j], 0, column + p)
    )
    all_spec = lambda column: pl.BlockSpec(
        (count, tokens, PAIR), lambda p, j, *rest: (0, 0, column + p)
    )
    part_spec = pl.BlockSpec((1, tokens, PAIR), lambda p, j, *rest: (j, 0, p))
    stat_spec = pl.BlockSpec((1, 1, 1, 2 * tokens), lambda p, j, *rest: (p, j, 0, 0))
    column_spec = pl.BlockSpec((1, 2 * tokens, 1), lambda p, j, *rest: (j, 0, 0))
    ids_spec = pl.BlockSpec((count, 1, tokens), lambda p, j, *rest: (0, 0, 0))
    part_shape = jax.ShapeDtypeStruct((heads, tokens, group), low)
    stat_shape = jax.ShapeDtypeStruct((pairs, heads, 1, 2 * tokens), wide)
    grid = (pairs, heads)
    unit = 2 * heads * tokens * total * group

    attended_own, lse = attention_call(
        attend_body,
        "attend",
        (
            after(own_slots, route_rows),
            places,
            query_bounds,
        ),
        (own_queries, keys, keys, id_columns, id_rows),
        [part_spec, all_spec(0), all_spec(pairs), column_spec, ids_spec],
        (part_shape, stat_shape),
        (part_spec, stat_spec),
        grid,
        2 * unit,
        count,
    )
    attended_back = swap_heads(lax.dynamic_index_in_dim(attended_own, 1 - head, 0, False))
    attended_kept = lax.dynamic_index_in_dim(attended_own, head, 0, False)
    attended = jnp.where(
        head == 0,
        jnp.concatenate([attended_kept, attended_back], axis=1),
        jnp.concatenate([attended_back, attended_kept], axis=1),
    )
    inputs_wide = inputs.astype(wide)
    mixed_rows = inputs_wide + matmul(attended, full_out)
    normed_ffn = rms_scale(mixed_rows, gain_second).astype(low)

    half_pad = HEAD_DIM - shared_slice
    shared_pair = jnp.pad(
        shared_in.reshape(width, 2, shared_slice), ((0, 0), (0, 0), (0, half_pad))
    ).reshape(width, PAIR)
    feed_weight = jnp.concatenate(
        [shared_pair, router, jnp.zeros((width, PAIR - EXPERTS), low)], axis=1
    )
    down_pad = jnp.pad(shared_down, ((0, PAIR - shared_slice), (0, 0)))
    router_rows = jnp.transpose(jnp.concatenate([router, router], axis=1))

    near = normed_ffn[None]
    for step in steps[:-2]:
        arrived = hop(near, step)
        if step is steps[0]:
            gate = after(gain_first[None], near)
            queries, token = project_call(inputs_near, gate, query_weight, scale_factor, count, None)
            arrived = after(arrived, token)
        if step is steps[1]:
            gate = after(gain_first[None], near)
            queries, token = project_call(inputs_far, gate, query_weight, scale_factor, count, queries)
            arrived = after(arrived, token)
        near = grow(near, arrived)
    pick, shared_grad, chosen = choose_call(
        after(expert, near), slot_sources_own, cot_all, route_rows, down_pad, count, tokens
    )
    near = grow(near, after(hop(near, cross[1]), chosen, feed_weight))
    arrived = hop(near, chip)
    row_near, row_far, *saved = feed_call(
        expert, near, arrived, route_rows, pick, shared_grad, chosen, feed_weight, router_rows,
        expert_gate, expert_up, expert_down,
    )
    terms = [row_near, hop(row_far, chip)]
    row_upper = upper(terms)
    out_near, out_far, grad_egate, grad_eup, grad_edown, grad_feed, grad_sdown = rest_call(
        after(expert, row_upper), slot_sources_own, near, arrived, cot_all, chosen, saved, down_pad,
        expert_gate.shape[2],
    )
    terms = lower(terms) + [after(hop(row_upper, cross[1]), out_near)]
    out_far, terms[-1] = lax.optimization_barrier((out_far, terms[-1]))
    out_terms = [out_near, hop(out_far, chip)]
    grad_sdown = grad_sdown[:shared_slice]
    out_upper = upper(out_terms)
    terms = scatter_step(terms, BOTH, count, cross[0])
    terms[-1], out_upper = lax.optimization_barrier((terms[-1], out_upper))
    out_arrived = hop(out_upper, cross[1])
    grad_shared, terms[-1] = lax.optimization_barrier((grad_feed[:PAIR], terms[-1]))
    grad_shared = grad_shared.reshape(2, HEAD_DIM, width)[:, :shared_slice].reshape(-1, width)
    grad_shared = jnp.transpose(grad_shared).astype(low)
    grad_shared_back = lax.all_to_all(grad_shared, BOTH, split_axis=0, concat_axis=1, tiled=True)
    for step in reversed(far_steps):
        terms = scatter_step(terms, BOTH, count, step)
    normed_ffn_grad = finish(terms)
    grad_router = jnp.transpose(
        grad_feed[PAIR : PAIR + EXPERTS] + grad_feed[PAIR + EXPERTS : PAIR + 2 * EXPERTS]
    )

    unused_second, second_pull = jax.vjp(rms_scale, mixed_rows, gain_second)
    mixed_part, grad_gain_ffn = second_pull(normed_ffn_grad)
    mixed_grad = cotangent.astype(wide) + mixed_part
    mixed_low = after(mixed_grad.astype(low), out_arrived, grad_shared_back)
    mixed_pair = head_order(head, mixed_low, swap_heads(mixed_low)).reshape(heads * tokens, width)
    own_out = lax.dynamic_slice_in_dim(full_out, head * group, group, 0)
    attended_grad = right_contract(mixed_pair, own_out).astype(low)
    attended_flat = attended_own.reshape(heads * tokens, group)
    head_marks = (
        jnp.arange(group)[None] // HEAD_DIM == jnp.arange(2 * pairs)[:, None]
    ).astype(wide)
    delta = lax.dot_general(
        head_marks,
        attended_grad.astype(wide) * attended_flat.astype(wide),
        (((1,), (1,)), ((), ())),
        precision=lax.Precision.HIGHEST,
    )
    delta = (
        delta.reshape(pairs, 2, heads, tokens)
        .transpose(0, 2, 1, 3)
        .reshape(pairs, heads, 1, 2 * tokens)
    )
    stats = jnp.stack([lse, delta]).transpose(2, 0, 1, 3, 4).reshape(heads, -1)
    stats_rows = jnp.concatenate(two_parts(stats), axis=1).reshape(heads, -1, group)
    grad_parts = attended_grad.reshape(heads, tokens, group)
    grads = [jnp.concatenate([grad_parts, stats_rows], axis=1)[None]]
    def next_out(terms, arrived, gate):
        terms = terms + [arrived]
        sent = upper(terms)
        gate, sent = lax.optimization_barrier((gate, sent))
        return lower(terms), sent, gate

    columns = two_parts(jnp.concatenate([grad_gain_ffn[:, None], grad_router], axis=1))
    extra = columns[0].shape[1]
    columns = jnp.concatenate(columns, axis=1)
    columns = jnp.pad(columns, ((0, 0), (1, PAIR - 1 - 2 * extra)))
    out_terms, sent, grads[0] = next_out(lower(out_terms), out_arrived, grads[0])
    out_arrived = hop(sent, cross[0])
    tail = list(reversed(far_steps))
    for place, step in enumerate(short_steps[:-1]):
        if place == 1:
            grads[-1] = after(grads[-1], out_arrived, columns)
        if place == len(short_steps) - 2:
            out_terms, sent, grads[-1] = next_out(out_terms, out_arrived, grads[-1])
            out_arrived = hop(sent, tail[0])
        grads.append(grow(grads[-1], permute(grads[-1], "blk", line, step)))
    query_q = after(own_slots, grads[-2])
    query_grad = attention_call(
        query_body,
        "query_gradient",
        (query_q, places, query_bounds),
        (own_queries, keys, keys, grad_parts, lse, delta, id_columns, id_rows),
        [
            part_spec,
            all_spec(0),
            all_spec(pairs),
            part_spec,
            stat_spec,
            stat_spec,
            column_spec,
            ids_spec,
        ],
        part_shape,
        part_spec,
        grid,
        3 * unit,
        count,
    )
    start = after(grads[-1], query_grad)
    out_terms, sent, start = next_out(out_terms, out_arrived, start)
    for step in tail[1:-1]:
        out_terms, sent, start = next_out(out_terms, hop(sent, step), start)
    out_arrived = hop(sent, tail[-1])
    grads.append(grow(start, permute(start, "blk", line, short_steps[-1])))
    grads_all = grads[-1].reshape(count, -1, group)
    stats_all = grads_all[:, tokens:].reshape(line, heads, 2, -1).astype(wide)
    stats_all = (stats_all[:, :, 0] + stats_all[:, :, 1]).reshape(-1, 1, 2 * tokens)
    key_grad, value_grad = attention_call(
        key_body,
        "key_gradient",
        (own_slots, places, grad_slots, key_bounds),
        (keys, keys, queries, grads_all, stats_all, id_columns, id_rows),
        [
            own_spec(0),
            own_spec(pairs),
            all_spec(0),
            all_spec(0),
            pl.BlockSpec(stats_all.shape, lambda p, j, *rest: (0, 0, 0)),
            column_spec,
            ids_spec,
        ],
        (part_shape, part_shape),
        (part_spec, part_spec),
        grid,
        4 * unit,
        count,
    )

    near, far, normed_part = weights_call(
        short_places, pair_inputs, gain_first[None], query_grad, key_grad, value_grad,
        query_weight, key_weight, columns, attended_flat, mixed_pair, line,
    )
    backward = list(reversed(short_steps))
    sums = [near, permute(far, "blk", line, backward[0])]
    out_terms.append(out_arrived)
    for place, step in enumerate(backward[1:]):
        sums = scatter_step(sums, "blk", line, step)
        if place == 0:
            first_sum = sums[-1]
            sums[-1] = after(sums[-1], out_arrived)
    output = (mixed_rows + finish(out_terms)).astype(low)
    sums = [sums]
    summed = finish(sums[0])
    grad_wout_own = summed[:, :, 3 * group + PAIR :].transpose(1, 0, 2).reshape(rows, width)
    summed = summed[:, :, : 3 * group + PAIR]
    summed_back = swap_heads(
        lax.dynamic_index_in_dim(summed, 1 - head, 0, False).astype(low)
    ).astype(wide)
    summed_kept = lax.dynamic_index_in_dim(summed, head, 0, False)
    joined = head_order(head, summed_kept, summed_back)
    small = jnp.sum(joined[:, :, 3 * group :], axis=0)
    gain_column = small[:, 0] + small[:, PAIR - 1]
    small = small[:, 1 : extra + 1] + small[:, extra + 1 : 2 * extra + 1]
    joined = joined[:, :, : 3 * group].reshape(heads, rows, 3, group)
    joined = joined.transpose(2, 1, 0, 3).reshape(3, rows, width)

    normed_parts = normed_part.reshape(heads, tokens, width)
    arrived = swap_heads(lax.dynamic_index_in_dim(normed_parts, 1 - head, 0, False).astype(low))
    normed_grad = lax.dynamic_index_in_dim(normed_parts, head, 0, False) + arrived.astype(wide)
    unused_first, first_pull = jax.vjp(lambda rows_in: rms_scale(rows_in, gain_first), inputs_wide)
    grad_inputs = mixed_grad + first_pull(after(normed_grad, first_sum))[0]
    grad_shared_back = after(grad_shared_back, first_sum).reshape(rows, count, 2, shared_slice)
    grad_sgate = grad_shared_back[:, :, 0].reshape(rows, -1).astype(wide)
    grad_sup = grad_shared_back[:, :, 1].reshape(rows, -1).astype(wide)

    return (
        output,
        grad_inputs,
        gain_column,
        joined[0].astype(wide),
        joined[1].astype(wide),
        joined[2].astype(wide),
        grad_wout_own,
        small[:, 0],
        small[:, 1:],
        grad_sgate,
        grad_sup,
        grad_sdown,
        grad_egate[None],
        grad_eup[None],
        grad_edown[None],
    )


def solution(mesh):
    both = P(BOTH)
    rows = P(BOTH, None)
    slabs = P(BOTH, None, None)
    return jax.shard_map(
        shards,
        mesh=mesh,
        in_specs=(
            rows, P(), rows, both, rows, rows, rows, rows, both, rows, rows, rows, rows,
            slabs, slabs, slabs, rows,
        ),
        out_specs=(
            rows, rows, both, rows, rows, rows, rows, both, rows, rows, rows, rows,
            slabs, slabs, slabs,
        ),
        check_vma=False,
    )
```

```python
import functools

import jax
import jax.numpy as jnp
import numpy as np
from jax import lax
from jax.experimental import pallas as pl
from jax.experimental.pallas import tpu as pltpu
from jax.sharding import PartitionSpec as P

HEAD_DIM = 64
EXPERTS = 16
CAP = 32
PAIR = 2 * HEAD_DIM
TILE_BLOCKS = 8
BOTH = ("head", "blk")

epsilon = 1e-05
scale_factor = 0.125
masked_value = -1e30
low = jnp.bfloat16
wide = jnp.float32


def matmul(left_side, right_side):
    return jnp.dot(left_side, right_side, preferred_element_type=wide)


def left_contraction(left_side, right_side):
    return lax.dot_general(
        left_side, right_side, (((0,), (0,)), ((), ())), preferred_element_type=wide
    )


def right_contract(left_side, right_side):
    return lax.dot_general(
        left_side, right_side, (((1,), (1,)), ((), ())), preferred_element_type=wide
    )


def rms_scale(values, gain_row):
    return (
        values * lax.rsqrt(jnp.mean(values * values, axis=-1, keepdims=True) + epsilon) * gain_row
    )


def silu_parts(gate_pre, up_pre):
    gate = jax.nn.sigmoid(gate_pre)
    swish = gate_pre * gate
    return swish * up_pre, gate * (1.0 + gate_pre * (1.0 - gate)) * up_pre, swish


def whole_steps(count):
    bits = count.bit_length() - 1
    steps = [functools.partial(flip, bit, bit) for bit in range(bits - 2, 1, -1)]
    return steps + [
        functools.partial(flip, 1, bits - 1),
        functools.partial(flip, bits - 1, 1),
        functools.partial(flip, 0, 0),
    ]


def flip(even_bit, odd_bit, index):
    return index ^ (1 << (odd_bit if index & 1 else even_bit))


def line_steps(count):
    bits = count.bit_length() - 1
    return [functools.partial(flip, bit, bit) for bit in range(bits - 1, -1, -1)]


def weight_steps(count):
    steps = line_steps(count)
    return [steps[-2]] + steps[:-2] + [steps[-1]]


def slot_sources(count, steps):
    order = [[i] for i in range(count)]
    for step in steps:
        order = [order[i] + order[step(i)] for i in range(count)]
    return np.array(order, np.int32)


def permute(values, axis, count, step):
    return lax.ppermute(values, axis, [(i, step(i)) for i in range(count)])


def after(value, *needed):
    return lax.optimization_barrier((value,) + needed)[0]


def two_parts(values):
    high = lax.reduce_precision(values, 8, 7)
    return [high.astype(low), (values - high).astype(low)]


def grow(held, arrived):
    return jnp.concatenate([held, arrived], axis=0)


def gather(values, axis, count, steps):
    held = values[None]
    for step in steps:
        held = grow(held, permute(held, axis, count, step))
    return held


def upper(terms):
    half = terms[0].shape[0] // 2
    return sum(term[half:].astype(wide) for term in terms).astype(low)


def lower(terms):
    half = terms[0].shape[0] // 2
    return [term[:half] for term in terms]


def scatter_step(terms, axis, count, step):
    return lower(terms) + [permute(upper(terms), axis, count, step)]


def finish(terms):
    return sum(term[0].astype(wide) for term in terms)


def scatter_sum(slots, axis, count, steps):
    terms = [slots]
    for step in reversed(steps):
        terms = scatter_step(terms, axis, count, step)
    return finish(terms)


def swap_heads(values):
    return lax.ppermute(values, "head", [(0, 1), (1, 0)])


def head_order(head, own, other):
    return jnp.where(head == 0, jnp.stack([own, other]), jnp.stack([other, own]))


def stack_heads(rows):
    first = lax.broadcasted_iota(jnp.int32, rows.shape, 1) < HEAD_DIM
    zero = jnp.zeros_like(rows)
    return jnp.concatenate([jnp.where(first, rows, zero), jnp.where(first, zero, rows)], axis=0)


def join_heads(stacked):
    half = stacked.shape[0] // 2
    top = stacked[:half]
    first = lax.broadcasted_iota(jnp.int32, top.shape, 1) < HEAD_DIM
    return jnp.where(first, top, stacked[half:])


def load_tile(ref, slots, index):
    return jnp.concatenate(
        [ref[slots[index * TILE_BLOCKS + part]] for part in range(TILE_BLOCKS)], axis=0
    )


def load_ids(ref, index):
    return jnp.concatenate(
        [ref[index * TILE_BLOCKS + part] for part in range(TILE_BLOCKS)], axis=1
    )


def as_column(row):
    return jnp.transpose(jnp.broadcast_to(row, (PAIR, row.shape[1])))[:, :1]


def attend_body(own, slots, bounds, q_ref, k_ref, v_ref, qid_ref, kid_ref, out_ref, lse_ref):
    part = pl.program_id(1)
    stacked = stack_heads(q_ref[0])
    rows = stacked.shape[0]

    def step(masked, index, state):
        top, total, weighted = state
        scores = right_contract(stacked, load_tile(k_ref, slots, index))
        if masked:
            scores = jnp.where(load_ids(kid_ref, index) <= qid_ref[0], scores, masked_value)
        new_top = jnp.maximum(top, jnp.max(scores, axis=-1, keepdims=True))
        weights = jnp.exp(scores - new_top)
        rescale = jnp.exp(top - new_top)
        total = total * rescale + jnp.sum(weights, axis=-1, keepdims=True)
        weighted = weighted * rescale + matmul(weights.astype(low), load_tile(v_ref, slots, index))
        return new_top, total, weighted

    state = (
        jnp.full((rows, 1), masked_value, wide),
        jnp.zeros((rows, 1), wide),
        jnp.zeros((rows, PAIR), wide),
    )
    state = lax.fori_loop(0, bounds[0, part], functools.partial(step, False), state)
    top, total, weighted = lax.fori_loop(
        bounds[0, part], bounds[1, part], functools.partial(step, True), state
    )
    out_ref[0] = join_heads(weighted / total).astype(low)
    lse = jnp.broadcast_to(top + jnp.log(total), (rows, PAIR))
    lse_ref[0, 0] = jnp.transpose(lse)[:1]


def query_body(
    own, slots, bounds, q_ref, k_ref, v_ref, g_ref, lse_ref, delta_ref, qid_ref, kid_ref, dq_ref
):
    part = pl.program_id(1)
    stacked = stack_heads(q_ref[0])
    grads = stack_heads(g_ref[0])
    lse = as_column(lse_ref[0, 0])
    delta = as_column(delta_ref[0, 0])

    def step(masked, index, total):
        keys = load_tile(k_ref, slots, index)
        probs = jnp.exp(right_contract(stacked, keys) - lse)
        if masked:
            probs = jnp.where(load_ids(kid_ref, index) <= qid_ref[0], probs, 0.0)
        moved = right_contract(grads, load_tile(v_ref, slots, index)) - delta
        return total + matmul((probs * moved).astype(low), keys)

    total = jnp.zeros((stacked.shape[0], PAIR), wide)
    total = lax.fori_loop(0, bounds[0, part], functools.partial(step, False), total)
    total = lax.fori_loop(
        bounds[0, part], bounds[1, part], functools.partial(step, True), total
    )
    dq_ref[0] = (join_heads(total) * scale_factor).astype(low)


def key_body(
    own, slots, gslots, bounds, k_ref, v_ref, q_ref, g_near, g_far, stat_ref, kid_ref, qid_ref,
    dk_ref, dv_ref,
):
    pair = pl.program_id(0)
    part = pl.program_id(1)
    pairs = pl.num_programs(0)
    keys = stack_heads(k_ref[0])
    values = stack_heads(v_ref[0])
    rows = keys.shape[0]
    half = g_near.shape[0]

    def stat_rows(index, which):
        tops, bottoms = [], []
        for piece in range(TILE_BLOCKS):
            slot = gslots[index * TILE_BLOCKS + piece]
            place = slot * (2 * pairs) + which * pairs + pair
            row = stat_ref[place]
            tops.append(row[:, :PAIR])
            bottoms.append(row[:, PAIR:])
        shape = (rows // 2, TILE_BLOCKS * PAIR)
        return jnp.concatenate(
            [
                jnp.broadcast_to(jnp.concatenate(tops, axis=1), shape),
                jnp.broadcast_to(jnp.concatenate(bottoms, axis=1), shape),
            ],
            axis=0,
        )

    def step(masked, index, state):
        dk_total, dv_total = state
        queries = load_tile(q_ref, slots, index)
        grads = []
        for piece in range(TILE_BLOCKS):
            slot = gslots[index * TILE_BLOCKS + piece]
            near = g_near[jnp.minimum(slot, half - 1)]
            grads.append(jnp.where(slot < half, near, g_far[jnp.maximum(slot - half, 0)]))
        grads = jnp.concatenate(grads, axis=0)
        probs = jnp.exp(right_contract(keys, queries) - stat_rows(index, 0))
        if masked:
            probs = jnp.where(kid_ref[0] <= load_ids(qid_ref, index), probs, 0.0)
        moved = right_contract(values, grads) - stat_rows(index, 1)
        dk_total = dk_total + matmul((probs * moved).astype(low), queries)
        dv_total = dv_total + matmul(probs.astype(low), grads)
        return dk_total, dv_total

    state = (jnp.zeros((rows, PAIR), wide), jnp.zeros((rows, PAIR), wide))
    state = lax.fori_loop(
        bounds[0, part], bounds[1, part], functools.partial(step, True), state
    )
    dk_total, dv_total = lax.fori_loop(
        bounds[1, part], bounds[2, part], functools.partial(step, False), state
    )
    dk_ref[0] = join_heads(dk_total).astype(low)
    dv_ref[0] = join_heads(dv_total).astype(low)


def attention_call(body, name, tables, arrays, specs, outs, out_specs, grid, cost, count):
    return pl.pallas_call(
        body,
        out_shape=outs,
        grid_spec=pltpu.PrefetchScalarGridSpec(
            num_scalar_prefetch=len(tables), grid=grid, in_specs=specs, out_specs=out_specs
        ),
        compiler_params=pltpu.CompilerParams(
            dimension_semantics=("arbitrary", "arbitrary"),
            vmem_limit_bytes=60 << 20,
        ),
        cost_estimate=pl.CostEstimate(
            flops=8 * cost, bytes_accessed=cost // 512, transcendentals=cost // 512
        ),
        name=name,
    )(*tables, *arrays)


def unpack_body(slots, near_ref, far_ref, query_ref, key_ref):
    half, heads, unused, group = near_ref.shape
    line = 2 * half
    rows = query_ref.shape[0] // (heads * line)
    for spot in range(line):
        slot = slots[spot]
        is_near = slot < half
        low_slot, high_slot = jnp.minimum(slot, half - 1), jnp.maximum(slot - half, 0)
        for source in range(heads):
            block = jnp.where(is_near, near_ref[low_slot, source], far_ref[high_slot, source])
            first = (source * line + spot) * rows
            query_ref[first : first + rows] = block[:rows]
            for part in range(2):
                key_ref[first : first + rows, part * group : (part + 1) * group] = block[
                    (part + 1) * rows : (part + 2) * rows
                ]


def unpack_call(slots, near, far, width):
    half, heads, unused, group = near.shape
    whole = lambda shape: pl.BlockSpec(shape, lambda i, *rest: (0,) * len(shape))
    shapes = ((width, group), (width, 2 * group))
    return pl.pallas_call(
        unpack_body,
        out_shape=tuple(jax.ShapeDtypeStruct(shape, low) for shape in shapes),
        grid_spec=pltpu.PrefetchScalarGridSpec(
            num_scalar_prefetch=1,
            grid=(1,),
            in_specs=[whole(near.shape), whole(far.shape)],
            out_specs=tuple(whole(shape) for shape in shapes),
        ),
        compiler_params=pltpu.CompilerParams(
            dimension_semantics=("arbitrary",), vmem_limit_bytes=32 << 20
        ),
        cost_estimate=pl.CostEstimate(
            flops=0, bytes_accessed=8 * near.size, transcendentals=0
        ),
        name="unpack",
    )(slots, near, far)


PROJECT = 4


def project_body(scale, x_ref, gain_ref, weight_ref, *refs):
    out_ref, token_ref = refs[-2:]
    token_ref[...] = jnp.zeros_like(token_ref)
    blocks, tokens, width = x_ref.shape
    rows = x_ref[...].reshape(blocks * tokens, width).astype(wide)
    normed = rms_scale(rows, gain_ref[...]).astype(low)
    out = matmul(normed, weight_ref[...]) * scale
    out_ref[...] = out.astype(low).reshape(blocks, tokens, -1)


def project_call(rows, gain, weight, scale, count, before):
    blocks, tokens, width = rows.shape
    columns = weight.shape[1]
    skip = 0 if before is None else (count - blocks) // PROJECT
    flat = lambda array: pl.BlockSpec(array.shape, lambda i: (0, 0))
    more = [] if before is None else [before]
    return pl.pallas_call(
        functools.partial(project_body, scale),
        out_shape=(
            jax.ShapeDtypeStruct((count, tokens, columns), low),
            jax.ShapeDtypeStruct((8, PAIR), wide),
        ),
        grid=(blocks // PROJECT,),
        in_specs=[
            pl.BlockSpec((PROJECT, tokens, width), lambda i: (i, 0, 0)),
            flat(gain),
            flat(weight),
        ]
        + [pl.BlockSpec(memory_space=pl.ANY)] * len(more),
        out_specs=(
            pl.BlockSpec((PROJECT, tokens, columns), lambda i: (i + skip, 0, 0)),
            pl.BlockSpec((8, PAIR), lambda i: (0, 0)),
        ),
        input_output_aliases={3: 0} if more else {},
        compiler_params=pltpu.CompilerParams(
            dimension_semantics=("arbitrary",), vmem_limit_bytes=60 << 20
        ),
        cost_estimate=pl.CostEstimate(
            flops=4 * blocks * tokens * width * columns,
            bytes_accessed=2 * blocks * tokens * (width + columns),
            transcendentals=0,
        ),
        name="project",
    )(rows, gain, weight, *more)


def weights_body(
    slots, x_ref, gain_ref, dq_ref, dk_ref, dv_ref, query_ref, key_ref, columns_ref, attended_ref, mixed_ref,
    near_ref, far_ref, part_ref,
):
    half, heads, rows, unused = near_ref.shape
    group = dq_ref.shape[1]
    unit = rms_scale(x_ref[...].astype(wide), 1.0)
    normed = (unit * gain_ref[...]).astype(low)
    grads = (dq_ref[...], dk_ref[...], dv_ref[...])
    part = (
        right_contract(grads[0], query_ref[...])
        + right_contract(grads[1], key_ref[:, :group])
        + right_contract(grads[2], key_ref[:, group:])
    )
    part_ref[...] = part
    gain = jnp.sum(part * unit, axis=0, keepdims=True)
    gain = jnp.transpose(jnp.broadcast_to(gain, (PAIR, gain.shape[1])))
    gain_high = gain.astype(low)
    gain_low = (gain - gain_high.astype(wide)).astype(low)
    lane = lax.broadcasted_iota(jnp.int32, gain.shape, 1)
    columns = jnp.where(lane == 0, gain_high, columns_ref[...])
    columns = jnp.where(lane == PAIR - 1, gain_low, columns)
    pieces = [left_contraction(normed, grad).astype(low) for grad in grads] + [columns]
    wout = left_contraction(attended_ref[...], mixed_ref[...]).astype(low)
    starts = [0, group, 2 * group, 3 * group]
    for spot in range(2 * half):
        slot = slots[spot]

        def give(ref, at, spot=spot):
            for source in range(heads):
                first = (source * 2 * half + spot) * rows
                for start, piece in zip(starts, pieces):
                    ref[at, source, :, start : start + piece.shape[1]] = piece[first : first + rows]
                ref[at, source, :, 3 * group + PAIR :] = wout[
                    spot * rows : (spot + 1) * rows, source * group : (source + 1) * group
                ]

        @pl.when(slot < half)
        def to_near():
            give(near_ref, slot)

        @pl.when(slot >= half)
        def to_far():
            give(far_ref, slot - half)


def weights_call(slots, inputs, gain, dq, dk, dv, query_weight, key_weight, columns, attended, mixed, line):
    heads, tokens, group = dq.shape
    width = inputs.shape[1]
    rows = width // (heads * line)
    flat = lambda array: array.reshape(heads * tokens, group)
    arrays = (inputs, gain, flat(dq), flat(dk), flat(dv), query_weight, key_weight, columns, attended, mixed)
    whole = lambda shape: pl.BlockSpec(shape, lambda i, *rest: (0,) * len(shape))
    parts = (line // 2, heads, rows, 4 * group + PAIR)
    return pl.pallas_call(
        weights_body,
        out_shape=(
            jax.ShapeDtypeStruct(parts, low),
            jax.ShapeDtypeStruct(parts, low),
            jax.ShapeDtypeStruct(inputs.shape, wide),
        ),
        grid_spec=pltpu.PrefetchScalarGridSpec(
            num_scalar_prefetch=1,
            grid=(1,),
            in_specs=[whole(array.shape) for array in arrays],
            out_specs=(whole(parts), whole(parts), whole(inputs.shape)),
        ),
        compiler_params=pltpu.CompilerParams(
            dimension_semantics=("arbitrary",), vmem_limit_bytes=60 << 20
        ),
        cost_estimate=pl.CostEstimate(
            flops=20 * heads * tokens * width * group, bytes_accessed=8 << 20, transcendentals=0
        ),
        name="weight_gradients",
    )(slots, *arrays)


GROUP = 8


class Stream:
    def __init__(self, pieces, buffers, semaphores, turns):
        self.pieces, self.buffers, self.semaphores = pieces, buffers, semaphores
        self.each, self.blocks = turns // len(pieces), buffers.shape[1]

    def load(self, index, place):
        self.begin(index, place, lambda part, buffer: (part, buffer))

    def store(self, index, place):
        self.begin(index, place, lambda part, buffer: (buffer, part))

    def begin(self, index, place, ends):
        for number, piece in enumerate(self.pieces):

            @pl.when(index // self.each == number)
            def start(piece=piece):
                part = piece.at[pl.ds(index % self.each * self.blocks, self.blocks)]
                source, target = ends(part, self.buffers.at[place])
                pltpu.make_async_copy(source, target, self.semaphores.at[place]).start()

    def loaded(self, place):
        pltpu.make_async_copy(
            self.pieces[0].at[pl.ds(0, self.blocks)],
            self.buffers.at[place],
            self.semaphores.at[place],
        ).wait()

    def stored(self, place):
        pltpu.make_async_copy(
            self.buffers.at[place],
            self.pieces[0].at[pl.ds(0, self.blocks)],
            self.semaphores.at[place],
        ).wait()


class Picked:
    def __init__(self, source, order, buffers, semaphores):
        self.source, self.order, self.buffers, self.semaphores = source, order, buffers, semaphores
        self.blocks, self.rows = buffers.shape[1:3]

    def load(self, index, place):
        for part in range(self.blocks):
            block = self.source.at[self.order[index * self.blocks + part], pl.ds(0, self.rows)]
            pltpu.make_async_copy(
                block, self.buffers.at[place, part], self.semaphores.at[place]
            ).start()

    def loaded(self, place):
        pltpu.make_async_copy(
            self.source.at[pl.ds(0, self.blocks), pl.ds(0, self.rows)],
            self.buffers.at[place],
            self.semaphores.at[place],
        ).wait()


PIECES = 4


def load_ahead(streams, turn, turns):
    slot = turn % 2

    @pl.when(turn == 0)
    def first():
        for stream in streams:
            stream.load(turn, slot)

    @pl.when(turn + 1 < turns)
    def ahead():
        for stream in streams:
            stream.load(turn + 1, 1 - slot)

    for stream in streams:
        stream.loaded(slot)
    return slot


def free_slot(streams, turn, slot):
    @pl.when(turn >= 2)
    def free():
        for stream in streams:
            stream.stored(slot)


def store_out(streams, turn, turns, slot):
    for stream in streams:
        stream.store(turn, slot)

    @pl.when(turn == turns - 1)
    def drain():
        for place in range(2):
            for stream in streams:
                stream.stored(place)


def choose_body(
    expert, order, c_all, route_ref, sd_ref, pick_ref, hidden_ref, chosen_ref, c_bufs, c_sems
):
    turn, turns = pl.program_id(0), pl.num_programs(0)
    slot = load_ahead([Picked(c_all, order, c_bufs, c_sems)], turn, turns)
    c_ref = c_bufs.at[slot]
    blocks, tokens, width = c_ref.shape
    hidden_ref[...] = right_contract(c_ref[...].reshape(blocks * tokens, width), sd_ref[...])
    routed = (route_ref[:, 0, :] == expert[0]) | (route_ref[:, 1, :] == expert[0])
    before = (
        lax.broadcasted_iota(jnp.int32, (tokens, tokens), 0)
        < lax.broadcasted_iota(jnp.int32, (tokens, tokens), 1)
    )
    rank = matmul(
        jnp.where(routed, 1.0, 0.0).astype(low), jnp.where(before, 1.0, 0.0).astype(low)
    )
    rank = jnp.where(routed, rank, -1.0)
    slot_ids = lax.broadcasted_iota(jnp.int32, (CAP, tokens), 0).astype(wide)
    for index in range(blocks):
        selector = jnp.where(rank[index : index + 1] == slot_ids, 1.0, 0.0).astype(low)
        chosen_ref[index] = selector
        pick_ref[index * CAP : (index + 1) * CAP] = matmul(selector, c_ref[index]).astype(low)


def feed_body(expert, *refs):
    x_pieces, refs = refs[:PIECES], refs[PIECES:]
    (route_ref, pick_ref, shared_ref, chosen_ref, cat_ref, rt_ref, eg_ref, eu_ref, ed_ref), refs = (
        refs[:9], refs[9:]
    )
    row_pieces, refs = refs[:PIECES], refs[PIECES:]
    (xs_ref, pg_ref, hid_ref, gg_ref, ug_ref, give_ref, sh_ref, sg_ref, lg_ref), refs = (
        refs[:9], refs[9:]
    )
    x_bufs, row_bufs, x_sems, row_sems = refs
    turn, turns = pl.program_id(0), pl.num_programs(0)
    slot = load_ahead([Stream(x_pieces, x_bufs, x_sems, turns)], turn, turns)
    rows_out = [Stream(row_pieces, row_bufs, row_sems, turns)]
    free_slot(rows_out, turn, slot)
    x_ref, row_ref = x_bufs.at[slot], row_bufs.at[slot]
    blocks, tokens, width = x_ref.shape
    count = blocks * tokens

    outcome = matmul(x_ref[...].reshape(count, width), cat_ref[...])
    pre = outcome[:, :PAIR]
    inside = lax.broadcasted_iota(jnp.int32, pre.shape, 1) < HEAD_DIM
    product, gate_slope, up_slope = silu_parts(pre, pltpu.roll(pre, HEAD_DIM, 1))
    sh_ref[...] = jnp.where(inside, product, 0.0).astype(low)
    shared_hidden_grad = shared_ref[...]
    gate_side = jnp.where(inside, shared_hidden_grad * gate_slope, 0.0)
    up_side = jnp.where(inside, shared_hidden_grad * up_slope, 0.0)
    shared_grad = (gate_side + pltpu.roll(up_side, HEAD_DIM, 1)).astype(low)
    sg_ref[...] = shared_grad

    first = route_ref[:, 0, :]
    second = route_ref[:, 1, :]
    is_first = first == expert[0]
    expert_ids = lax.broadcasted_iota(jnp.int32, (EXPERTS, tokens), 0)
    contrasts, shares, leans, picked = [], [], [], []
    for index in range(blocks):
        span = slice(index * tokens, (index + 1) * tokens)
        logits = jnp.transpose(outcome[span, PAIR:])[:EXPERTS]
        contrast = jnp.where(expert_ids == first[index : index + 1], 1.0, 0.0) - jnp.where(
            expert_ids == second[index : index + 1], 1.0, 0.0
        )
        gap = jnp.sum(logits * contrast, axis=0, keepdims=True)
        share_first = jax.nn.sigmoid(gap)
        share_second = jax.nn.sigmoid(-gap)
        mark = is_first[index : index + 1]
        share = jnp.where(mark, share_first, share_second)
        lean = jnp.where(mark, 1.0, -1.0) * share_first * share_second
        selector = chosen_ref[index].astype(wide)
        contrasts.append(contrast)
        shares.append(jnp.sum(selector * share, axis=1, keepdims=True))
        leans.append(jnp.sum(selector * lean, axis=1, keepdims=True))
        picked.append(matmul(chosen_ref[index], x_ref[index]).astype(low))
    picked = jnp.concatenate(picked, axis=0)
    picked_grad = pick_ref[...].astype(wide)
    share_rows = jnp.concatenate(shares, axis=0)
    lean_rows = jnp.concatenate(leans, axis=0)
    xs_ref[...] = picked

    product, gate_slope, up_slope = silu_parts(
        matmul(picked, eg_ref[0]), matmul(picked, eu_ref[0])
    )
    hidden = product.astype(low)
    hid_ref[...] = hidden
    partial_rows = matmul(hidden, ed_ref[0]).astype(low).astype(wide)
    dots = lean_rows * jnp.sum(picked_grad * partial_rows, axis=1, keepdims=True)
    partial_grad = (share_rows * picked_grad).astype(low)
    pg_ref[...] = partial_grad
    give_ref[...] = (share_rows * partial_rows).astype(low)
    hidden_grad = right_contract(partial_grad, ed_ref[0])
    gate_grad = (hidden_grad * gate_slope).astype(low)
    up_grad = (hidden_grad * up_slope).astype(low)
    gg_ref[...] = gate_grad
    ug_ref[...] = up_grad
    row_grad = (
        right_contract(gate_grad, eg_ref[0]) + right_contract(up_grad, eu_ref[0])
    ).astype(low)

    shared_row = right_contract(shared_grad, cat_ref[:, :PAIR])
    for index in range(blocks):
        span = slice(index * tokens, (index + 1) * tokens)
        slots = slice(index * CAP, (index + 1) * CAP)
        selector = chosen_ref[index]
        lean = jnp.sum(selector.astype(wide) * dots[slots], axis=0, keepdims=True)
        logits_grad = lean * contrasts[index]
        logits_high = logits_grad.astype(low)
        logits_low = (logits_grad - logits_high.astype(wide)).astype(low)
        logits_grad = jnp.concatenate([logits_high, logits_low], axis=0)
        lg_ref[index] = logits_grad
        row_ref[index] = (
            shared_row[span]
            + left_contraction(
                jnp.concatenate([selector, logits_grad], axis=0),
                jnp.concatenate([row_grad[slots], rt_ref[...]], axis=0),
            )
        ).astype(low)
    store_out(rows_out, turn, turns, slot)


def rest_body(gate, order, *refs):
    x_pieces, refs = refs[:PIECES], refs[PIECES:]
    c_all, chosen_ref, xs_ref, pg_ref, hid_ref, gg_ref, ug_ref, give_ref = refs[:8]
    (sh_ref, sg_ref, lg_ref, sd_ref), refs = refs[8:12], refs[12:]
    out_pieces, refs = refs[:PIECES], refs[PIECES:]
    deg_ref, deu_ref, ded_ref, dcat_ref, dsd_ref = refs[:5]
    x_bufs, c_bufs, out_bufs, x_sems, c_sems, out_sems = refs[5:]
    turn, turns = pl.program_id(0), pl.num_programs(0)
    streams = [Stream(x_pieces, x_bufs, x_sems, turns), Picked(c_all, order, c_bufs, c_sems)]
    slot = load_ahead(streams, turn, turns)
    outs = [Stream(out_pieces, out_bufs, out_sems, turns)]
    free_slot(outs, turn, slot)
    x_ref, c_ref, out_ref = x_bufs.at[slot], c_bufs.at[slot], out_bufs.at[slot]
    blocks, tokens, width = x_ref.shape

    @pl.when(turn == 0)
    def clear():
        for ref in (deg_ref, deu_ref, ded_ref, dcat_ref, dsd_ref):
            ref[...] = jnp.zeros_like(ref)

    hidden_rows = x_ref[...].reshape(blocks * tokens, width)
    picked = xs_ref[...]
    ded_ref[...] += left_contraction(hid_ref[...], pg_ref[...])
    deg_ref[...] += left_contraction(picked, gg_ref[...])
    deu_ref[...] += left_contraction(picked, ug_ref[...])
    dsd_ref[...] += left_contraction(sh_ref[...], c_ref[...].reshape(blocks * tokens, width))
    dcat_ref[:PAIR] += left_contraction(sg_ref[...], hidden_rows)
    logits = jnp.concatenate([lg_ref[index] for index in range(blocks)], axis=1)
    dcat_ref[PAIR:] += matmul(logits, hidden_rows)
    shared_out = matmul(sh_ref[...], sd_ref[...])
    for index in range(blocks):
        span = slice(index * tokens, (index + 1) * tokens)
        slots = slice(index * CAP, (index + 1) * CAP)
        out_ref[index] = (
            shared_out[span] + left_contraction(chosen_ref[index], give_ref[slots])
        ).astype(low)
    store_out(outs, turn, turns, slot)


def grouped(shape):
    return pl.BlockSpec(shape, lambda i, *rest: (i,) + (0,) * (len(shape) - 1))


def fixed(shape):
    return pl.BlockSpec(
        shape, lambda i, *rest: (0,) * len(shape), pipeline_mode=pl.Buffered(1)
    )


def feed_kernel(body, name, scalars, arrays, in_specs, shapes, out_specs, scratch, flops, moved, turns):
    return pl.pallas_call(
        body,
        out_shape=shapes,
        grid_spec=pltpu.PrefetchScalarGridSpec(
            num_scalar_prefetch=len(scalars),
            grid=(turns,),
            in_specs=in_specs,
            out_specs=out_specs,
            scratch_shapes=scratch,
        ),
        compiler_params=pltpu.CompilerParams(
            dimension_semantics=("arbitrary",), vmem_limit_bytes=60 << 20
        ),
        cost_estimate=pl.CostEstimate(flops=flops, bytes_accessed=moved, transcendentals=0),
        name=name,
    )(*scalars, *arrays)


anywhere = pl.BlockSpec(memory_space=pl.ANY)


def choose_call(expert, order, c_all, route_rows, sd, count, tokens):
    width = c_all.shape[2]
    return feed_kernel(
        choose_body,
        "choose",
        (expert, order),
        (c_all, route_rows, sd),
        [anywhere, grouped((GROUP, 2, tokens)), fixed(sd.shape)],
        (
            jax.ShapeDtypeStruct((count * CAP, width), low),
            jax.ShapeDtypeStruct((count * tokens, PAIR), wide),
            jax.ShapeDtypeStruct((count, CAP, tokens), low),
        ),
        (grouped((GROUP * CAP, width)), grouped((GROUP * tokens, PAIR)), grouped((GROUP, CAP, tokens))),
        [pltpu.VMEM((2, GROUP, tokens, width), low), pltpu.SemaphoreType.DMA((2,))],
        8 * count * tokens * width * PAIR,
        count * tokens * width * 3,
        count // GROUP,
    )


def feed_call(expert, pieces, route_rows, pick, shared, chosen, cat, rt, gate, up, down):
    each, tokens, width = pieces[0].shape
    count, units = PIECES * each, gate.shape[2]
    slots, rows = GROUP * CAP, GROUP * tokens
    parts = jax.ShapeDtypeStruct(pieces[0].shape, low)
    saved = (
        (count * CAP, width), (count * CAP, width), (count * CAP, units), (count * CAP, units),
        (count * CAP, units), (count * CAP, width), (count * tokens, PAIR), (count * tokens, PAIR),
        (count, 2 * EXPERTS, tokens),
    )
    return feed_kernel(
        feed_body,
        "feed",
        (expert,),
        tuple(pieces) + (route_rows, pick, shared, chosen, cat, rt, gate, up, down),
        [anywhere] * PIECES
        + [
            grouped((GROUP, 2, tokens)),
            grouped((slots, width)),
            grouped((rows, PAIR)),
            grouped((GROUP, CAP, tokens)),
            fixed(cat.shape),
            fixed(rt.shape),
            fixed(gate.shape),
            fixed(up.shape),
            fixed(down.shape),
        ],
        (parts,) * PIECES + tuple(jax.ShapeDtypeStruct(shape, low) for shape in saved),
        (anywhere,) * PIECES
        + tuple(grouped((shape[0] * GROUP // count,) + shape[1:]) for shape in saved),
        [pltpu.VMEM((2, GROUP, tokens, width), low)] * 2 + [pltpu.SemaphoreType.DMA((2,))] * 2,
        48 * count * CAP * width * units // 2,
        count * tokens * width * 6,
        count // GROUP,
    )


def rest_call(gate, order, pieces, c_all, chosen, saved, sd, units):
    each, tokens, width = pieces[0].shape
    count = PIECES * each
    parts = jax.ShapeDtypeStruct(pieces[0].shape, low)
    shapes = ((width, units), (width, units), (units, width), (PAIR + 2 * EXPERTS, width), (PAIR, width))
    return feed_kernel(
        rest_body,
        "rest",
        (gate, order),
        tuple(pieces) + (c_all, chosen) + tuple(saved) + (sd,),
        [anywhere] * (PIECES + 1)
        + [grouped((GROUP, CAP, tokens))]
        + [grouped((array.shape[0] * GROUP // count,) + array.shape[1:]) for array in saved]
        + [fixed(sd.shape)],
        (parts,) * PIECES + tuple(jax.ShapeDtypeStruct(shape, wide) for shape in shapes),
        (anywhere,) * PIECES + tuple(fixed(shape) for shape in shapes),
        [pltpu.VMEM((2, GROUP, tokens, width), low)] * 3 + [pltpu.SemaphoreType.DMA((2,))] * 3,
        24 * count * CAP * width * units // 2,
        count * tokens * width * 8,
        count // GROUP,
    )


def shards(
    inputs,
    blocks,
    routes,
    attn_gain,
    w_query,
    w_key,
    w_value,
    w_out,
    ffn_gain,
    w_router,
    shared_gate,
    shared_up,
    shared_down,
    expert_gate,
    expert_up,
    expert_down,
    cotangent,
):
    heads, line = lax.axis_size("head"), lax.axis_size("blk")
    count = heads * line
    head, spot = lax.axis_index("head"), lax.axis_index("blk")
    device = head * line + spot
    tokens, width = inputs.shape
    total = count * tokens
    group = width // heads
    pairs = group // PAIR
    rows = w_query.shape[0]
    steps, short_steps = whole_steps(count), line_steps(line)
    sources = slot_sources(count, steps)
    places = jnp.asarray(np.argsort(sources, axis=1).astype(np.int32))[device]
    slot_sources_own = jnp.asarray(sources)[device]
    short_sources = slot_sources(line, short_steps)
    short_order = jnp.asarray(short_sources)[spot]
    short_places = jnp.asarray(np.argsort(short_sources, axis=1).astype(np.int32))[spot]

    def pad_rows(flat):
        extra = -flat.shape[0] % width
        return jnp.pad(flat, (0, extra)).reshape(-1, width)

    def pad_tall(values):
        return jnp.pad(values, ((0, -values.shape[0] % 16), (0, 0)))

    hop = lambda values, step: permute(values, BOTH, count, step)
    far_steps, cross, chip = steps[:-3], steps[-3:-1], steps[-1]

    own_blocks = jnp.arange(heads, dtype=jnp.int32) * line + spot
    own_slots = places[own_blocks]
    tile = TILE_BLOCKS * tokens
    own_ids = jnp.take(blocks.reshape(count, tokens), own_blocks, axis=0, mode="clip")
    low_id, high_id = own_ids[:, :1], own_ids[:, -1:]

    def counted(test):
        return jnp.sum(test, axis=1, dtype=jnp.int32)

    query_bounds = jnp.stack(
        [
            counted(blocks[None] <= low_id) // tile,
            (counted(blocks[None] <= high_id) + tile - 1) // tile,
        ]
    )
    key_bounds = jnp.stack(
        [
            counted(blocks[None] < low_id) // tile,
            (counted(blocks[None] < high_id) + tile - 1) // tile,
            jnp.full((heads,), total // tile, jnp.int32),
        ]
    )
    id_columns = jnp.tile(own_ids, (1, 2))[:, :, None]
    id_rows = blocks.reshape(count, 1, tokens)

    block_ids = jnp.arange(count, dtype=jnp.int32)
    grad_slots = short_places[block_ids % line] * heads + block_ids // line
    first_steps = weight_steps(line)
    first_places = jnp.asarray(
        np.argsort(slot_sources(line, first_steps), axis=1).astype(np.int32)
    )[spot]
    beside = places[(1 - head) * line + spot]
    expert = (device % EXPERTS).astype(jnp.int32).reshape(1)
    tables = (
        own_slots, query_bounds, key_bounds,
        id_columns, grad_slots, first_places, beside, slot_sources_own, expert,
    )

    halves = lambda matrix: matrix.reshape(rows, heads, group).transpose(1, 0, 2)
    extras = jnp.concatenate(
        [attn_gain, ffn_gain, w_router.reshape(-1), routes.T.reshape(-1).astype(low)]
    )
    extras = jnp.pad(extras, (0, -extras.shape[0] % group)).reshape(-1, group)
    split = [halves(matrix) for matrix in (w_query, w_key, w_value)]
    split = jnp.concatenate(split + [jnp.broadcast_to(extras, (heads,) + extras.shape)], axis=1)
    split = jnp.pad(split, ((0, 0), (0, -split.shape[1] % 16), (0, 0)))
    kept = lax.dynamic_index_in_dim(split, head, 0, False)
    sent = lax.dynamic_index_in_dim(split, 1 - head, 0, False)
    weights = [head_order(head, kept, swap_heads(sent))[None]]
    for step in first_steps[:-1]:
        weights.append(grow(weights[-1], permute(weights[-1], "blk", line, step)))
    weights_far = permute(weights[-1], "blk", line, first_steps[-1])
    held = [inputs[None]]
    shared_slice = shared_gate.shape[1] // count
    shared_pack = jnp.stack(
        [
            shared_gate.reshape(rows, count, shared_slice),
            shared_up.reshape(rows, count, shared_slice),
        ],
        axis=2,
    ).reshape(rows, count * 2 * shared_slice)
    for place, step in enumerate(steps[:-1]):
        start = held[-1]
        if step is cross[1]:
            start, shared_pack = lax.optimization_barrier((start, shared_pack))
        arrived = after(hop(start, step), weights[min(place, len(weights) - 1)])
        if step is cross[0]:
            arrived = after(arrived, *tables[:3])
        if step is cross[1]:
            arrived = after(arrived, *tables[3:])
        held.append(grow(start, arrived))
    shared_in = lax.all_to_all(shared_pack, BOTH, split_axis=1, concat_axis=0, tiled=True)
    inputs_near = held[-1]
    inputs_far = hop(after(inputs_near, shared_in), chip)

    cot_all = after(jnp.concatenate([cotangent, w_out], axis=0), held[len(far_steps) + 1])
    cot_all = lax.all_gather(cot_all, BOTH, axis=0, tiled=False)
    full_out = cot_all[:, tokens:].reshape(width, width)

    query_weight, key_weight = unpack_call(first_places, weights[-1], weights_far, width)
    first_row = 3 * rows
    flat = grow(weights[-1][:, :, first_row:], weights_far[:, :, first_row:])
    flat = flat.reshape(line, heads, -1)
    flat = jnp.take(flat, first_places, axis=0, mode="clip").transpose(1, 0, 2)
    flat = flat.reshape(count, -1)
    gain_first = flat[:, :rows].reshape(width).astype(wide)
    gain_second = flat[:, rows : 2 * rows].reshape(width).astype(wide)
    router = flat[:, 2 * rows : (2 + EXPERTS) * rows].reshape(width, EXPERTS)
    route_rows = flat[:, (2 + EXPERTS) * rows : (2 + EXPERTS) * rows + 2 * tokens]
    route_rows = jnp.take(route_rows, slot_sources_own, axis=0, mode="clip")
    route_rows = route_rows.reshape(count, 2, tokens).astype(jnp.int32)

    keys, token = project_call(inputs_near, gain_first[None], key_weight, 1.0, count, None)
    keys, token = project_call(inputs_far, gain_first[None], key_weight, 1.0, count, keys)
    neighbour = lax.dynamic_index_in_dim(
        inputs_near, beside, 0, False
    )
    pair_inputs = head_order(head, inputs, neighbour).reshape(heads * tokens, width)
    pair_normed = rms_scale(pair_inputs.astype(wide), gain_first).astype(low)
    own_queries = (matmul(pair_normed, query_weight) * scale_factor).astype(low)
    own_queries = own_queries.reshape(heads, tokens, group)

    own_spec = lambda column: pl.BlockSpec(
        (1, tokens, PAIR), lambda p, j, own, *rest: (own[j], 0, column + p)
    )
    all_spec = lambda column: pl.BlockSpec(
        (count, tokens, PAIR), lambda p, j, *rest: (0, 0, column + p)
    )
    half_spec = pl.BlockSpec((count // 2, tokens, PAIR), lambda p, j, *rest: (0, 0, p))
    part_spec = pl.BlockSpec((1, tokens, PAIR), lambda p, j, *rest: (j, 0, p))
    stat_spec = pl.BlockSpec((1, 1, 1, 2 * tokens), lambda p, j, *rest: (p, j, 0, 0))
    column_spec = pl.BlockSpec((1, 2 * tokens, 1), lambda p, j, *rest: (j, 0, 0))
    ids_spec = pl.BlockSpec((count, 1, tokens), lambda p, j, *rest: (0, 0, 0))
    part_shape = jax.ShapeDtypeStruct((heads, tokens, group), low)
    stat_shape = jax.ShapeDtypeStruct((pairs, heads, 1, 2 * tokens), wide)
    grid = (pairs, heads)
    unit = 2 * heads * tokens * total * group

    attended_own, lse = attention_call(
        attend_body,
        "attend",
        (
            after(own_slots, route_rows),
            places,
            query_bounds,
        ),
        (own_queries, keys, keys, id_columns, id_rows),
        [part_spec, all_spec(0), all_spec(pairs), column_spec, ids_spec],
        (part_shape, stat_shape),
        (part_spec, stat_spec),
        grid,
        2 * unit,
        count,
    )
    attended_back = swap_heads(lax.dynamic_index_in_dim(attended_own, 1 - head, 0, False))
    attended_kept = lax.dynamic_index_in_dim(attended_own, head, 0, False)
    attended = jnp.where(
        head == 0,
        jnp.concatenate([attended_kept, attended_back], axis=1),
        jnp.concatenate([attended_back, attended_kept], axis=1),
    )
    inputs_wide = inputs.astype(wide)
    mixed_rows = inputs_wide + matmul(attended, full_out)
    normed_ffn = rms_scale(mixed_rows, gain_second).astype(low)

    half_pad = HEAD_DIM - shared_slice
    shared_pair = jnp.pad(
        shared_in.reshape(width, 2, shared_slice), ((0, 0), (0, 0), (0, half_pad))
    ).reshape(width, PAIR)
    feed_weight = jnp.concatenate(
        [shared_pair, router, jnp.zeros((width, PAIR - EXPERTS), low)], axis=1
    )
    down_pad = jnp.pad(shared_down, ((0, PAIR - shared_slice), (0, 0)))
    router_rows = jnp.transpose(jnp.concatenate([router, router], axis=1))

    near = normed_ffn[None]
    for step in steps[:-2]:
        arrived = hop(near, step)
        if step is steps[1]:
            queries, token = project_call(
                inputs_near, after(gain_first[None], near), query_weight, scale_factor, count, None
            )
            queries, token = project_call(
                inputs_far, gain_first[None], query_weight, scale_factor, count, queries
            )
            arrived = after(arrived, queries)
        near = grow(near, arrived)
    near_far = hop(near, chip)
    pick, shared_grad, chosen = choose_call(
        after(expert, near), slot_sources_own, cot_all, route_rows, down_pad, count, tokens
    )
    crossed = after(hop(near, cross[1]), chosen, feed_weight, near_far)
    pieces = [near, crossed, near_far, hop(crossed, chip)]
    near_low, near_high, far_low, far_high, *saved = feed_call(
        expert, pieces, route_rows, pick, shared_grad, chosen, feed_weight, router_rows,
        expert_gate, expert_up, expert_down,
    )
    row_upper = (near_high.astype(wide) + hop(far_high, chip).astype(wide)).astype(low)
    terms = [near_low, hop(after(far_low, row_upper), chip)]
    (
        out_low, out_high, out_far_low, out_far_high,
        grad_egate, grad_eup, grad_edown, grad_feed, grad_sdown,
    ) = rest_call(
        after(expert, row_upper), slot_sources_own, pieces, cot_all, chosen, saved, down_pad,
        expert_gate.shape[2],
    )
    terms = terms + [after(hop(row_upper, cross[1]), out_low)]
    out_far_high, terms[-1] = lax.optimization_barrier((out_far_high, terms[-1]))
    out_upper = (out_high.astype(wide) + hop(out_far_high, chip).astype(wide)).astype(low)
    out_terms = [out_low, hop(after(out_far_low, out_upper), chip)]
    grad_sdown = grad_sdown[:shared_slice]
    terms = scatter_step(terms, BOTH, count, cross[0])
    terms[-1], out_upper = lax.optimization_barrier((terms[-1], out_upper))
    out_arrived = hop(out_upper, cross[1])
    grad_shared, terms[-1] = lax.optimization_barrier((grad_feed[:PAIR], terms[-1]))
    grad_shared = grad_shared.reshape(2, HEAD_DIM, width)[:, :shared_slice].reshape(-1, width)
    grad_shared = jnp.transpose(grad_shared).astype(low)
    grad_shared_back = lax.all_to_all(grad_shared, BOTH, split_axis=0, concat_axis=1, tiled=True)
    for step in reversed(far_steps):
        terms = scatter_step(terms, BOTH, count, step)
    normed_ffn_grad = finish(terms)
    grad_router = jnp.transpose(
        grad_feed[PAIR : PAIR + EXPERTS] + grad_feed[PAIR + EXPERTS : PAIR + 2 * EXPERTS]
    )

    unused_second, second_pull = jax.vjp(rms_scale, mixed_rows, gain_second)
    mixed_part, grad_gain_ffn = second_pull(normed_ffn_grad)
    mixed_grad = cotangent.astype(wide) + mixed_part
    mixed_low = after(mixed_grad.astype(low), out_arrived, grad_shared_back)
    mixed_pair = head_order(head, mixed_low, swap_heads(mixed_low)).reshape(heads * tokens, width)
    own_out = lax.dynamic_slice_in_dim(full_out, head * group, group, 0)
    attended_grad = right_contract(mixed_pair, own_out).astype(low)
    attended_flat = attended_own.reshape(heads * tokens, group)
    head_marks = (
        jnp.arange(group)[None] // HEAD_DIM == jnp.arange(2 * pairs)[:, None]
    ).astype(wide)
    delta = lax.dot_general(
        head_marks,
        attended_grad.astype(wide) * attended_flat.astype(wide),
        (((1,), (1,)), ((), ())),
        precision=lax.Precision.HIGHEST,
    )
    delta = (
        delta.reshape(pairs, 2, heads, tokens)
        .transpose(0, 2, 1, 3)
        .reshape(pairs, heads, 1, 2 * tokens)
    )
    stats = jnp.stack([lse, delta]).transpose(2, 0, 1, 3, 4).reshape(heads, -1)
    stats_rows = jnp.concatenate(two_parts(stats), axis=1).reshape(heads, -1, group)
    grad_parts = attended_grad.reshape(heads, tokens, group)
    grads = [jnp.concatenate([grad_parts, stats_rows], axis=1)[None]]
    def next_out(terms, arrived, gate):
        terms = terms + [arrived]
        sent = upper(terms)
        gate, sent = lax.optimization_barrier((gate, sent))
        return lower(terms), sent, gate

    columns = two_parts(jnp.concatenate([grad_gain_ffn[:, None], grad_router], axis=1))
    extra = columns[0].shape[1]
    columns = jnp.concatenate(columns, axis=1)
    columns = jnp.pad(columns, ((0, 0), (1, PAIR - 1 - 2 * extra)))
    out_terms, sent, grads[0] = next_out(out_terms, out_arrived, grads[0])
    out_arrived = hop(sent, cross[0])
    tail = list(reversed(far_steps))
    for place, step in enumerate(short_steps[:-1]):
        if place == 1:
            grads[-1] = after(grads[-1], out_arrived, columns)
        if place == len(short_steps) - 2:
            out_terms, sent, grads[-1] = next_out(out_terms, out_arrived, grads[-1])
            out_arrived = hop(sent, tail[0])
        grads.append(grow(grads[-1], permute(grads[-1], "blk", line, step)))
    query_q = after(own_slots, grads[-2])
    query_grad = attention_call(
        query_body,
        "query_gradient",
        (query_q, places, query_bounds),
        (own_queries, keys, keys, grad_parts, lse, delta, id_columns, id_rows),
        [
            part_spec,
            all_spec(0),
            all_spec(pairs),
            part_spec,
            stat_spec,
            stat_spec,
            column_spec,
            ids_spec,
        ],
        part_shape,
        part_spec,
        grid,
        3 * unit,
        count,
    )
    start = after(grads[-1], query_grad)
    out_terms, sent, start = next_out(out_terms, out_arrived, start)
    for step in tail[1:-1]:
        out_terms, sent, start = next_out(out_terms, hop(sent, step), start)
    out_arrived = hop(sent, tail[-1])
    grads.append(permute(start, "blk", line, short_steps[-1]))
    grad_halves = [part.reshape(count // 2, -1, group) for part in (start, grads[-1])]

    def stat_part(part):
        part = part[:, tokens:].reshape(count // 2, 2, -1).astype(wide)
        return (part[:, 0] + part[:, 1]).reshape(-1, 1, 2 * tokens)

    stats_all = jnp.concatenate([stat_part(part) for part in grad_halves])
    key_grad, value_grad = attention_call(
        key_body,
        "key_gradient",
        (own_slots, places, grad_slots, key_bounds),
        (keys, keys, queries, *grad_halves, stats_all, id_columns, id_rows),
        [
            own_spec(0),
            own_spec(pairs),
            all_spec(0),
            half_spec,
            half_spec,
            pl.BlockSpec(stats_all.shape, lambda p, j, *rest: (0, 0, 0)),
            column_spec,
            ids_spec,
        ],
        (part_shape, part_shape),
        (part_spec, part_spec),
        grid,
        4 * unit,
        count,
    )

    near, far, normed_part = weights_call(
        short_places, pair_inputs, gain_first[None], query_grad, key_grad, value_grad,
        query_weight, key_weight, columns, attended_flat, mixed_pair, line,
    )
    backward = list(reversed(short_steps))
    sums = [near, permute(far, "blk", line, backward[0])]
    out_terms.append(out_arrived)
    for place, step in enumerate(backward[1:]):
        sums = scatter_step(sums, "blk", line, step)
        if place == 0:
            first_sum = sums[-1]
            sums[-1] = after(sums[-1], out_arrived)
    output = (mixed_rows + finish(out_terms)).astype(low)
    sums = [sums]
    summed = finish(sums[0])
    grad_wout_own = summed[:, :, 3 * group + PAIR :].transpose(1, 0, 2).reshape(rows, width)
    summed = summed[:, :, : 3 * group + PAIR]
    summed_back = swap_heads(
        lax.dynamic_index_in_dim(summed, 1 - head, 0, False).astype(low)
    ).astype(wide)
    summed_kept = lax.dynamic_index_in_dim(summed, head, 0, False)
    joined = head_order(head, summed_kept, summed_back)
    small = jnp.sum(joined[:, :, 3 * group :], axis=0)
    gain_column = small[:, 0] + small[:, PAIR - 1]
    small = small[:, 1 : extra + 1] + small[:, extra + 1 : 2 * extra + 1]
    joined = joined[:, :, : 3 * group].reshape(heads, rows, 3, group)
    joined = joined.transpose(2, 1, 0, 3).reshape(3, rows, width)

    normed_parts = normed_part.reshape(heads, tokens, width)
    arrived = swap_heads(lax.dynamic_index_in_dim(normed_parts, 1 - head, 0, False).astype(low))
    normed_grad = lax.dynamic_index_in_dim(normed_parts, head, 0, False) + arrived.astype(wide)
    unused_first, first_pull = jax.vjp(lambda rows_in: rms_scale(rows_in, gain_first), inputs_wide)
    grad_inputs = mixed_grad + first_pull(after(normed_grad, first_sum))[0]
    grad_shared_back = after(grad_shared_back, first_sum).reshape(rows, count, 2, shared_slice)
    grad_sgate = grad_shared_back[:, :, 0].reshape(rows, -1).astype(wide)
    grad_sup = grad_shared_back[:, :, 1].reshape(rows, -1).astype(wide)

    return (
        output,
        grad_inputs,
        gain_column,
        joined[0].astype(wide),
        joined[1].astype(wide),
        joined[2].astype(wide),
        grad_wout_own,
        small[:, 0],
        small[:, 1:],
        grad_sgate,
        grad_sup,
        grad_sdown,
        grad_egate[None],
        grad_eup[None],
        grad_edown[None],
    )


def solution(mesh):
    both = P(BOTH)
    rows = P(BOTH, None)
    slabs = P(BOTH, None, None)
    return jax.shard_map(
        shards,
        mesh=mesh,
        in_specs=(
            rows, P(), rows, both, rows, rows, rows, rows, both, rows, rows, rows, rows,
            slabs, slabs, slabs, rows,
        ),
        out_specs=(
            rows, rows, both, rows, rows, rows, rows, both, rows, rows, rows, rows,
            slabs, slabs, slabs,
        ),
        check_vma=False,
    )
```

```python
import functools

import jax
import jax.numpy as jnp
import numpy as np
from jax import lax
from jax.experimental import pallas as pl
from jax.experimental.pallas import tpu as pltpu
from jax.sharding import PartitionSpec as P

HEAD_DIM = 64
EXPERTS = 16
CAP = 32
PAIR = 2 * HEAD_DIM
TILE_BLOCKS = 8
BOTH = ("head", "blk")

epsilon = 1e-05
scale_factor = 0.125
masked_value = -1e30
low = jnp.bfloat16
wide = jnp.float32


def matmul(left_side, right_side):
    return jnp.dot(left_side, right_side, preferred_element_type=wide)


def left_contraction(left_side, right_side):
    return lax.dot_general(
        left_side, right_side, (((0,), (0,)), ((), ())), preferred_element_type=wide
    )


def right_contract(left_side, right_side):
    return lax.dot_general(
        left_side, right_side, (((1,), (1,)), ((), ())), preferred_element_type=wide
    )


def rms_scale(values, gain_row):
    return (
        values * lax.rsqrt(jnp.mean(values * values, axis=-1, keepdims=True) + epsilon) * gain_row
    )


def silu_parts(gate_pre, up_pre):
    gate = jax.nn.sigmoid(gate_pre)
    swish = gate_pre * gate
    return swish * up_pre, gate * (1.0 + gate_pre * (1.0 - gate)) * up_pre, swish


def whole_steps(count):
    bits = count.bit_length() - 1
    steps = [functools.partial(flip, bit, bit) for bit in range(bits - 2, 1, -1)]
    return steps + [
        functools.partial(flip, 1, bits - 1),
        functools.partial(flip, bits - 1, 1),
        functools.partial(flip, 0, 0),
    ]


def flip(even_bit, odd_bit, index):
    return index ^ (1 << (odd_bit if index & 1 else even_bit))


def line_steps(count):
    bits = count.bit_length() - 1
    return [functools.partial(flip, bit, bit) for bit in range(bits - 1, -1, -1)]


def weight_steps(count):
    steps = line_steps(count)
    return [steps[-2]] + steps[:-2] + [steps[-1]]


def slot_sources(count, steps):
    order = [[i] for i in range(count)]
    for step in steps:
        order = [order[i] + order[step(i)] for i in range(count)]
    return np.array(order, np.int32)


def permute(values, axis, count, step):
    return lax.ppermute(values, axis, [(i, step(i)) for i in range(count)])


def after(value, *needed):
    return lax.optimization_barrier((value,) + needed)[0]


def two_parts(values):
    high = lax.reduce_precision(values, 8, 7)
    return [high.astype(low), (values - high).astype(low)]


def grow(held, arrived):
    return jnp.concatenate([held, arrived], axis=0)


def gather(values, axis, count, steps):
    held = values[None]
    for step in steps:
        held = grow(held, permute(held, axis, count, step))
    return held


def upper(terms):
    half = terms[0].shape[0] // 2
    return sum(term[half:].astype(wide) for term in terms).astype(low)


def lower(terms):
    half = terms[0].shape[0] // 2
    return [term[:half] for term in terms]


def scatter_step(terms, axis, count, step):
    return lower(terms) + [permute(upper(terms), axis, count, step)]


def finish(terms):
    return sum(term[0].astype(wide) for term in terms)


def scatter_sum(slots, axis, count, steps):
    terms = [slots]
    for step in reversed(steps):
        terms = scatter_step(terms, axis, count, step)
    return finish(terms)


def swap_heads(values):
    return lax.ppermute(values, "head", [(0, 1), (1, 0)])


def head_order(head, own, other):
    return jnp.where(head == 0, jnp.stack([own, other]), jnp.stack([other, own]))


def stack_heads(rows):
    first = lax.broadcasted_iota(jnp.int32, rows.shape, 1) < HEAD_DIM
    zero = jnp.zeros_like(rows)
    return jnp.concatenate([jnp.where(first, rows, zero), jnp.where(first, zero, rows)], axis=0)


def join_heads(stacked):
    half = stacked.shape[0] // 2
    top = stacked[:half]
    first = lax.broadcasted_iota(jnp.int32, top.shape, 1) < HEAD_DIM
    return jnp.where(first, top, stacked[half:])


def load_tile(ref, slots, index):
    return jnp.concatenate(
        [ref[slots[index * TILE_BLOCKS + part]] for part in range(TILE_BLOCKS)], axis=0
    )


def load_ids(ref, index):
    return jnp.concatenate(
        [ref[index * TILE_BLOCKS + part] for part in range(TILE_BLOCKS)], axis=1
    )


def as_column(row):
    return jnp.transpose(jnp.broadcast_to(row, (PAIR, row.shape[1])))[:, :1]


def attend_body(own, slots, bounds, q_ref, k_ref, v_ref, qid_ref, kid_ref, out_ref, lse_ref):
    part = pl.program_id(1)
    stacked = stack_heads(q_ref[0])
    rows = stacked.shape[0]

    def step(masked, index, state):
        top, total, weighted = state
        scores = right_contract(stacked, load_tile(k_ref, slots, index))
        if masked:
            scores = jnp.where(load_ids(kid_ref, index) <= qid_ref[0], scores, masked_value)
        new_top = jnp.maximum(top, jnp.max(scores, axis=-1, keepdims=True))
        weights = jnp.exp(scores - new_top)
        rescale = jnp.exp(top - new_top)
        total = total * rescale + jnp.sum(weights, axis=-1, keepdims=True)
        weighted = weighted * rescale + matmul(weights.astype(low), load_tile(v_ref, slots, index))
        return new_top, total, weighted

    state = (
        jnp.full((rows, 1), masked_value, wide),
        jnp.zeros((rows, 1), wide),
        jnp.zeros((rows, PAIR), wide),
    )
    state = lax.fori_loop(0, bounds[0, part], functools.partial(step, False), state)
    top, total, weighted = lax.fori_loop(
        bounds[0, part], bounds[1, part], functools.partial(step, True), state
    )
    out_ref[0] = join_heads(weighted / total).astype(low)
    lse = jnp.broadcast_to(top + jnp.log(total), (rows, PAIR))
    lse_ref[0, 0] = jnp.transpose(lse)[:1]


def query_body(
    own, slots, bounds, q_ref, k_ref, v_ref, g_ref, lse_ref, delta_ref, qid_ref, kid_ref, dq_ref
):
    part = pl.program_id(1)
    stacked = stack_heads(q_ref[0])
    grads = stack_heads(g_ref[0])
    lse = as_column(lse_ref[0, 0])
    delta = as_column(delta_ref[0, 0])

    def step(masked, index, total):
        keys = load_tile(k_ref, slots, index)
        probs = jnp.exp(right_contract(stacked, keys) - lse)
        if masked:
            probs = jnp.where(load_ids(kid_ref, index) <= qid_ref[0], probs, 0.0)
        moved = right_contract(grads, load_tile(v_ref, slots, index)) - delta
        return total + matmul((probs * moved).astype(low), keys)

    total = jnp.zeros((stacked.shape[0], PAIR), wide)
    total = lax.fori_loop(0, bounds[0, part], functools.partial(step, False), total)
    total = lax.fori_loop(
        bounds[0, part], bounds[1, part], functools.partial(step, True), total
    )
    dq_ref[0] = (join_heads(total) * scale_factor).astype(low)


def key_body(
    own, slots, gslots, bounds, k_ref, v_ref, q_ref, g_near, g_far, stat_ref, kid_ref, qid_ref,
    dk_ref, dv_ref,
):
    pair = pl.program_id(0)
    part = pl.program_id(1)
    pairs = pl.num_programs(0)
    keys = stack_heads(k_ref[0])
    values = stack_heads(v_ref[0])
    rows = keys.shape[0]
    half = g_near.shape[0]

    def stat_rows(index, which):
        tops, bottoms = [], []
        for piece in range(TILE_BLOCKS):
            slot = gslots[index * TILE_BLOCKS + piece]
            place = slot * (2 * pairs) + which * pairs + pair
            row = stat_ref[place]
            tops.append(row[:, :PAIR])
            bottoms.append(row[:, PAIR:])
        shape = (rows // 2, TILE_BLOCKS * PAIR)
        return jnp.concatenate(
            [
                jnp.broadcast_to(jnp.concatenate(tops, axis=1), shape),
                jnp.broadcast_to(jnp.concatenate(bottoms, axis=1), shape),
            ],
            axis=0,
        )

    def step(masked, index, state):
        dk_total, dv_total = state
        queries = load_tile(q_ref, slots, index)
        grads = []
        for piece in range(TILE_BLOCKS):
            slot = gslots[index * TILE_BLOCKS + piece]
            near = g_near[jnp.minimum(slot, half - 1)]
            grads.append(jnp.where(slot < half, near, g_far[jnp.maximum(slot - half, 0)]))
        grads = jnp.concatenate(grads, axis=0)
        probs = jnp.exp(right_contract(keys, queries) - stat_rows(index, 0))
        if masked:
            probs = jnp.where(kid_ref[0] <= load_ids(qid_ref, index), probs, 0.0)
        moved = right_contract(values, grads) - stat_rows(index, 1)
        dk_total = dk_total + matmul((probs * moved).astype(low), queries)
        dv_total = dv_total + matmul(probs.astype(low), grads)
        return dk_total, dv_total

    state = (jnp.zeros((rows, PAIR), wide), jnp.zeros((rows, PAIR), wide))
    state = lax.fori_loop(
        bounds[0, part], bounds[1, part], functools.partial(step, True), state
    )
    dk_total, dv_total = lax.fori_loop(
        bounds[1, part], bounds[2, part], functools.partial(step, False), state
    )
    dk_ref[0] = join_heads(dk_total).astype(low)
    dv_ref[0] = join_heads(dv_total).astype(low)


def attention_call(body, name, tables, arrays, specs, outs, out_specs, grid, cost, count):
    return pl.pallas_call(
        body,
        out_shape=outs,
        grid_spec=pltpu.PrefetchScalarGridSpec(
            num_scalar_prefetch=len(tables), grid=grid, in_specs=specs, out_specs=out_specs
        ),
        compiler_params=pltpu.CompilerParams(
            dimension_semantics=("arbitrary", "arbitrary"),
            vmem_limit_bytes=60 << 20,
        ),
        cost_estimate=pl.CostEstimate(
            flops=8 * cost, bytes_accessed=cost // 512, transcendentals=cost // 512
        ),
        name=name,
    )(*tables, *arrays)


def unpack_body(slots, near_ref, far_ref, query_ref, key_ref):
    half, heads, unused, group = near_ref.shape
    line = 2 * half
    rows = query_ref.shape[0] // (heads * line)
    for spot in range(line):
        slot = slots[spot]
        is_near = slot < half
        low_slot, high_slot = jnp.minimum(slot, half - 1), jnp.maximum(slot - half, 0)
        for source in range(heads):
            block = jnp.where(is_near, near_ref[low_slot, source], far_ref[high_slot, source])
            first = (source * line + spot) * rows
            query_ref[first : first + rows] = block[:rows]
            for part in range(2):
                key_ref[first : first + rows, part * group : (part + 1) * group] = block[
                    (part + 1) * rows : (part + 2) * rows
                ]


def unpack_call(slots, near, far, width):
    half, heads, unused, group = near.shape
    whole = lambda shape: pl.BlockSpec(shape, lambda i, *rest: (0,) * len(shape))
    shapes = ((width, group), (width, 2 * group))
    return pl.pallas_call(
        unpack_body,
        out_shape=tuple(jax.ShapeDtypeStruct(shape, low) for shape in shapes),
        grid_spec=pltpu.PrefetchScalarGridSpec(
            num_scalar_prefetch=1,
            grid=(1,),
            in_specs=[whole(near.shape), whole(far.shape)],
            out_specs=tuple(whole(shape) for shape in shapes),
        ),
        compiler_params=pltpu.CompilerParams(
            dimension_semantics=("arbitrary",), vmem_limit_bytes=32 << 20
        ),
        cost_estimate=pl.CostEstimate(
            flops=0, bytes_accessed=8 * near.size, transcendentals=0
        ),
        name="unpack",
    )(slots, near, far)


PROJECT = 4


def project_body(scale, x_ref, gain_ref, weight_ref, *refs):
    out_ref, token_ref = refs[-2:]
    token_ref[...] = jnp.zeros_like(token_ref)
    blocks, tokens, width = x_ref.shape
    rows = x_ref[...].reshape(blocks * tokens, width).astype(wide)
    normed = rms_scale(rows, gain_ref[...]).astype(low)
    out = matmul(normed, weight_ref[...]) * scale
    out_ref[...] = out.astype(low).reshape(blocks, tokens, -1)


def project_call(rows, gain, weight, scale, count, before):
    blocks, tokens, width = rows.shape
    columns = weight.shape[1]
    skip = 0 if before is None else (count - blocks) // PROJECT
    flat = lambda array: pl.BlockSpec(array.shape, lambda i: (0, 0))
    more = [] if before is None else [before]
    return pl.pallas_call(
        functools.partial(project_body, scale),
        out_shape=(
            jax.ShapeDtypeStruct((count, tokens, columns), low),
            jax.ShapeDtypeStruct((8, PAIR), wide),
        ),
        grid=(blocks // PROJECT,),
        in_specs=[
            pl.BlockSpec((PROJECT, tokens, width), lambda i: (i, 0, 0)),
            flat(gain),
            flat(weight),
        ]
        + [pl.BlockSpec(memory_space=pl.ANY)] * len(more),
        out_specs=(
            pl.BlockSpec((PROJECT, tokens, columns), lambda i: (i + skip, 0, 0)),
            pl.BlockSpec((8, PAIR), lambda i: (0, 0)),
        ),
        input_output_aliases={3: 0} if more else {},
        compiler_params=pltpu.CompilerParams(
            dimension_semantics=("arbitrary",), vmem_limit_bytes=60 << 20
        ),
        cost_estimate=pl.CostEstimate(
            flops=4 * blocks * tokens * width * columns,
            bytes_accessed=2 * blocks * tokens * (width + columns),
            transcendentals=0,
        ),
        name="project",
    )(rows, gain, weight, *more)


def weights_body(
    slots, x_ref, gain_ref, dq_ref, dk_ref, dv_ref, query_ref, key_ref, columns_ref, attended_ref, mixed_ref,
    near_ref, far_ref, part_ref,
):
    half, heads, rows, unused = near_ref.shape
    group = dq_ref.shape[1]
    unit = rms_scale(x_ref[...].astype(wide), 1.0)
    normed = (unit * gain_ref[...]).astype(low)
    grads = (dq_ref[...], dk_ref[...], dv_ref[...])
    part = (
        right_contract(grads[0], query_ref[...])
        + right_contract(grads[1], key_ref[:, :group])
        + right_contract(grads[2], key_ref[:, group:])
    )
    part_ref[...] = part
    gain = jnp.sum(part * unit, axis=0, keepdims=True)
    gain = jnp.transpose(jnp.broadcast_to(gain, (PAIR, gain.shape[1])))
    gain_high = gain.astype(low)
    gain_low = (gain - gain_high.astype(wide)).astype(low)
    lane = lax.broadcasted_iota(jnp.int32, gain.shape, 1)
    columns = jnp.where(lane == 0, gain_high, columns_ref[...])
    columns = jnp.where(lane == PAIR - 1, gain_low, columns)
    pieces = [left_contraction(normed, grad).astype(low) for grad in grads] + [columns]
    wout = left_contraction(attended_ref[...], mixed_ref[...]).astype(low)
    starts = [0, group, 2 * group, 3 * group]
    for spot in range(2 * half):
        slot = slots[spot]

        def give(ref, at, spot=spot):
            for source in range(heads):
                first = (source * 2 * half + spot) * rows
                for start, piece in zip(starts, pieces):
                    ref[at, source, :, start : start + piece.shape[1]] = piece[first : first + rows]
                ref[at, source, :, 3 * group + PAIR :] = wout[
                    spot * rows : (spot + 1) * rows, source * group : (source + 1) * group
                ]

        @pl.when(slot < half)
        def to_near():
            give(near_ref, slot)

        @pl.when(slot >= half)
        def to_far():
            give(far_ref, slot - half)


def weights_call(slots, inputs, gain, dq, dk, dv, query_weight, key_weight, columns, attended, mixed, line):
    heads, tokens, group = dq.shape
    width = inputs.shape[1]
    rows = width // (heads * line)
    flat = lambda array: array.reshape(heads * tokens, group)
    arrays = (inputs, gain, flat(dq), flat(dk), flat(dv), query_weight, key_weight, columns, attended, mixed)
    whole = lambda shape: pl.BlockSpec(shape, lambda i, *rest: (0,) * len(shape))
    parts = (line // 2, heads, rows, 4 * group + PAIR)
    return pl.pallas_call(
        weights_body,
        out_shape=(
            jax.ShapeDtypeStruct(parts, low),
            jax.ShapeDtypeStruct(parts, low),
            jax.ShapeDtypeStruct(inputs.shape, wide),
        ),
        grid_spec=pltpu.PrefetchScalarGridSpec(
            num_scalar_prefetch=1,
            grid=(1,),
            in_specs=[whole(array.shape) for array in arrays],
            out_specs=(whole(parts), whole(parts), whole(inputs.shape)),
        ),
        compiler_params=pltpu.CompilerParams(
            dimension_semantics=("arbitrary",), vmem_limit_bytes=60 << 20
        ),
        cost_estimate=pl.CostEstimate(
            flops=20 * heads * tokens * width * group, bytes_accessed=8 << 20, transcendentals=0
        ),
        name="weight_gradients",
    )(slots, *arrays)


GROUP = 8


class Stream:
    def __init__(self, pieces, buffers, semaphores, turns):
        self.pieces, self.buffers, self.semaphores = pieces, buffers, semaphores
        self.each, self.blocks = turns // len(pieces), buffers.shape[1]

    def load(self, index, place):
        self.begin(index, place, lambda part, buffer: (part, buffer))

    def store(self, index, place):
        self.begin(index, place, lambda part, buffer: (buffer, part))

    def begin(self, index, place, ends):
        for number, piece in enumerate(self.pieces):

            @pl.when(index // self.each == number)
            def start(piece=piece):
                part = piece.at[pl.ds(index % self.each * self.blocks, self.blocks)]
                source, target = ends(part, self.buffers.at[place])
                pltpu.make_async_copy(source, target, self.semaphores.at[place]).start()

    def loaded(self, place):
        pltpu.make_async_copy(
            self.pieces[0].at[pl.ds(0, self.blocks)],
            self.buffers.at[place],
            self.semaphores.at[place],
        ).wait()

    def stored(self, place):
        pltpu.make_async_copy(
            self.buffers.at[place],
            self.pieces[0].at[pl.ds(0, self.blocks)],
            self.semaphores.at[place],
        ).wait()


class Picked:
    def __init__(self, source, order, buffers, semaphores):
        self.source, self.order, self.buffers, self.semaphores = source, order, buffers, semaphores
        self.blocks, self.rows = buffers.shape[1:3]

    def load(self, index, place):
        for part in range(self.blocks):
            block = self.source.at[self.order[index * self.blocks + part], pl.ds(0, self.rows)]
            pltpu.make_async_copy(
                block, self.buffers.at[place, part], self.semaphores.at[place]
            ).start()

    def loaded(self, place):
        pltpu.make_async_copy(
            self.source.at[pl.ds(0, self.blocks), pl.ds(0, self.rows)],
            self.buffers.at[place],
            self.semaphores.at[place],
        ).wait()


PIECES = 4


def load_ahead(streams, turn, turns):
    slot = turn % 2

    @pl.when(turn == 0)
    def first():
        for stream in streams:
            stream.load(turn, slot)

    @pl.when(turn + 1 < turns)
    def ahead():
        for stream in streams:
            stream.load(turn + 1, 1 - slot)

    for stream in streams:
        stream.loaded(slot)
    return slot


def free_slot(streams, turn, slot):
    @pl.when(turn >= 2)
    def free():
        for stream in streams:
            stream.stored(slot)


def store_out(streams, turn, turns, slot):
    for stream in streams:
        stream.store(turn, slot)

    @pl.when(turn == turns - 1)
    def drain():
        for place in range(2):
            for stream in streams:
                stream.stored(place)


def choose_body(
    expert, order, c_all, route_ref, sd_ref, pick_ref, hidden_ref, chosen_ref, c_bufs, c_sems
):
    turn, turns = pl.program_id(0), pl.num_programs(0)
    slot = load_ahead([Picked(c_all, order, c_bufs, c_sems)], turn, turns)
    c_ref = c_bufs.at[slot]
    blocks, tokens, width = c_ref.shape
    hidden_ref[...] = right_contract(c_ref[...].reshape(blocks * tokens, width), sd_ref[...])
    routed = (route_ref[:, 0, :] == expert[0]) | (route_ref[:, 1, :] == expert[0])
    before = (
        lax.broadcasted_iota(jnp.int32, (tokens, tokens), 0)
        < lax.broadcasted_iota(jnp.int32, (tokens, tokens), 1)
    )
    rank = matmul(
        jnp.where(routed, 1.0, 0.0).astype(low), jnp.where(before, 1.0, 0.0).astype(low)
    )
    rank = jnp.where(routed, rank, -1.0)
    slot_ids = lax.broadcasted_iota(jnp.int32, (CAP, tokens), 0).astype(wide)
    for index in range(blocks):
        selector = jnp.where(rank[index : index + 1] == slot_ids, 1.0, 0.0).astype(low)
        chosen_ref[index] = selector
        pick_ref[index * CAP : (index + 1) * CAP] = matmul(selector, c_ref[index]).astype(low)


def feed_body(expert, *refs):
    x_pieces, refs = refs[:PIECES], refs[PIECES:]
    (route_ref, pick_ref, shared_ref, chosen_ref, cat_ref, rt_ref, eg_ref, eu_ref, ed_ref), refs = (
        refs[:9], refs[9:]
    )
    row_pieces, refs = refs[:PIECES], refs[PIECES:]
    (xs_ref, pg_ref, hid_ref, gg_ref, ug_ref, give_ref, sh_ref, sg_ref, lg_ref), refs = (
        refs[:9], refs[9:]
    )
    x_bufs, row_bufs, x_sems, row_sems = refs
    turn, turns = pl.program_id(0), pl.num_programs(0)
    slot = load_ahead([Stream(x_pieces, x_bufs, x_sems, turns)], turn, turns)
    rows_out = [Stream(row_pieces, row_bufs, row_sems, turns)]
    free_slot(rows_out, turn, slot)
    x_ref, row_ref = x_bufs.at[slot], row_bufs.at[slot]
    blocks, tokens, width = x_ref.shape
    count = blocks * tokens

    outcome = matmul(x_ref[...].reshape(count, width), cat_ref[...])
    pre = outcome[:, :PAIR]
    inside = lax.broadcasted_iota(jnp.int32, pre.shape, 1) < HEAD_DIM
    product, gate_slope, up_slope = silu_parts(pre, pltpu.roll(pre, HEAD_DIM, 1))
    sh_ref[...] = jnp.where(inside, product, 0.0).astype(low)
    shared_hidden_grad = shared_ref[...]
    gate_side = jnp.where(inside, shared_hidden_grad * gate_slope, 0.0)
    up_side = jnp.where(inside, shared_hidden_grad * up_slope, 0.0)
    shared_grad = (gate_side + pltpu.roll(up_side, HEAD_DIM, 1)).astype(low)
    sg_ref[...] = shared_grad

    first = route_ref[:, 0, :]
    second = route_ref[:, 1, :]
    is_first = first == expert[0]
    expert_ids = lax.broadcasted_iota(jnp.int32, (EXPERTS, tokens), 0)
    contrasts, shares, leans, picked = [], [], [], []
    for index in range(blocks):
        span = slice(index * tokens, (index + 1) * tokens)
        logits = jnp.transpose(outcome[span, PAIR:])[:EXPERTS]
        contrast = jnp.where(expert_ids == first[index : index + 1], 1.0, 0.0) - jnp.where(
            expert_ids == second[index : index + 1], 1.0, 0.0
        )
        gap = jnp.sum(logits * contrast, axis=0, keepdims=True)
        share_first = jax.nn.sigmoid(gap)
        share_second = jax.nn.sigmoid(-gap)
        mark = is_first[index : index + 1]
        share = jnp.where(mark, share_first, share_second)
        lean = jnp.where(mark, 1.0, -1.0) * share_first * share_second
        selector = chosen_ref[index].astype(wide)
        contrasts.append(contrast)
        shares.append(jnp.sum(selector * share, axis=1, keepdims=True))
        leans.append(jnp.sum(selector * lean, axis=1, keepdims=True))
        picked.append(matmul(chosen_ref[index], x_ref[index]).astype(low))
    picked = jnp.concatenate(picked, axis=0)
    picked_grad = pick_ref[...].astype(wide)
    share_rows = jnp.concatenate(shares, axis=0)
    lean_rows = jnp.concatenate(leans, axis=0)
    xs_ref[...] = picked

    product, gate_slope, up_slope = silu_parts(
        matmul(picked, eg_ref[0]), matmul(picked, eu_ref[0])
    )
    hidden = product.astype(low)
    hid_ref[...] = hidden
    partial_rows = matmul(hidden, ed_ref[0]).astype(low).astype(wide)
    dots = lean_rows * jnp.sum(picked_grad * partial_rows, axis=1, keepdims=True)
    partial_grad = (share_rows * picked_grad).astype(low)
    pg_ref[...] = partial_grad
    give_ref[...] = (share_rows * partial_rows).astype(low)
    hidden_grad = right_contract(partial_grad, ed_ref[0])
    gate_grad = (hidden_grad * gate_slope).astype(low)
    up_grad = (hidden_grad * up_slope).astype(low)
    gg_ref[...] = gate_grad
    ug_ref[...] = up_grad
    row_grad = (
        right_contract(gate_grad, eg_ref[0]) + right_contract(up_grad, eu_ref[0])
    ).astype(low)

    shared_row = right_contract(shared_grad, cat_ref[:, :PAIR])
    for index in range(blocks):
        span = slice(index * tokens, (index + 1) * tokens)
        slots = slice(index * CAP, (index + 1) * CAP)
        selector = chosen_ref[index]
        lean = jnp.sum(selector.astype(wide) * dots[slots], axis=0, keepdims=True)
        logits_grad = lean * contrasts[index]
        logits_high = logits_grad.astype(low)
        logits_low = (logits_grad - logits_high.astype(wide)).astype(low)
        logits_grad = jnp.concatenate([logits_high, logits_low], axis=0)
        lg_ref[index] = logits_grad
        row_ref[index] = (
            shared_row[span]
            + left_contraction(
                jnp.concatenate([selector, logits_grad], axis=0),
                jnp.concatenate([row_grad[slots], rt_ref[...]], axis=0),
            )
        ).astype(low)
    store_out(rows_out, turn, turns, slot)


def rest_body(gate, order, *refs):
    x_pieces, refs = refs[:PIECES], refs[PIECES:]
    c_all, chosen_ref, xs_ref, pg_ref, hid_ref, gg_ref, ug_ref, give_ref = refs[:8]
    (sh_ref, sg_ref, lg_ref, sd_ref), refs = refs[8:12], refs[12:]
    out_pieces, refs = refs[:PIECES], refs[PIECES:]
    deg_ref, deu_ref, ded_ref, dcat_ref, dsd_ref = refs[:5]
    x_bufs, c_bufs, out_bufs, x_sems, c_sems, out_sems = refs[5:]
    turn, turns = pl.program_id(0), pl.num_programs(0)
    streams = [Stream(x_pieces, x_bufs, x_sems, turns), Picked(c_all, order, c_bufs, c_sems)]
    slot = load_ahead(streams, turn, turns)
    outs = [Stream(out_pieces, out_bufs, out_sems, turns)]
    free_slot(outs, turn, slot)
    x_ref, c_ref, out_ref = x_bufs.at[slot], c_bufs.at[slot], out_bufs.at[slot]
    blocks, tokens, width = x_ref.shape

    @pl.when(turn == 0)
    def clear():
        for ref in (deg_ref, deu_ref, ded_ref, dcat_ref, dsd_ref):
            ref[...] = jnp.zeros_like(ref)

    hidden_rows = x_ref[...].reshape(blocks * tokens, width)
    picked = xs_ref[...]
    ded_ref[...] += left_contraction(hid_ref[...], pg_ref[...])
    deg_ref[...] += left_contraction(picked, gg_ref[...])
    deu_ref[...] += left_contraction(picked, ug_ref[...])
    dsd_ref[...] += left_contraction(sh_ref[...], c_ref[...].reshape(blocks * tokens, width))
    dcat_ref[:PAIR] += left_contraction(sg_ref[...], hidden_rows)
    logits = jnp.concatenate([lg_ref[index] for index in range(blocks)], axis=1)
    dcat_ref[PAIR:] += matmul(logits, hidden_rows)
    shared_out = matmul(sh_ref[...], sd_ref[...])
    for index in range(blocks):
        span = slice(index * tokens, (index + 1) * tokens)
        slots = slice(index * CAP, (index + 1) * CAP)
        out_ref[index] = (
            shared_out[span] + left_contraction(chosen_ref[index], give_ref[slots])
        ).astype(low)
    store_out(outs, turn, turns, slot)


def grouped(shape):
    return pl.BlockSpec(shape, lambda i, *rest: (i,) + (0,) * (len(shape) - 1))


def fixed(shape):
    return pl.BlockSpec(
        shape, lambda i, *rest: (0,) * len(shape), pipeline_mode=pl.Buffered(1)
    )


def feed_kernel(body, name, scalars, arrays, in_specs, shapes, out_specs, scratch, flops, moved, turns):
    return pl.pallas_call(
        body,
        out_shape=shapes,
        grid_spec=pltpu.PrefetchScalarGridSpec(
            num_scalar_prefetch=len(scalars),
            grid=(turns,),
            in_specs=in_specs,
            out_specs=out_specs,
            scratch_shapes=scratch,
        ),
        compiler_params=pltpu.CompilerParams(
            dimension_semantics=("arbitrary",), vmem_limit_bytes=60 << 20
        ),
        cost_estimate=pl.CostEstimate(flops=flops, bytes_accessed=moved, transcendentals=0),
        name=name,
    )(*scalars, *arrays)


anywhere = pl.BlockSpec(memory_space=pl.ANY)


def choose_call(expert, order, c_all, route_rows, sd, count, tokens):
    width = c_all.shape[2]
    return feed_kernel(
        choose_body,
        "choose",
        (expert, order),
        (c_all, route_rows, sd),
        [anywhere, grouped((GROUP, 2, tokens)), fixed(sd.shape)],
        (
            jax.ShapeDtypeStruct((count * CAP, width), low),
            jax.ShapeDtypeStruct((count * tokens, PAIR), wide),
            jax.ShapeDtypeStruct((count, CAP, tokens), low),
        ),
        (grouped((GROUP * CAP, width)), grouped((GROUP * tokens, PAIR)), grouped((GROUP, CAP, tokens))),
        [pltpu.VMEM((2, GROUP, tokens, width), low), pltpu.SemaphoreType.DMA((2,))],
        8 * count * tokens * width * PAIR,
        count * tokens * width * 3,
        count // GROUP,
    )


def feed_call(expert, pieces, route_rows, pick, shared, chosen, cat, rt, gate, up, down):
    each, tokens, width = pieces[0].shape
    count, units = PIECES * each, gate.shape[2]
    slots, rows = GROUP * CAP, GROUP * tokens
    parts = jax.ShapeDtypeStruct(pieces[0].shape, low)
    saved = (
        (count * CAP, width), (count * CAP, width), (count * CAP, units), (count * CAP, units),
        (count * CAP, units), (count * CAP, width), (count * tokens, PAIR), (count * tokens, PAIR),
        (count, 2 * EXPERTS, tokens),
    )
    return feed_kernel(
        feed_body,
        "feed",
        (expert,),
        tuple(pieces) + (route_rows, pick, shared, chosen, cat, rt, gate, up, down),
        [anywhere] * PIECES
        + [
            grouped((GROUP, 2, tokens)),
            grouped((slots, width)),
            grouped((rows, PAIR)),
            grouped((GROUP, CAP, tokens)),
            fixed(cat.shape),
            fixed(rt.shape),
            fixed(gate.shape),
            fixed(up.shape),
            fixed(down.shape),
        ],
        (parts,) * PIECES + tuple(jax.ShapeDtypeStruct(shape, low) for shape in saved),
        (anywhere,) * PIECES
        + tuple(grouped((shape[0] * GROUP // count,) + shape[1:]) for shape in saved),
        [pltpu.VMEM((2, GROUP, tokens, width), low)] * 2 + [pltpu.SemaphoreType.DMA((2,))] * 2,
        48 * count * CAP * width * units // 2,
        count * tokens * width * 6,
        count // GROUP,
    )


def rest_call(gate, order, pieces, c_all, chosen, saved, sd, units):
    each, tokens, width = pieces[0].shape
    count = PIECES * each
    parts = jax.ShapeDtypeStruct(pieces[0].shape, low)
    shapes = ((width, units), (width, units), (units, width), (PAIR + 2 * EXPERTS, width), (PAIR, width))
    return feed_kernel(
        rest_body,
        "rest",
        (gate, order),
        tuple(pieces) + (c_all, chosen) + tuple(saved) + (sd,),
        [anywhere] * (PIECES + 1)
        + [grouped((GROUP, CAP, tokens))]
        + [grouped((array.shape[0] * GROUP // count,) + array.shape[1:]) for array in saved]
        + [fixed(sd.shape)],
        (parts,) * PIECES + tuple(jax.ShapeDtypeStruct(shape, wide) for shape in shapes),
        (anywhere,) * PIECES + tuple(fixed(shape) for shape in shapes),
        [pltpu.VMEM((2, GROUP, tokens, width), low)] * 3 + [pltpu.SemaphoreType.DMA((2,))] * 3,
        24 * count * CAP * width * units // 2,
        count * tokens * width * 8,
        count // GROUP,
    )


def shards(
    inputs,
    blocks,
    routes,
    attn_gain,
    w_query,
    w_key,
    w_value,
    w_out,
    ffn_gain,
    w_router,
    shared_gate,
    shared_up,
    shared_down,
    expert_gate,
    expert_up,
    expert_down,
    cotangent,
):
    heads, line = lax.axis_size("head"), lax.axis_size("blk")
    count = heads * line
    head, spot = lax.axis_index("head"), lax.axis_index("blk")
    device = head * line + spot
    tokens, width = inputs.shape
    total = count * tokens
    group = width // heads
    pairs = group // PAIR
    rows = w_query.shape[0]
    steps, short_steps = whole_steps(count), line_steps(line)
    sources = slot_sources(count, steps)
    places = jnp.asarray(np.argsort(sources, axis=1).astype(np.int32))[device]
    slot_sources_own = jnp.asarray(sources)[device]
    short_sources = slot_sources(line, short_steps)
    short_order = jnp.asarray(short_sources)[spot]
    short_places = jnp.asarray(np.argsort(short_sources, axis=1).astype(np.int32))[spot]

    def pad_rows(flat):
        extra = -flat.shape[0] % width
        return jnp.pad(flat, (0, extra)).reshape(-1, width)

    def pad_tall(values):
        return jnp.pad(values, ((0, -values.shape[0] % 16), (0, 0)))

    hop = lambda values, step: permute(values, BOTH, count, step)
    far_steps, cross, chip = steps[:-3], steps[-3:-1], steps[-1]

    halves = lambda matrix: matrix.reshape(rows, heads, group).transpose(1, 0, 2)
    extras = jnp.concatenate(
        [attn_gain, ffn_gain, w_router.reshape(-1), routes.T.reshape(-1).astype(low)]
    )
    extras = jnp.pad(extras, (0, -extras.shape[0] % group)).reshape(-1, group)
    split = [halves(matrix) for matrix in (w_query, w_key, w_value)]
    split = jnp.concatenate(split + [jnp.broadcast_to(extras, (heads,) + extras.shape)], axis=1)
    split = jnp.pad(split, ((0, 0), (0, -split.shape[1] % 16), (0, 0)))
    kept = lax.dynamic_index_in_dim(split, head, 0, False)
    sent = lax.dynamic_index_in_dim(split, 1 - head, 0, False)
    weights = [head_order(head, kept, swap_heads(sent))[None]]
    first_steps = weight_steps(line)
    for step in first_steps[:-1]:
        weights.append(grow(weights[-1], permute(weights[-1], "blk", line, step)))
    weights_far = permute(weights[-1], "blk", line, first_steps[-1])
    held = [inputs[None]]
    shared_slice = shared_gate.shape[1] // count
    shared_pack = jnp.stack(
        [
            shared_gate.reshape(rows, count, shared_slice),
            shared_up.reshape(rows, count, shared_slice),
        ],
        axis=2,
    ).reshape(rows, count * 2 * shared_slice)
    for place, step in enumerate(steps[:-2]):
        arrived = after(hop(held[-1], step), weights[min(place, len(weights) - 1)])
        held.append(grow(held[-1], arrived))
    blocks = after(blocks, held[-1])

    own_blocks = jnp.arange(heads, dtype=jnp.int32) * line + spot
    own_slots = places[own_blocks]
    tile = TILE_BLOCKS * tokens
    own_ids = jnp.take(blocks.reshape(count, tokens), own_blocks, axis=0, mode="clip")
    low_id, high_id = own_ids[:, :1], own_ids[:, -1:]

    def counted(test):
        return jnp.sum(test, axis=1, dtype=jnp.int32)

    query_bounds = jnp.stack(
        [
            counted(blocks[None] <= low_id) // tile,
            (counted(blocks[None] <= high_id) + tile - 1) // tile,
        ]
    )
    key_bounds = jnp.stack(
        [
            counted(blocks[None] < low_id) // tile,
            (counted(blocks[None] < high_id) + tile - 1) // tile,
            jnp.full((heads,), total // tile, jnp.int32),
        ]
    )
    id_columns = jnp.tile(own_ids, (1, 2))[:, :, None]
    id_rows = blocks.reshape(count, 1, tokens)

    block_ids = jnp.arange(count, dtype=jnp.int32)
    grad_slots = short_places[block_ids % line] * heads + block_ids // line
    first_places = jnp.asarray(
        np.argsort(slot_sources(line, first_steps), axis=1).astype(np.int32)
    )[spot]
    beside = places[(1 - head) * line + spot]
    expert = (device % EXPERTS).astype(jnp.int32).reshape(1)
    tables = (
        own_slots, query_bounds, key_bounds,
        id_columns, grad_slots, first_places, beside, slot_sources_own, expert,
    )

    start, shared_pack = lax.optimization_barrier((held[-1], shared_pack))
    arrived = after(hop(start, cross[1]), weights[-1], *tables)
    held.append(grow(start, arrived))
    shared_in = lax.all_to_all(shared_pack, BOTH, split_axis=1, concat_axis=0, tiled=True)
    inputs_near = held[-1]
    inputs_far = hop(after(inputs_near, shared_in), chip)

    cot_all = after(jnp.concatenate([cotangent, w_out], axis=0), held[len(far_steps) + 1])
    cot_all = lax.all_gather(cot_all, BOTH, axis=0, tiled=False)
    full_out = cot_all[:, tokens:].reshape(width, width)

    query_weight, key_weight = unpack_call(first_places, weights[-1], weights_far, width)
    first_row = 3 * rows
    flat = grow(weights[-1][:, :, first_row:], weights_far[:, :, first_row:])
    flat = flat.reshape(line, heads, -1)
    flat = jnp.take(flat, first_places, axis=0, mode="clip").transpose(1, 0, 2)
    flat = flat.reshape(count, -1)
    gain_first = flat[:, :rows].reshape(width).astype(wide)
    gain_second = flat[:, rows : 2 * rows].reshape(width).astype(wide)
    router = flat[:, 2 * rows : (2 + EXPERTS) * rows].reshape(width, EXPERTS)
    route_rows = flat[:, (2 + EXPERTS) * rows : (2 + EXPERTS) * rows + 2 * tokens]
    route_rows = jnp.take(route_rows, slot_sources_own, axis=0, mode="clip")
    route_rows = route_rows.reshape(count, 2, tokens).astype(jnp.int32)

    keys, token = project_call(inputs_near, gain_first[None], key_weight, 1.0, count, None)
    keys, token = project_call(inputs_far, gain_first[None], key_weight, 1.0, count, keys)
    neighbour = lax.dynamic_index_in_dim(
        inputs_near, beside, 0, False
    )
    pair_inputs = head_order(head, inputs, neighbour).reshape(heads * tokens, width)
    pair_normed = rms_scale(pair_inputs.astype(wide), gain_first).astype(low)
    own_queries = (matmul(pair_normed, query_weight) * scale_factor).astype(low)
    own_queries = own_queries.reshape(heads, tokens, group)

    own_spec = lambda column: pl.BlockSpec(
        (1, tokens, PAIR), lambda p, j, own, *rest: (own[j], 0, column + p)
    )
    all_spec = lambda column: pl.BlockSpec(
        (count, tokens, PAIR), lambda p, j, *rest: (0, 0, column + p)
    )
    half_spec = pl.BlockSpec((count // 2, tokens, PAIR), lambda p, j, *rest: (0, 0, p))
    part_spec = pl.BlockSpec((1, tokens, PAIR), lambda p, j, *rest: (j, 0, p))
    stat_spec = pl.BlockSpec((1, 1, 1, 2 * tokens), lambda p, j, *rest: (p, j, 0, 0))
    column_spec = pl.BlockSpec((1, 2 * tokens, 1), lambda p, j, *rest: (j, 0, 0))
    ids_spec = pl.BlockSpec((count, 1, tokens), lambda p, j, *rest: (0, 0, 0))
    part_shape = jax.ShapeDtypeStruct((heads, tokens, group), low)
    stat_shape = jax.ShapeDtypeStruct((pairs, heads, 1, 2 * tokens), wide)
    grid = (pairs, heads)
    unit = 2 * heads * tokens * total * group

    attended_own, lse = attention_call(
        attend_body,
        "attend",
        (
            after(own_slots, route_rows),
            places,
            query_bounds,
        ),
        (own_queries, keys, keys, id_columns, id_rows),
        [part_spec, all_spec(0), all_spec(pairs), column_spec, ids_spec],
        (part_shape, stat_shape),
        (part_spec, stat_spec),
        grid,
        2 * unit,
        count,
    )
    attended_back = swap_heads(lax.dynamic_index_in_dim(attended_own, 1 - head, 0, False))
    attended_kept = lax.dynamic_index_in_dim(attended_own, head, 0, False)
    attended = jnp.where(
        head == 0,
        jnp.concatenate([attended_kept, attended_back], axis=1),
        jnp.concatenate([attended_back, attended_kept], axis=1),
    )
    inputs_wide = inputs.astype(wide)
    mixed_rows = inputs_wide + matmul(attended, full_out)
    normed_ffn = rms_scale(mixed_rows, gain_second).astype(low)

    half_pad = HEAD_DIM - shared_slice
    shared_pair = jnp.pad(
        shared_in.reshape(width, 2, shared_slice), ((0, 0), (0, 0), (0, half_pad))
    ).reshape(width, PAIR)
    feed_weight = jnp.concatenate(
        [shared_pair, router, jnp.zeros((width, PAIR - EXPERTS), low)], axis=1
    )
    down_pad = jnp.pad(shared_down, ((0, PAIR - shared_slice), (0, 0)))
    router_rows = jnp.transpose(jnp.concatenate([router, router], axis=1))

    near = normed_ffn[None]
    for step in steps[:-2]:
        arrived = hop(near, step)
        if step is steps[1]:
            queries, token = project_call(
                inputs_near, after(gain_first[None], near), query_weight, scale_factor, count, None
            )
            queries, token = project_call(
                inputs_far, gain_first[None], query_weight, scale_factor, count, queries
            )
            arrived = after(arrived, queries)
        near = grow(near, arrived)
    near_far = hop(near, chip)
    pick, shared_grad, chosen = choose_call(
        after(expert, near), slot_sources_own, cot_all, route_rows, down_pad, count, tokens
    )
    crossed = after(hop(near, cross[1]), chosen, feed_weight, near_far)
    pieces = [near, crossed, near_far, hop(crossed, chip)]
    near_low, near_high, far_low, far_high, *saved = feed_call(
        expert, pieces, route_rows, pick, shared_grad, chosen, feed_weight, router_rows,
        expert_gate, expert_up, expert_down,
    )
    row_upper = (near_high.astype(wide) + hop(far_high, chip).astype(wide)).astype(low)
    terms = [near_low, hop(after(far_low, row_upper), chip)]
    (
        out_low, out_high, out_far_low, out_far_high,
        grad_egate, grad_eup, grad_edown, grad_feed, grad_sdown,
    ) = rest_call(
        after(expert, row_upper), slot_sources_own, pieces, cot_all, chosen, saved, down_pad,
        expert_gate.shape[2],
    )
    terms = terms + [after(hop(row_upper, cross[1]), out_low)]
    out_far_high, terms[-1] = lax.optimization_barrier((out_far_high, terms[-1]))
    out_upper = (out_high.astype(wide) + hop(out_far_high, chip).astype(wide)).astype(low)
    out_terms = [out_low, hop(after(out_far_low, out_upper), chip)]
    grad_sdown = grad_sdown[:shared_slice]
    terms = scatter_step(terms, BOTH, count, cross[0])
    terms[-1], out_upper = lax.optimization_barrier((terms[-1], out_upper))
    out_arrived = hop(out_upper, cross[1])
    grad_shared, terms[-1] = lax.optimization_barrier((grad_feed[:PAIR], terms[-1]))
    grad_shared = grad_shared.reshape(2, HEAD_DIM, width)[:, :shared_slice].reshape(-1, width)
    grad_shared = jnp.transpose(grad_shared).astype(low)
    grad_shared_back = lax.all_to_all(grad_shared, BOTH, split_axis=0, concat_axis=1, tiled=True)
    for step in reversed(far_steps):
        terms = scatter_step(terms, BOTH, count, step)
    normed_ffn_grad = finish(terms)
    grad_router = jnp.transpose(
        grad_feed[PAIR : PAIR + EXPERTS] + grad_feed[PAIR + EXPERTS : PAIR + 2 * EXPERTS]
    )

    unused_second, second_pull = jax.vjp(rms_scale, mixed_rows, gain_second)
    mixed_part, grad_gain_ffn = second_pull(normed_ffn_grad)
    mixed_grad = cotangent.astype(wide) + mixed_part
    mixed_low = after(mixed_grad.astype(low), out_arrived, grad_shared_back)
    mixed_pair = head_order(head, mixed_low, swap_heads(mixed_low)).reshape(heads * tokens, width)
    own_out = lax.dynamic_slice_in_dim(full_out, head * group, group, 0)
    attended_grad = right_contract(mixed_pair, own_out).astype(low)
    attended_flat = attended_own.reshape(heads * tokens, group)
    head_marks = (
        jnp.arange(group)[None] // HEAD_DIM == jnp.arange(2 * pairs)[:, None]
    ).astype(wide)
    delta = lax.dot_general(
        head_marks,
        attended_grad.astype(wide) * attended_flat.astype(wide),
        (((1,), (1,)), ((), ())),
        precision=lax.Precision.HIGHEST,
    )
    delta = (
        delta.reshape(pairs, 2, heads, tokens)
        .transpose(0, 2, 1, 3)
        .reshape(pairs, heads, 1, 2 * tokens)
    )
    stats = jnp.stack([lse, delta]).transpose(2, 0, 1, 3, 4).reshape(heads, -1)
    stats_rows = jnp.concatenate(two_parts(stats), axis=1).reshape(heads, -1, group)
    grad_parts = attended_grad.reshape(heads, tokens, group)
    grads = [jnp.concatenate([grad_parts, stats_rows], axis=1)[None]]
    def next_out(terms, arrived, gate):
        terms = terms + [arrived]
        sent = upper(terms)
        gate, sent = lax.optimization_barrier((gate, sent))
        return lower(terms), sent, gate

    columns = two_parts(jnp.concatenate([grad_gain_ffn[:, None], grad_router], axis=1))
    extra = columns[0].shape[1]
    columns = jnp.concatenate(columns, axis=1)
    columns = jnp.pad(columns, ((0, 0), (1, PAIR - 1 - 2 * extra)))
    out_terms, sent, grads[0] = next_out(out_terms, out_arrived, grads[0])
    out_arrived = hop(sent, cross[0])
    tail = list(reversed(far_steps))
    for place, step in enumerate(short_steps[:-1]):
        if place == 1:
            grads[-1] = after(grads[-1], out_arrived, columns)
        if place == len(short_steps) - 2:
            out_terms, sent, grads[-1] = next_out(out_terms, out_arrived, grads[-1])
            out_arrived = hop(sent, tail[0])
        grads.append(grow(grads[-1], permute(grads[-1], "blk", line, step)))
    query_q = after(own_slots, grads[-2])
    query_grad = attention_call(
        query_body,
        "query_gradient",
        (query_q, places, query_bounds),
        (own_queries, keys, keys, grad_parts, lse, delta, id_columns, id_rows),
        [
            part_spec,
            all_spec(0),
            all_spec(pairs),
            part_spec,
            stat_spec,
            stat_spec,
            column_spec,
            ids_spec,
        ],
        part_shape,
        part_spec,
        grid,
        3 * unit,
        count,
    )
    start = after(grads[-1], query_grad)
    out_terms, sent, start = next_out(out_terms, out_arrived, start)
    for step in tail[1:-1]:
        out_terms, sent, start = next_out(out_terms, hop(sent, step), start)
    out_arrived = hop(sent, tail[-1])
    grads.append(permute(start, "blk", line, short_steps[-1]))
    grad_halves = [part.reshape(count // 2, -1, group) for part in (start, grads[-1])]

    def stat_part(part):
        part = part[:, tokens:].reshape(count // 2, 2, -1).astype(wide)
        return (part[:, 0] + part[:, 1]).reshape(-1, 1, 2 * tokens)

    stats_all = jnp.concatenate([stat_part(part) for part in grad_halves])
    key_grad, value_grad = attention_call(
        key_body,
        "key_gradient",
        (own_slots, places, grad_slots, key_bounds),
        (keys, keys, queries, *grad_halves, stats_all, id_columns, id_rows),
        [
            own_spec(0),
            own_spec(pairs),
            all_spec(0),
            half_spec,
            half_spec,
            pl.BlockSpec(stats_all.shape, lambda p, j, *rest: (0, 0, 0)),
            column_spec,
            ids_spec,
        ],
        (part_shape, part_shape),
        (part_spec, part_spec),
        grid,
        4 * unit,
        count,
    )

    near, far, normed_part = weights_call(
        short_places, pair_inputs, gain_first[None], query_grad, key_grad, value_grad,
        query_weight, key_weight, columns, attended_flat, mixed_pair, line,
    )
    backward = list(reversed(short_steps))
    sums = [near, permute(far, "blk", line, backward[0])]
    out_terms.append(out_arrived)
    for place, step in enumerate(backward[1:]):
        sums = scatter_step(sums, "blk", line, step)
        if place == 0:
            first_sum = sums[-1]
            sums[-1] = after(sums[-1], out_arrived)
    output = (mixed_rows + finish(out_terms)).astype(low)
    sums = [sums]
    summed = finish(sums[0])
    grad_wout_own = summed[:, :, 3 * group + PAIR :].transpose(1, 0, 2).reshape(rows, width)
    summed = summed[:, :, : 3 * group + PAIR]
    summed_back = swap_heads(
        lax.dynamic_index_in_dim(summed, 1 - head, 0, False).astype(low)
    ).astype(wide)
    summed_kept = lax.dynamic_index_in_dim(summed, head, 0, False)
    joined = head_order(head, summed_kept, summed_back)
    small = jnp.sum(joined[:, :, 3 * group :], axis=0)
    gain_column = small[:, 0] + small[:, PAIR - 1]
    small = small[:, 1 : extra + 1] + small[:, extra + 1 : 2 * extra + 1]
    joined = joined[:, :, : 3 * group].reshape(heads, rows, 3, group)
    joined = joined.transpose(2, 1, 0, 3).reshape(3, rows, width)

    normed_parts = normed_part.reshape(heads, tokens, width)
    arrived = swap_heads(lax.dynamic_index_in_dim(normed_parts, 1 - head, 0, False).astype(low))
    normed_grad = lax.dynamic_index_in_dim(normed_parts, head, 0, False) + arrived.astype(wide)
    unused_first, first_pull = jax.vjp(lambda rows_in: rms_scale(rows_in, gain_first), inputs_wide)
    grad_inputs = mixed_grad + first_pull(after(normed_grad, first_sum))[0]
    grad_shared_back = after(grad_shared_back, first_sum).reshape(rows, count, 2, shared_slice)
    grad_sgate = grad_shared_back[:, :, 0].reshape(rows, -1).astype(wide)
    grad_sup = grad_shared_back[:, :, 1].reshape(rows, -1).astype(wide)

    return (
        output,
        grad_inputs,
        gain_column,
        joined[0].astype(wide),
        joined[1].astype(wide),
        joined[2].astype(wide),
        grad_wout_own,
        small[:, 0],
        small[:, 1:],
        grad_sgate,
        grad_sup,
        grad_sdown,
        grad_egate[None],
        grad_eup[None],
        grad_edown[None],
    )


def solution(mesh):
    both = P(BOTH)
    rows = P(BOTH, None)
    slabs = P(BOTH, None, None)
    return jax.shard_map(
        shards,
        mesh=mesh,
        in_specs=(
            rows, P(), rows, both, rows, rows, rows, rows, both, rows, rows, rows, rows,
            slabs, slabs, slabs, rows,
        ),
        out_specs=(
            rows, rows, both, rows, rows, rows, rows, both, rows, rows, rows, rows,
            slabs, slabs, slabs,
        ),
        check_vma=False,
    )
```

```python
import functools

import jax
import jax.numpy as jnp
import numpy as np
from jax import lax
from jax.experimental import pallas as pl
from jax.experimental.pallas import tpu as pltpu
from jax.sharding import PartitionSpec as P

HEAD_DIM = 64
EXPERTS = 16
CAP = 32
PAIR = 2 * HEAD_DIM
TILE_BLOCKS = 8
BOTH = ("head", "blk")

epsilon = 1e-05
scale_factor = 0.125
masked_value = -1e30
low = jnp.bfloat16
wide = jnp.float32


def matmul(left_side, right_side):
    return jnp.dot(left_side, right_side, preferred_element_type=wide)


def left_contraction(left_side, right_side):
    return lax.dot_general(
        left_side, right_side, (((0,), (0,)), ((), ())), preferred_element_type=wide
    )


def right_contract(left_side, right_side):
    return lax.dot_general(
        left_side, right_side, (((1,), (1,)), ((), ())), preferred_element_type=wide
    )


def rms_scale(values, gain_row):
    return (
        values * lax.rsqrt(jnp.mean(values * values, axis=-1, keepdims=True) + epsilon) * gain_row
    )


def silu_parts(gate_pre, up_pre):
    gate = jax.nn.sigmoid(gate_pre)
    swish = gate_pre * gate
    return swish * up_pre, gate * (1.0 + gate_pre * (1.0 - gate)) * up_pre, swish


def whole_steps(count):
    bits = count.bit_length() - 1
    steps = [functools.partial(flip, bit, bit) for bit in range(bits - 2, 1, -1)]
    return steps + [
        functools.partial(flip, 1, bits - 1),
        functools.partial(flip, bits - 1, 1),
        functools.partial(flip, 0, 0),
    ]


def flip(even_bit, odd_bit, index):
    return index ^ (1 << (odd_bit if index & 1 else even_bit))


def line_steps(count):
    bits = count.bit_length() - 1
    return [functools.partial(flip, bit, bit) for bit in range(bits - 1, -1, -1)]


def weight_steps(count):
    steps = line_steps(count)
    return [steps[-2]] + steps[:-2] + [steps[-1]]


def slot_sources(count, steps):
    order = [[i] for i in range(count)]
    for step in steps:
        order = [order[i] + order[step(i)] for i in range(count)]
    return np.array(order, np.int32)


def permute(values, axis, count, step):
    return lax.ppermute(values, axis, [(i, step(i)) for i in range(count)])


def after(value, *needed):
    return lax.optimization_barrier((value,) + needed)[0]


def two_parts(values):
    high = lax.reduce_precision(values, 8, 7)
    return [high.astype(low), (values - high).astype(low)]


def grow(held, arrived):
    return jnp.concatenate([held, arrived], axis=0)


def gather(values, axis, count, steps):
    held = values[None]
    for step in steps:
        held = grow(held, permute(held, axis, count, step))
    return held


def upper(terms):
    half = terms[0].shape[0] // 2
    return sum(term[half:].astype(wide) for term in terms).astype(low)


def lower(terms):
    half = terms[0].shape[0] // 2
    return [term[:half] for term in terms]


def scatter_step(terms, axis, count, step):
    return lower(terms) + [permute(upper(terms), axis, count, step)]


def finish(terms):
    return sum(term[0].astype(wide) for term in terms)


def scatter_sum(slots, axis, count, steps):
    terms = [slots]
    for step in reversed(steps):
        terms = scatter_step(terms, axis, count, step)
    return finish(terms)


def swap_heads(values):
    return lax.ppermute(values, "head", [(0, 1), (1, 0)])


def head_order(head, own, other):
    return jnp.where(head == 0, jnp.stack([own, other]), jnp.stack([other, own]))


def stack_heads(rows):
    first = lax.broadcasted_iota(jnp.int32, rows.shape, 1) < HEAD_DIM
    zero = jnp.zeros_like(rows)
    return jnp.concatenate([jnp.where(first, rows, zero), jnp.where(first, zero, rows)], axis=0)


def join_heads(stacked):
    half = stacked.shape[0] // 2
    top = stacked[:half]
    first = lax.broadcasted_iota(jnp.int32, top.shape, 1) < HEAD_DIM
    return jnp.where(first, top, stacked[half:])


def load_tile(ref, slots, index):
    return jnp.concatenate(
        [ref[slots[index * TILE_BLOCKS + part]] for part in range(TILE_BLOCKS)], axis=0
    )


def load_ids(ref, index):
    return jnp.concatenate(
        [ref[index * TILE_BLOCKS + part] for part in range(TILE_BLOCKS)], axis=1
    )


def as_column(row):
    return jnp.transpose(jnp.broadcast_to(row, (PAIR, row.shape[1])))[:, :1]


def attend_body(own, slots, bounds, q_ref, k_ref, v_ref, qid_ref, kid_ref, out_ref, lse_ref):
    part = pl.program_id(1)
    stacked = stack_heads(q_ref[0])
    rows = stacked.shape[0]

    def step(masked, index, state):
        top, total, weighted = state
        scores = right_contract(stacked, load_tile(k_ref, slots, index))
        if masked:
            scores = jnp.where(load_ids(kid_ref, index) <= qid_ref[0], scores, masked_value)
        new_top = jnp.maximum(top, jnp.max(scores, axis=-1, keepdims=True))
        weights = jnp.exp(scores - new_top)
        rescale = jnp.exp(top - new_top)
        total = total * rescale + jnp.sum(weights, axis=-1, keepdims=True)
        weighted = weighted * rescale + matmul(weights.astype(low), load_tile(v_ref, slots, index))
        return new_top, total, weighted

    state = (
        jnp.full((rows, 1), masked_value, wide),
        jnp.zeros((rows, 1), wide),
        jnp.zeros((rows, PAIR), wide),
    )
    state = lax.fori_loop(0, bounds[0, part], functools.partial(step, False), state)
    top, total, weighted = lax.fori_loop(
        bounds[0, part], bounds[1, part], functools.partial(step, True), state
    )
    out_ref[0] = join_heads(weighted / total).astype(low)
    lse = jnp.broadcast_to(top + jnp.log(total), (rows, PAIR))
    lse_ref[0, 0] = jnp.transpose(lse)[:1]


def query_body(
    own, slots, bounds, q_ref, k_ref, v_ref, g_ref, lse_ref, delta_ref, qid_ref, kid_ref, dq_ref
):
    part = pl.program_id(1)
    stacked = stack_heads(q_ref[0])
    grads = stack_heads(g_ref[0])
    lse = as_column(lse_ref[0, 0])
    delta = as_column(delta_ref[0, 0])

    def step(masked, index, total):
        keys = load_tile(k_ref, slots, index)
        probs = jnp.exp(right_contract(stacked, keys) - lse)
        if masked:
            probs = jnp.where(load_ids(kid_ref, index) <= qid_ref[0], probs, 0.0)
        moved = right_contract(grads, load_tile(v_ref, slots, index)) - delta
        return total + matmul((probs * moved).astype(low), keys)

    total = jnp.zeros((stacked.shape[0], PAIR), wide)
    total = lax.fori_loop(0, bounds[0, part], functools.partial(step, False), total)
    total = lax.fori_loop(
        bounds[0, part], bounds[1, part], functools.partial(step, True), total
    )
    dq_ref[0] = (join_heads(total) * scale_factor).astype(low)


def key_body(
    own, slots, gslots, bounds, k_ref, v_ref, q_ref, g_near, g_far, stat_ref, kid_ref, qid_ref,
    dk_ref, dv_ref,
):
    pair = pl.program_id(0)
    part = pl.program_id(1)
    pairs = pl.num_programs(0)
    keys = stack_heads(k_ref[0])
    values = stack_heads(v_ref[0])
    rows = keys.shape[0]
    half = g_near.shape[0]

    def stat_rows(index, which):
        tops, bottoms = [], []
        for piece in range(TILE_BLOCKS):
            slot = gslots[index * TILE_BLOCKS + piece]
            place = slot * (2 * pairs) + which * pairs + pair
            row = stat_ref[place]
            tops.append(row[:, :PAIR])
            bottoms.append(row[:, PAIR:])
        shape = (rows // 2, TILE_BLOCKS * PAIR)
        return jnp.concatenate(
            [
                jnp.broadcast_to(jnp.concatenate(tops, axis=1), shape),
                jnp.broadcast_to(jnp.concatenate(bottoms, axis=1), shape),
            ],
            axis=0,
        )

    def step(masked, index, state):
        dk_total, dv_total = state
        queries = load_tile(q_ref, slots, index)
        grads = []
        for piece in range(TILE_BLOCKS):
            slot = gslots[index * TILE_BLOCKS + piece]
            near = g_near[jnp.minimum(slot, half - 1)]
            grads.append(jnp.where(slot < half, near, g_far[jnp.maximum(slot - half, 0)]))
        grads = jnp.concatenate(grads, axis=0)
        probs = jnp.exp(right_contract(keys, queries) - stat_rows(index, 0))
        if masked:
            probs = jnp.where(kid_ref[0] <= load_ids(qid_ref, index), probs, 0.0)
        moved = right_contract(values, grads) - stat_rows(index, 1)
        dk_total = dk_total + matmul((probs * moved).astype(low), queries)
        dv_total = dv_total + matmul(probs.astype(low), grads)
        return dk_total, dv_total

    state = (jnp.zeros((rows, PAIR), wide), jnp.zeros((rows, PAIR), wide))
    state = lax.fori_loop(
        bounds[0, part], bounds[1, part], functools.partial(step, True), state
    )
    dk_total, dv_total = lax.fori_loop(
        bounds[1, part], bounds[2, part], functools.partial(step, False), state
    )
    dk_ref[0] = join_heads(dk_total).astype(low)
    dv_ref[0] = join_heads(dv_total).astype(low)


def attention_call(body, name, tables, arrays, specs, outs, out_specs, grid, cost, count):
    return pl.pallas_call(
        body,
        out_shape=outs,
        grid_spec=pltpu.PrefetchScalarGridSpec(
            num_scalar_prefetch=len(tables), grid=grid, in_specs=specs, out_specs=out_specs
        ),
        compiler_params=pltpu.CompilerParams(
            dimension_semantics=("arbitrary", "arbitrary"),
            vmem_limit_bytes=60 << 20,
        ),
        cost_estimate=pl.CostEstimate(
            flops=8 * cost, bytes_accessed=cost // 512, transcendentals=cost // 512
        ),
        name=name,
    )(*tables, *arrays)


def unpack_body(slots, near_ref, far_ref, query_ref, key_ref):
    half, heads, unused, group = near_ref.shape
    line = 2 * half
    rows = query_ref.shape[0] // (heads * line)
    for spot in range(line):
        slot = slots[spot]
        is_near = slot < half
        low_slot, high_slot = jnp.minimum(slot, half - 1), jnp.maximum(slot - half, 0)
        for source in range(heads):
            block = jnp.where(is_near, near_ref[low_slot, source], far_ref[high_slot, source])
            first = (source * line + spot) * rows
            query_ref[first : first + rows] = block[:rows]
            for part in range(2):
                key_ref[first : first + rows, part * group : (part + 1) * group] = block[
                    (part + 1) * rows : (part + 2) * rows
                ]


def unpack_call(slots, near, far, width):
    half, heads, unused, group = near.shape
    whole = lambda shape: pl.BlockSpec(shape, lambda i, *rest: (0,) * len(shape))
    shapes = ((width, group), (width, 2 * group))
    return pl.pallas_call(
        unpack_body,
        out_shape=tuple(jax.ShapeDtypeStruct(shape, low) for shape in shapes),
        grid_spec=pltpu.PrefetchScalarGridSpec(
            num_scalar_prefetch=1,
            grid=(1,),
            in_specs=[whole(near.shape), whole(far.shape)],
            out_specs=tuple(whole(shape) for shape in shapes),
        ),
        compiler_params=pltpu.CompilerParams(
            dimension_semantics=("arbitrary",), vmem_limit_bytes=32 << 20
        ),
        cost_estimate=pl.CostEstimate(
            flops=0, bytes_accessed=8 * near.size, transcendentals=0
        ),
        name="unpack",
    )(slots, near, far)


def weights_body(
    slots, x_ref, gain_ref, dq_ref, dk_ref, dv_ref, query_ref, key_ref, columns_ref, attended_ref, mixed_ref,
    near_ref, far_ref, part_ref,
):
    half, heads, rows, unused = near_ref.shape
    group = dq_ref.shape[1]
    unit = rms_scale(x_ref[...].astype(wide), 1.0)
    normed = (unit * gain_ref[...]).astype(low)
    grads = (dq_ref[...], dk_ref[...], dv_ref[...])
    part = (
        right_contract(grads[0], query_ref[...])
        + right_contract(grads[1], key_ref[:, :group])
        + right_contract(grads[2], key_ref[:, group:])
    )
    part_ref[...] = part
    gain = jnp.sum(part * unit, axis=0, keepdims=True)
    gain = jnp.transpose(jnp.broadcast_to(gain, (PAIR, gain.shape[1])))
    gain_high = gain.astype(low)
    gain_low = (gain - gain_high.astype(wide)).astype(low)
    lane = lax.broadcasted_iota(jnp.int32, gain.shape, 1)
    columns = jnp.where(lane == 0, gain_high, columns_ref[...])
    columns = jnp.where(lane == PAIR - 1, gain_low, columns)
    pieces = [left_contraction(normed, grad).astype(low) for grad in grads] + [columns]
    wout = left_contraction(attended_ref[...], mixed_ref[...]).astype(low)
    starts = [0, group, 2 * group, 3 * group]
    for spot in range(2 * half):
        slot = slots[spot]

        def give(ref, at, spot=spot):
            for source in range(heads):
                first = (source * 2 * half + spot) * rows
                for start, piece in zip(starts, pieces):
                    ref[at, source, :, start : start + piece.shape[1]] = piece[first : first + rows]
                ref[at, source, :, 3 * group + PAIR :] = wout[
                    spot * rows : (spot + 1) * rows, source * group : (source + 1) * group
                ]

        @pl.when(slot < half)
        def to_near():
            give(near_ref, slot)

        @pl.when(slot >= half)
        def to_far():
            give(far_ref, slot - half)


def weights_call(slots, inputs, gain, dq, dk, dv, query_weight, key_weight, columns, attended, mixed, line):
    heads, tokens, group = dq.shape
    width = inputs.shape[1]
    rows = width // (heads * line)
    flat = lambda array: array.reshape(heads * tokens, group)
    arrays = (inputs, gain, flat(dq), flat(dk), flat(dv), query_weight, key_weight, columns, attended, mixed)
    whole = lambda shape: pl.BlockSpec(shape, lambda i, *rest: (0,) * len(shape))
    parts = (line // 2, heads, rows, 4 * group + PAIR)
    return pl.pallas_call(
        weights_body,
        out_shape=(
            jax.ShapeDtypeStruct(parts, low),
            jax.ShapeDtypeStruct(parts, low),
            jax.ShapeDtypeStruct(inputs.shape, wide),
        ),
        grid_spec=pltpu.PrefetchScalarGridSpec(
            num_scalar_prefetch=1,
            grid=(1,),
            in_specs=[whole(array.shape) for array in arrays],
            out_specs=(whole(parts), whole(parts), whole(inputs.shape)),
        ),
        compiler_params=pltpu.CompilerParams(
            dimension_semantics=("arbitrary",), vmem_limit_bytes=60 << 20
        ),
        cost_estimate=pl.CostEstimate(
            flops=20 * heads * tokens * width * group, bytes_accessed=8 << 20, transcendentals=0
        ),
        name="weight_gradients",
    )(slots, *arrays)


GROUP = 8


class Stream:
    def __init__(self, pieces, buffers, semaphores, turns):
        self.pieces, self.buffers, self.semaphores = pieces, buffers, semaphores
        self.each, self.blocks = turns // len(pieces), buffers.shape[1]

    def load(self, index, place):
        self.begin(index, place, lambda part, buffer: (part, buffer))

    def store(self, index, place):
        self.begin(index, place, lambda part, buffer: (buffer, part))

    def begin(self, index, place, ends):
        for number, piece in enumerate(self.pieces):

            @pl.when(index // self.each == number)
            def start(piece=piece):
                part = piece.at[pl.ds(index % self.each * self.blocks, self.blocks)]
                source, target = ends(part, self.buffers.at[place])
                pltpu.make_async_copy(source, target, self.semaphores.at[place]).start()

    def loaded(self, place):
        pltpu.make_async_copy(
            self.pieces[0].at[pl.ds(0, self.blocks)],
            self.buffers.at[place],
            self.semaphores.at[place],
        ).wait()

    def stored(self, place):
        pltpu.make_async_copy(
            self.buffers.at[place],
            self.pieces[0].at[pl.ds(0, self.blocks)],
            self.semaphores.at[place],
        ).wait()


class Picked:
    def __init__(self, source, order, buffers, semaphores):
        self.source, self.order, self.buffers, self.semaphores = source, order, buffers, semaphores
        self.blocks, self.rows = buffers.shape[1:3]

    def load(self, index, place):
        for part in range(self.blocks):
            block = self.source.at[self.order[index * self.blocks + part], pl.ds(0, self.rows)]
            pltpu.make_async_copy(
                block, self.buffers.at[place, part], self.semaphores.at[place]
            ).start()

    def loaded(self, place):
        pltpu.make_async_copy(
            self.source.at[pl.ds(0, self.blocks), pl.ds(0, self.rows)],
            self.buffers.at[place],
            self.semaphores.at[place],
        ).wait()


PIECES = 4


def load_ahead(streams, turn, turns):
    slot = turn % 2

    @pl.when(turn == 0)
    def first():
        for stream in streams:
            stream.load(turn, slot)

    @pl.when(turn + 1 < turns)
    def ahead():
        for stream in streams:
            stream.load(turn + 1, 1 - slot)

    for stream in streams:
        stream.loaded(slot)
    return slot


def free_slot(streams, turn, slot):
    @pl.when(turn >= 2)
    def free():
        for stream in streams:
            stream.stored(slot)


def store_out(streams, turn, turns, slot):
    for stream in streams:
        stream.store(turn, slot)

    @pl.when(turn == turns - 1)
    def drain():
        for place in range(2):
            for stream in streams:
                stream.stored(place)


def choose_body(
    expert, order, c_all, route_ref, sd_ref, pick_ref, hidden_ref, chosen_ref, c_bufs, c_sems
):
    turn, turns = pl.program_id(0), pl.num_programs(0)
    slot = load_ahead([Picked(c_all, order, c_bufs, c_sems)], turn, turns)
    c_ref = c_bufs.at[slot]
    blocks, tokens, width = c_ref.shape
    hidden_ref[...] = right_contract(c_ref[...].reshape(blocks * tokens, width), sd_ref[...])
    routed = (route_ref[:, 0, :] == expert[0]) | (route_ref[:, 1, :] == expert[0])
    before = (
        lax.broadcasted_iota(jnp.int32, (tokens, tokens), 0)
        < lax.broadcasted_iota(jnp.int32, (tokens, tokens), 1)
    )
    rank = matmul(
        jnp.where(routed, 1.0, 0.0).astype(low), jnp.where(before, 1.0, 0.0).astype(low)
    )
    rank = jnp.where(routed, rank, -1.0)
    slot_ids = lax.broadcasted_iota(jnp.int32, (CAP, tokens), 0).astype(wide)
    for index in range(blocks):
        selector = jnp.where(rank[index : index + 1] == slot_ids, 1.0, 0.0).astype(low)
        chosen_ref[index] = selector
        pick_ref[index * CAP : (index + 1) * CAP] = matmul(selector, c_ref[index]).astype(low)


def feed_body(expert, *refs):
    x_pieces, refs = refs[:PIECES], refs[PIECES:]
    (route_ref, pick_ref, shared_ref, chosen_ref, cat_ref, rt_ref, eg_ref, eu_ref, ed_ref), refs = (
        refs[:9], refs[9:]
    )
    row_pieces, refs = refs[:PIECES], refs[PIECES:]
    (xs_ref, pg_ref, hid_ref, gg_ref, ug_ref, give_ref, sh_ref, sg_ref, lg_ref), refs = (
        refs[:9], refs[9:]
    )
    x_bufs, row_bufs, x_sems, row_sems = refs
    turn, turns = pl.program_id(0), pl.num_programs(0)
    slot = load_ahead([Stream(x_pieces, x_bufs, x_sems, turns)], turn, turns)
    rows_out = [Stream(row_pieces, row_bufs, row_sems, turns)]
    free_slot(rows_out, turn, slot)
    x_ref, row_ref = x_bufs.at[slot], row_bufs.at[slot]
    blocks, tokens, width = x_ref.shape
    count = blocks * tokens

    outcome = matmul(x_ref[...].reshape(count, width), cat_ref[...])
    pre = outcome[:, :PAIR]
    inside = lax.broadcasted_iota(jnp.int32, pre.shape, 1) < HEAD_DIM
    product, gate_slope, up_slope = silu_parts(pre, pltpu.roll(pre, HEAD_DIM, 1))
    sh_ref[...] = jnp.where(inside, product, 0.0).astype(low)
    shared_hidden_grad = shared_ref[...]
    gate_side = jnp.where(inside, shared_hidden_grad * gate_slope, 0.0)
    up_side = jnp.where(inside, shared_hidden_grad * up_slope, 0.0)
    shared_grad = (gate_side + pltpu.roll(up_side, HEAD_DIM, 1)).astype(low)
    sg_ref[...] = shared_grad

    first = route_ref[:, 0, :]
    second = route_ref[:, 1, :]
    is_first = first == expert[0]
    expert_ids = lax.broadcasted_iota(jnp.int32, (EXPERTS, tokens), 0)
    contrasts, shares, leans, picked = [], [], [], []
    for index in range(blocks):
        span = slice(index * tokens, (index + 1) * tokens)
        logits = jnp.transpose(outcome[span, PAIR:])[:EXPERTS]
        contrast = jnp.where(expert_ids == first[index : index + 1], 1.0, 0.0) - jnp.where(
            expert_ids == second[index : index + 1], 1.0, 0.0
        )
        gap = jnp.sum(logits * contrast, axis=0, keepdims=True)
        share_first = jax.nn.sigmoid(gap)
        share_second = jax.nn.sigmoid(-gap)
        mark = is_first[index : index + 1]
        share = jnp.where(mark, share_first, share_second)
        lean = jnp.where(mark, 1.0, -1.0) * share_first * share_second
        selector = chosen_ref[index].astype(wide)
        contrasts.append(contrast)
        shares.append(jnp.sum(selector * share, axis=1, keepdims=True))
        leans.append(jnp.sum(selector * lean, axis=1, keepdims=True))
        picked.append(matmul(chosen_ref[index], x_ref[index]).astype(low))
    picked = jnp.concatenate(picked, axis=0)
    picked_grad = pick_ref[...].astype(wide)
    share_rows = jnp.concatenate(shares, axis=0)
    lean_rows = jnp.concatenate(leans, axis=0)
    xs_ref[...] = picked

    product, gate_slope, up_slope = silu_parts(
        matmul(picked, eg_ref[0]), matmul(picked, eu_ref[0])
    )
    hidden = product.astype(low)
    hid_ref[...] = hidden
    partial_rows = matmul(hidden, ed_ref[0]).astype(low).astype(wide)
    dots = lean_rows * jnp.sum(picked_grad * partial_rows, axis=1, keepdims=True)
    partial_grad = (share_rows * picked_grad).astype(low)
    pg_ref[...] = partial_grad
    give_ref[...] = (share_rows * partial_rows).astype(low)
    hidden_grad = right_contract(partial_grad, ed_ref[0])
    gate_grad = (hidden_grad * gate_slope).astype(low)
    up_grad = (hidden_grad * up_slope).astype(low)
    gg_ref[...] = gate_grad
    ug_ref[...] = up_grad
    row_grad = (
        right_contract(gate_grad, eg_ref[0]) + right_contract(up_grad, eu_ref[0])
    ).astype(low)

    shared_row = right_contract(shared_grad, cat_ref[:, :PAIR])
    for index in range(blocks):
        span = slice(index * tokens, (index + 1) * tokens)
        slots = slice(index * CAP, (index + 1) * CAP)
        selector = chosen_ref[index]
        lean = jnp.sum(selector.astype(wide) * dots[slots], axis=0, keepdims=True)
        logits_grad = lean * contrasts[index]
        logits_high = logits_grad.astype(low)
        logits_low = (logits_grad - logits_high.astype(wide)).astype(low)
        logits_grad = jnp.concatenate([logits_high, logits_low], axis=0)
        lg_ref[index] = logits_grad
        row_ref[index] = (
            shared_row[span]
            + left_contraction(
                jnp.concatenate([selector, logits_grad], axis=0),
                jnp.concatenate([row_grad[slots], rt_ref[...]], axis=0),
            )
        ).astype(low)
    store_out(rows_out, turn, turns, slot)


def rest_body(gate, order, *refs):
    x_pieces, refs = refs[:PIECES], refs[PIECES:]
    c_all, chosen_ref, xs_ref, pg_ref, hid_ref, gg_ref, ug_ref, give_ref = refs[:8]
    (sh_ref, sg_ref, lg_ref, sd_ref), refs = refs[8:12], refs[12:]
    out_pieces, refs = refs[:PIECES], refs[PIECES:]
    deg_ref, deu_ref, ded_ref, dcat_ref, dsd_ref = refs[:5]
    x_bufs, c_bufs, out_bufs, x_sems, c_sems, out_sems = refs[5:]
    turn, turns = pl.program_id(0), pl.num_programs(0)
    streams = [Stream(x_pieces, x_bufs, x_sems, turns), Picked(c_all, order, c_bufs, c_sems)]
    slot = load_ahead(streams, turn, turns)
    outs = [Stream(out_pieces, out_bufs, out_sems, turns)]
    free_slot(outs, turn, slot)
    x_ref, c_ref, out_ref = x_bufs.at[slot], c_bufs.at[slot], out_bufs.at[slot]
    blocks, tokens, width = x_ref.shape

    @pl.when(turn == 0)
    def clear():
        for ref in (deg_ref, deu_ref, ded_ref, dcat_ref, dsd_ref):
            ref[...] = jnp.zeros_like(ref)

    hidden_rows = x_ref[...].reshape(blocks * tokens, width)
    picked = xs_ref[...]
    ded_ref[...] += left_contraction(hid_ref[...], pg_ref[...])
    deg_ref[...] += left_contraction(picked, gg_ref[...])
    deu_ref[...] += left_contraction(picked, ug_ref[...])
    dsd_ref[...] += left_contraction(sh_ref[...], c_ref[...].reshape(blocks * tokens, width))
    dcat_ref[:PAIR] += left_contraction(sg_ref[...], hidden_rows)
    logits = jnp.concatenate([lg_ref[index] for index in range(blocks)], axis=1)
    dcat_ref[PAIR:] += matmul(logits, hidden_rows)
    shared_out = matmul(sh_ref[...], sd_ref[...])
    for index in range(blocks):
        span = slice(index * tokens, (index + 1) * tokens)
        slots = slice(index * CAP, (index + 1) * CAP)
        out_ref[index] = (
            shared_out[span] + left_contraction(chosen_ref[index], give_ref[slots])
        ).astype(low)
    store_out(outs, turn, turns, slot)


def grouped(shape):
    return pl.BlockSpec(shape, lambda i, *rest: (i,) + (0,) * (len(shape) - 1))


def fixed(shape):
    return pl.BlockSpec(
        shape, lambda i, *rest: (0,) * len(shape), pipeline_mode=pl.Buffered(1)
    )


def feed_kernel(body, name, scalars, arrays, in_specs, shapes, out_specs, scratch, flops, moved, turns):
    return pl.pallas_call(
        body,
        out_shape=shapes,
        grid_spec=pltpu.PrefetchScalarGridSpec(
            num_scalar_prefetch=len(scalars),
            grid=(turns,),
            in_specs=in_specs,
            out_specs=out_specs,
            scratch_shapes=scratch,
        ),
        compiler_params=pltpu.CompilerParams(
            dimension_semantics=("arbitrary",), vmem_limit_bytes=60 << 20
        ),
        cost_estimate=pl.CostEstimate(flops=flops, bytes_accessed=moved, transcendentals=0),
        name=name,
    )(*scalars, *arrays)


anywhere = pl.BlockSpec(memory_space=pl.ANY)


def project_body(scale, near_ref, far_ref, gain_ref, weight_ref, out_ref, x_bufs, x_sems):
    turn, turns = pl.program_id(0), pl.num_programs(0)
    slot = load_ahead([Stream((near_ref, far_ref), x_bufs, x_sems, turns)], turn, turns)
    unused, blocks, tokens, width = x_bufs.shape
    rows = x_bufs[slot].reshape(blocks * tokens, width).astype(wide)
    normed = rms_scale(rows, gain_ref[...]).astype(low)
    out = matmul(normed, weight_ref[...]) * scale
    out_ref[...] = out.astype(low).reshape(blocks, tokens, -1)


def project_all(near, far, gain, weight, scale):
    half, tokens, width = near.shape
    count, columns, blocks = 2 * half, weight.shape[1], GROUP // 2
    return feed_kernel(
        functools.partial(project_body, scale),
        "project",
        (),
        (near, far, gain, weight),
        [anywhere, anywhere, fixed(gain.shape), fixed(weight.shape)],
        jax.ShapeDtypeStruct((count, tokens, columns), low),
        grouped((blocks, tokens, columns)),
        [pltpu.VMEM((2, blocks, tokens, width), low), pltpu.SemaphoreType.DMA((2,))],
        4 * count * tokens * width * columns,
        2 * count * tokens * (width + columns),
        count // blocks,
    )


def choose_call(expert, order, c_all, route_rows, sd, count, tokens):
    width = c_all.shape[2]
    return feed_kernel(
        choose_body,
        "choose",
        (expert, order),
        (c_all, route_rows, sd),
        [anywhere, grouped((GROUP, 2, tokens)), fixed(sd.shape)],
        (
            jax.ShapeDtypeStruct((count * CAP, width), low),
            jax.ShapeDtypeStruct((count * tokens, PAIR), wide),
            jax.ShapeDtypeStruct((count, CAP, tokens), low),
        ),
        (grouped((GROUP * CAP, width)), grouped((GROUP * tokens, PAIR)), grouped((GROUP, CAP, tokens))),
        [pltpu.VMEM((2, GROUP, tokens, width), low), pltpu.SemaphoreType.DMA((2,))],
        8 * count * tokens * width * PAIR,
        count * tokens * width * 3,
        count // GROUP,
    )


def feed_call(expert, pieces, route_rows, pick, shared, chosen, cat, rt, gate, up, down):
    each, tokens, width = pieces[0].shape
    count, units = PIECES * each, gate.shape[2]
    slots, rows = GROUP * CAP, GROUP * tokens
    parts = jax.ShapeDtypeStruct(pieces[0].shape, low)
    saved = (
        (count * CAP, width), (count * CAP, width), (count * CAP, units), (count * CAP, units),
        (count * CAP, units), (count * CAP, width), (count * tokens, PAIR), (count * tokens, PAIR),
        (count, 2 * EXPERTS, tokens),
    )
    return feed_kernel(
        feed_body,
        "feed",
        (expert,),
        tuple(pieces) + (route_rows, pick, shared, chosen, cat, rt, gate, up, down),
        [anywhere] * PIECES
        + [
            grouped((GROUP, 2, tokens)),
            grouped((slots, width)),
            grouped((rows, PAIR)),
            grouped((GROUP, CAP, tokens)),
            fixed(cat.shape),
            fixed(rt.shape),
            fixed(gate.shape),
            fixed(up.shape),
            fixed(down.shape),
        ],
        (parts,) * PIECES + tuple(jax.ShapeDtypeStruct(shape, low) for shape in saved),
        (anywhere,) * PIECES
        + tuple(grouped((shape[0] * GROUP // count,) + shape[1:]) for shape in saved),
        [pltpu.VMEM((2, GROUP, tokens, width), low)] * 2 + [pltpu.SemaphoreType.DMA((2,))] * 2,
        48 * count * CAP * width * units // 2,
        count * tokens * width * 6,
        count // GROUP,
    )


def rest_call(gate, order, pieces, c_all, chosen, saved, sd, units):
    each, tokens, width = pieces[0].shape
    count = PIECES * each
    parts = jax.ShapeDtypeStruct(pieces[0].shape, low)
    shapes = ((width, units), (width, units), (units, width), (PAIR + 2 * EXPERTS, width), (PAIR, width))
    return feed_kernel(
        rest_body,
        "rest",
        (gate, order),
        tuple(pieces) + (c_all, chosen) + tuple(saved) + (sd,),
        [anywhere] * (PIECES + 1)
        + [grouped((GROUP, CAP, tokens))]
        + [grouped((array.shape[0] * GROUP // count,) + array.shape[1:]) for array in saved]
        + [fixed(sd.shape)],
        (parts,) * PIECES + tuple(jax.ShapeDtypeStruct(shape, wide) for shape in shapes),
        (anywhere,) * PIECES + tuple(fixed(shape) for shape in shapes),
        [pltpu.VMEM((2, GROUP, tokens, width), low)] * 3 + [pltpu.SemaphoreType.DMA((2,))] * 3,
        24 * count * CAP * width * units // 2,
        count * tokens * width * 8,
        count // GROUP,
    )


def shards(
    inputs,
    blocks,
    routes,
    attn_gain,
    w_query,
    w_key,
    w_value,
    w_out,
    ffn_gain,
    w_router,
    shared_gate,
    shared_up,
    shared_down,
    expert_gate,
    expert_up,
    expert_down,
    cotangent,
):
    heads, line = lax.axis_size("head"), lax.axis_size("blk")
    count = heads * line
    head, spot = lax.axis_index("head"), lax.axis_index("blk")
    device = head * line + spot
    tokens, width = inputs.shape
    total = count * tokens
    group = width // heads
    pairs = group // PAIR
    rows = w_query.shape[0]
    steps, short_steps = whole_steps(count), line_steps(line)
    sources = slot_sources(count, steps)
    places = jnp.asarray(np.argsort(sources, axis=1).astype(np.int32))[device]
    slot_sources_own = jnp.asarray(sources)[device]
    short_sources = slot_sources(line, short_steps)
    short_order = jnp.asarray(short_sources)[spot]
    short_places = jnp.asarray(np.argsort(short_sources, axis=1).astype(np.int32))[spot]

    def pad_rows(flat):
        extra = -flat.shape[0] % width
        return jnp.pad(flat, (0, extra)).reshape(-1, width)

    def pad_tall(values):
        return jnp.pad(values, ((0, -values.shape[0] % 16), (0, 0)))

    hop = lambda values, step: permute(values, BOTH, count, step)
    far_steps, cross, chip = steps[:-3], steps[-3:-1], steps[-1]

    own_blocks = jnp.arange(heads, dtype=jnp.int32) * line + spot
    own_slots = places[own_blocks]
    tile = TILE_BLOCKS * tokens
    own_ids = jnp.take(blocks.reshape(count, tokens), own_blocks, axis=0, mode="clip")
    low_id, high_id = own_ids[:, :1], own_ids[:, -1:]

    def counted(test):
        return jnp.sum(test, axis=1, dtype=jnp.int32)

    query_bounds = jnp.stack(
        [
            counted(blocks[None] <= low_id) // tile,
            (counted(blocks[None] <= high_id) + tile - 1) // tile,
        ]
    )
    key_bounds = jnp.stack(
        [
            counted(blocks[None] < low_id) // tile,
            (counted(blocks[None] < high_id) + tile - 1) // tile,
            jnp.full((heads,), total // tile, jnp.int32),
        ]
    )
    id_columns = jnp.tile(own_ids, (1, 2))[:, :, None]
    id_rows = blocks.reshape(count, 1, tokens)

    block_ids = jnp.arange(count, dtype=jnp.int32)
    grad_slots = short_places[block_ids % line] * heads + block_ids // line
    first_steps = weight_steps(line)
    first_places = jnp.asarray(
        np.argsort(slot_sources(line, first_steps), axis=1).astype(np.int32)
    )[spot]
    beside = places[(1 - head) * line + spot]
    expert = (device % EXPERTS).astype(jnp.int32).reshape(1)
    tables = (
        own_slots, query_bounds, key_bounds,
        id_columns, grad_slots, first_places, beside, slot_sources_own, expert,
    )

    halves = lambda matrix: matrix.reshape(rows, heads, group).transpose(1, 0, 2)
    extras = jnp.concatenate(
        [attn_gain, ffn_gain, w_router.reshape(-1), routes.T.reshape(-1).astype(low)]
    )
    extras = jnp.pad(extras, (0, -extras.shape[0] % group)).reshape(-1, group)
    split = [halves(matrix) for matrix in (w_query, w_key, w_value)]
    split = jnp.concatenate(split + [jnp.broadcast_to(extras, (heads,) + extras.shape)], axis=1)
    split = jnp.pad(split, ((0, 0), (0, -split.shape[1] % 16), (0, 0)))
    kept = lax.dynamic_index_in_dim(split, head, 0, False)
    sent = lax.dynamic_index_in_dim(split, 1 - head, 0, False)
    weights = [head_order(head, kept, swap_heads(sent))[None]]
    for step in first_steps[:-1]:
        weights.append(grow(weights[-1], permute(weights[-1], "blk", line, step)))
    weights_far = permute(weights[-1], "blk", line, first_steps[-1])
    held = [inputs[None]]
    shared_slice = shared_gate.shape[1] // count
    shared_pack = jnp.stack(
        [
            shared_gate.reshape(rows, count, shared_slice),
            shared_up.reshape(rows, count, shared_slice),
        ],
        axis=2,
    ).reshape(rows, count * 2 * shared_slice)
    for place, step in enumerate(steps[:-1]):
        start = held[-1]
        if step is cross[1]:
            start, shared_pack = lax.optimization_barrier((start, shared_pack))
        arrived = after(hop(start, step), weights[min(place, len(weights) - 1)])
        if step is cross[0]:
            arrived = after(arrived, *tables[:3])
        if step is cross[1]:
            arrived = after(arrived, *tables[3:])
        held.append(grow(start, arrived))
    shared_in = lax.all_to_all(shared_pack, BOTH, split_axis=1, concat_axis=0, tiled=True)
    inputs_near = held[-1]
    inputs_far = hop(after(inputs_near, shared_in), chip)

    cot_all = after(jnp.concatenate([cotangent, w_out], axis=0), held[len(far_steps) + 1])
    cot_all = lax.all_gather(cot_all, BOTH, axis=0, tiled=False)
    full_out = cot_all[:, tokens:].reshape(width, width)

    query_weight, key_weight = unpack_call(first_places, weights[-1], weights_far, width)
    first_row = 3 * rows
    flat = grow(weights[-1][:, :, first_row:], weights_far[:, :, first_row:])
    flat = flat.reshape(line, heads, -1)
    flat = jnp.take(flat, first_places, axis=0, mode="clip").transpose(1, 0, 2)
    flat = flat.reshape(count, -1)
    gain_first = flat[:, :rows].reshape(width).astype(wide)
    gain_second = flat[:, rows : 2 * rows].reshape(width).astype(wide)
    router = flat[:, 2 * rows : (2 + EXPERTS) * rows].reshape(width, EXPERTS)
    route_rows = flat[:, (2 + EXPERTS) * rows : (2 + EXPERTS) * rows + 2 * tokens]
    route_rows = jnp.take(route_rows, slot_sources_own, axis=0, mode="clip")
    route_rows = route_rows.reshape(count, 2, tokens).astype(jnp.int32)

    keys = project_all(inputs_near, inputs_far, gain_first[None], key_weight, 1.0)
    neighbour = lax.dynamic_index_in_dim(
        inputs_near, beside, 0, False
    )
    pair_inputs = head_order(head, inputs, neighbour).reshape(heads * tokens, width)
    pair_normed = rms_scale(pair_inputs.astype(wide), gain_first).astype(low)
    own_queries = (matmul(pair_normed, query_weight) * scale_factor).astype(low)
    own_queries = own_queries.reshape(heads, tokens, group)

    own_spec = lambda column: pl.BlockSpec(
        (1, tokens, PAIR), lambda p, j, own, *rest: (own[j], 0, column + p)
    )
    all_spec = lambda column: pl.BlockSpec(
        (count, tokens, PAIR), lambda p, j, *rest: (0, 0, column + p)
    )
    half_spec = pl.BlockSpec((count // 2, tokens, PAIR), lambda p, j, *rest: (0, 0, p))
    part_spec = pl.BlockSpec((1, tokens, PAIR), lambda p, j, *rest: (j, 0, p))
    stat_spec = pl.BlockSpec((1, 1, 1, 2 * tokens), lambda p, j, *rest: (p, j, 0, 0))
    column_spec = pl.BlockSpec((1, 2 * tokens, 1), lambda p, j, *rest: (j, 0, 0))
    ids_spec = pl.BlockSpec((count, 1, tokens), lambda p, j, *rest: (0, 0, 0))
    part_shape = jax.ShapeDtypeStruct((heads, tokens, group), low)
    stat_shape = jax.ShapeDtypeStruct((pairs, heads, 1, 2 * tokens), wide)
    grid = (pairs, heads)
    unit = 2 * heads * tokens * total * group

    attended_own, lse = attention_call(
        attend_body,
        "attend",
        (
            after(own_slots, route_rows),
            places,
            query_bounds,
        ),
        (own_queries, keys, keys, id_columns, id_rows),
        [part_spec, all_spec(0), all_spec(pairs), column_spec, ids_spec],
        (part_shape, stat_shape),
        (part_spec, stat_spec),
        grid,
        2 * unit,
        count,
    )
    attended_back = swap_heads(lax.dynamic_index_in_dim(attended_own, 1 - head, 0, False))
    attended_kept = lax.dynamic_index_in_dim(attended_own, head, 0, False)
    attended = jnp.where(
        head == 0,
        jnp.concatenate([attended_kept, attended_back], axis=1),
        jnp.concatenate([attended_back, attended_kept], axis=1),
    )
    inputs_wide = inputs.astype(wide)
    mixed_rows = inputs_wide + matmul(attended, full_out)
    normed_ffn = rms_scale(mixed_rows, gain_second).astype(low)

    half_pad = HEAD_DIM - shared_slice
    shared_pair = jnp.pad(
        shared_in.reshape(width, 2, shared_slice), ((0, 0), (0, 0), (0, half_pad))
    ).reshape(width, PAIR)
    feed_weight = jnp.concatenate(
        [shared_pair, router, jnp.zeros((width, PAIR - EXPERTS), low)], axis=1
    )
    down_pad = jnp.pad(shared_down, ((0, PAIR - shared_slice), (0, 0)))
    router_rows = jnp.transpose(jnp.concatenate([router, router], axis=1))

    near = normed_ffn[None]
    for step in steps[:-2]:
        arrived = hop(near, step)
        if step is steps[1]:
            gate = after(gain_first[None], near)
            queries = project_all(inputs_near, inputs_far, gate, query_weight, scale_factor)
            arrived = after(arrived, queries)
        near = grow(near, arrived)
    near_far = hop(near, chip)
    pick, shared_grad, chosen = choose_call(
        after(expert, near), slot_sources_own, cot_all, route_rows, down_pad, count, tokens
    )
    crossed = after(hop(near, cross[1]), chosen, feed_weight, near_far)
    pieces = [near, crossed, near_far, hop(crossed, chip)]
    near_low, near_high, far_low, far_high, *saved = feed_call(
        expert, pieces, route_rows, pick, shared_grad, chosen, feed_weight, router_rows,
        expert_gate, expert_up, expert_down,
    )
    row_upper = (near_high.astype(wide) + hop(far_high, chip).astype(wide)).astype(low)
    terms = [near_low, hop(after(far_low, row_upper), chip)]
    (
        out_low, out_high, out_far_low, out_far_high,
        grad_egate, grad_eup, grad_edown, grad_feed, grad_sdown,
    ) = rest_call(
        after(expert, row_upper), slot_sources_own, pieces, cot_all, chosen, saved, down_pad,
        expert_gate.shape[2],
    )
    terms = terms + [after(hop(row_upper, cross[1]), out_low)]
    out_far_high, terms[-1] = lax.optimization_barrier((out_far_high, terms[-1]))
    out_upper = (out_high.astype(wide) + hop(out_far_high, chip).astype(wide)).astype(low)
    out_terms = [out_low, hop(after(out_far_low, out_upper), chip)]
    grad_sdown = grad_sdown[:shared_slice]
    terms = scatter_step(terms, BOTH, count, cross[0])
    terms[-1], out_upper = lax.optimization_barrier((terms[-1], out_upper))
    out_arrived = hop(out_upper, cross[1])
    grad_shared, terms[-1] = lax.optimization_barrier((grad_feed[:PAIR], terms[-1]))
    grad_shared = grad_shared.reshape(2, HEAD_DIM, width)[:, :shared_slice].reshape(-1, width)
    grad_shared = jnp.transpose(grad_shared).astype(low)
    grad_shared_back = lax.all_to_all(grad_shared, BOTH, split_axis=0, concat_axis=1, tiled=True)
    for step in reversed(far_steps):
        terms = scatter_step(terms, BOTH, count, step)
    normed_ffn_grad = finish(terms)
    grad_router = jnp.transpose(
        grad_feed[PAIR : PAIR + EXPERTS] + grad_feed[PAIR + EXPERTS : PAIR + 2 * EXPERTS]
    )

    unused_second, second_pull = jax.vjp(rms_scale, mixed_rows, gain_second)
    mixed_part, grad_gain_ffn = second_pull(normed_ffn_grad)
    mixed_grad = cotangent.astype(wide) + mixed_part
    mixed_low = after(mixed_grad.astype(low), out_arrived, grad_shared_back)
    mixed_pair = head_order(head, mixed_low, swap_heads(mixed_low)).reshape(heads * tokens, width)
    own_out = lax.dynamic_slice_in_dim(full_out, head * group, group, 0)
    attended_grad = right_contract(mixed_pair, own_out).astype(low)
    attended_flat = attended_own.reshape(heads * tokens, group)
    head_marks = (
        jnp.arange(group)[None] // HEAD_DIM == jnp.arange(2 * pairs)[:, None]
    ).astype(wide)
    delta = lax.dot_general(
        head_marks,
        attended_grad.astype(wide) * attended_flat.astype(wide),
        (((1,), (1,)), ((), ())),
        precision=lax.Precision.HIGHEST,
    )
    delta = (
        delta.reshape(pairs, 2, heads, tokens)
        .transpose(0, 2, 1, 3)
        .reshape(pairs, heads, 1, 2 * tokens)
    )
    stats = jnp.stack([lse, delta]).transpose(2, 0, 1, 3, 4).reshape(heads, -1)
    stats_rows = jnp.concatenate(two_parts(stats), axis=1).reshape(heads, -1, group)
    grad_parts = attended_grad.reshape(heads, tokens, group)
    grads = [jnp.concatenate([grad_parts, stats_rows], axis=1)[None]]
    def next_out(terms, arrived, gate):
        terms = terms + [arrived]
        sent = upper(terms)
        gate, sent = lax.optimization_barrier((gate, sent))
        return lower(terms), sent, gate

    columns = two_parts(jnp.concatenate([grad_gain_ffn[:, None], grad_router], axis=1))
    extra = columns[0].shape[1]
    columns = jnp.concatenate(columns, axis=1)
    columns = jnp.pad(columns, ((0, 0), (1, PAIR - 1 - 2 * extra)))
    out_terms, sent, grads[0] = next_out(out_terms, out_arrived, grads[0])
    out_arrived = hop(sent, cross[0])
    tail = list(reversed(far_steps))
    for place, step in enumerate(short_steps[:-1]):
        if place == 1:
            grads[-1] = after(grads[-1], out_arrived, columns)
        if place == len(short_steps) - 2:
            out_terms, sent, grads[-1] = next_out(out_terms, out_arrived, grads[-1])
            out_arrived = hop(sent, tail[0])
        grads.append(grow(grads[-1], permute(grads[-1], "blk", line, step)))
    query_q = after(own_slots, grads[-2])
    query_grad = attention_call(
        query_body,
        "query_gradient",
        (query_q, places, query_bounds),
        (own_queries, keys, keys, grad_parts, lse, delta, id_columns, id_rows),
        [
            part_spec,
            all_spec(0),
            all_spec(pairs),
            part_spec,
            stat_spec,
            stat_spec,
            column_spec,
            ids_spec,
        ],
        part_shape,
        part_spec,
        grid,
        3 * unit,
        count,
    )
    start = after(grads[-1], query_grad)
    out_terms, sent, start = next_out(out_terms, out_arrived, start)
    for step in tail[1:-1]:
        out_terms, sent, start = next_out(out_terms, hop(sent, step), start)
    out_arrived = hop(sent, tail[-1])
    grads.append(permute(start, "blk", line, short_steps[-1]))
    grad_halves = [part.reshape(count // 2, -1, group) for part in (start, grads[-1])]

    def stat_part(part):
        part = part[:, tokens:].reshape(count // 2, 2, -1).astype(wide)
        return (part[:, 0] + part[:, 1]).reshape(-1, 1, 2 * tokens)

    stats_all = jnp.concatenate([stat_part(part) for part in grad_halves])
    key_grad, value_grad = attention_call(
        key_body,
        "key_gradient",
        (own_slots, places, grad_slots, key_bounds),
        (keys, keys, queries, *grad_halves, stats_all, id_columns, id_rows),
        [
            own_spec(0),
            own_spec(pairs),
            all_spec(0),
            half_spec,
            half_spec,
            pl.BlockSpec(stats_all.shape, lambda p, j, *rest: (0, 0, 0)),
            column_spec,
            ids_spec,
        ],
        (part_shape, part_shape),
        (part_spec, part_spec),
        grid,
        4 * unit,
        count,
    )

    near, far, normed_part = weights_call(
        short_places, pair_inputs, gain_first[None], query_grad, key_grad, value_grad,
        query_weight, key_weight, columns, attended_flat, mixed_pair, line,
    )
    backward = list(reversed(short_steps))
    sums = [near, permute(far, "blk", line, backward[0])]
    out_terms.append(out_arrived)
    for place, step in enumerate(backward[1:]):
        sums = scatter_step(sums, "blk", line, step)
        if place == 0:
            first_sum = sums[-1]
            sums[-1] = after(sums[-1], out_arrived)
    output = (mixed_rows + finish(out_terms)).astype(low)
    sums = [sums]
    summed = finish(sums[0])
    grad_wout_own = summed[:, :, 3 * group + PAIR :].transpose(1, 0, 2).reshape(rows, width)
    summed = summed[:, :, : 3 * group + PAIR]
    summed_back = swap_heads(
        lax.dynamic_index_in_dim(summed, 1 - head, 0, False).astype(low)
    ).astype(wide)
    summed_kept = lax.dynamic_index_in_dim(summed, head, 0, False)
    joined = head_order(head, summed_kept, summed_back)
    small = jnp.sum(joined[:, :, 3 * group :], axis=0)
    gain_column = small[:, 0] + small[:, PAIR - 1]
    small = small[:, 1 : extra + 1] + small[:, extra + 1 : 2 * extra + 1]
    joined = joined[:, :, : 3 * group].reshape(heads, rows, 3, group)
    joined = joined.transpose(2, 1, 0, 3).reshape(3, rows, width)

    normed_parts = normed_part.reshape(heads, tokens, width)
    arrived = swap_heads(lax.dynamic_index_in_dim(normed_parts, 1 - head, 0, False).astype(low))
    normed_grad = lax.dynamic_index_in_dim(normed_parts, head, 0, False) + arrived.astype(wide)
    unused_first, first_pull = jax.vjp(lambda rows_in: rms_scale(rows_in, gain_first), inputs_wide)
    grad_inputs = mixed_grad + first_pull(after(normed_grad, first_sum))[0]
    grad_shared_back = after(grad_shared_back, first_sum).reshape(rows, count, 2, shared_slice)
    grad_sgate = grad_shared_back[:, :, 0].reshape(rows, -1).astype(wide)
    grad_sup = grad_shared_back[:, :, 1].reshape(rows, -1).astype(wide)

    return (
        output,
        grad_inputs,
        gain_column,
        joined[0].astype(wide),
        joined[1].astype(wide),
        joined[2].astype(wide),
        grad_wout_own,
        small[:, 0],
        small[:, 1:],
        grad_sgate,
        grad_sup,
        grad_sdown,
        grad_egate[None],
        grad_eup[None],
        grad_edown[None],
    )


def solution(mesh):
    both = P(BOTH)
    rows = P(BOTH, None)
    slabs = P(BOTH, None, None)
    return jax.shard_map(
        shards,
        mesh=mesh,
        in_specs=(
            rows, P(), rows, both, rows, rows, rows, rows, both, rows, rows, rows, rows,
            slabs, slabs, slabs, rows,
        ),
        out_specs=(
            rows, rows, both, rows, rows, rows, rows, both, rows, rows, rows, rows,
            slabs, slabs, slabs,
        ),
        check_vma=False,
    )
```
